128 devices in a mesh: row: 16 (over y_hi, x, core), col: 8 (over y_lo, z).
Axes of the slice: x: 4, y: 4 (y_hi: 2, y_lo: 2; y = y_hi * 2 + y_lo), z: 4, core: 2. Of those that a mesh axis runs over, the one named last changes fastest.
Arguments:
- features_t: float32 [18432, 512], P(('row', 'col')), may hold values from -0.0234375 to 0.0234375
- labels: int32 [512], replicated, may hold values from 0 to 1023
- inv_corr: float32 [18432, 18432], P('row', 'col'), may hold values from -1 to 13, as said below
- heads: float32 [18432, 1024], P('row', 'col'), may hold values from -6 to 6
Outputs:
- inv_corr_new: float32 [18432, 18432], P('row', 'col')
- heads_new: float32 [18432, 1024], P('row', 'col')
The draws below stay inside these ranges and needn't reach their ends.
Inputs may be any that keep to these rules, and one draw needn't show every extreme that they name: inv_corr is symmetric and positive definite, with smallest eigenvalue above 0.5.
All inputs are finite; a program needn't handle non-finite values.
Results may differ from the reference program's by a relative error of at most 0.0001.
Values sent between devices are 32-bit elements; how exact they have to be, the bound alone decides.
A program may use at most 128 MiB of HBM per device.

```python
import math
import jax
import jax.numpy as jnp
from jax import lax

D = 18432
CLASSES = 1024
EXAMPLES = 256
PHASES = 2
ALL_EXAMPLES = 512


def draw_inv_corr(key, part):
    base = jax.random.fold_in(key, 11)
    diag_key, noise_key = jax.random.split(base)
    diagonal = jax.random.uniform(diag_key, (D,), jnp.float32, 2.0, 6.0)
    noise = jax.random.uniform(noise_key, (D, D), jnp.float32, -1.0, 1.0)
    symmetric = (noise + noise.T) * (0.4 / math.sqrt(D))
    return symmetric + jnp.diag(diagonal)


def with_ends(drawn, key, least, top_value):
    longest = drawn.shape.index(max(drawn.shape))
    spots = []
    for shift in (0, 1):
        where = [jax.random.randint(jax.random.fold_in(key, axis), (), 0, length) for axis, length in enumerate(drawn.shape)]
        where[longest] = (where[longest] + shift) % drawn.shape[longest]
        spots.append(tuple(where))
    return drawn.at[spots[0]].set(least).at[spots[1]].set(top_value)


def level_of(own_key, shape, cuts, least, high):
    level = 1.0
    for axis_at, blocks in cuts:
        steps = jax.random.uniform(jax.random.fold_in(jax.random.fold_in(own_key, 6), axis_at), (blocks,), jnp.float32, least / len(cuts), high / len(cuts))
        level = level * jnp.repeat(jnp.exp(steps), shape[axis_at] // blocks).reshape((-1,) + (1,) * (len(shape) - 1 - axis_at))
    return level


def scatter_about(own_key, extent, spread, bound, cuts=(), kind=jnp.bfloat16):
    result = jax.random.normal(own_key, extent, jnp.float32) * spread
    if len(cuts) > 0:
        result = level_of(own_key, extent, cuts, -0.22, 0.18) * result
    return jnp.clip(result, min=-bound, max=bound).astype(kind)


def setup_inputs(seed: int = 0) -> dict:
    arg_keys = jax.random.split(jax.random.key(seed), 5)
    return {
        "features_t": scatter_about(arg_keys[0], (D, ALL_EXAMPLES), (4 * D) ** -0.5, 0.0234375, ((0, 128),), jnp.float32),
        "labels": with_ends(jax.random.randint(arg_keys[1], (ALL_EXAMPLES,), 0, CLASSES), jax.random.fold_in(arg_keys[1], 1), 0, CLASSES - 1).astype(jnp.int32),
        "inv_corr": draw_inv_corr(jax.random.fold_in(arg_keys[4], 71), 0),
        "heads": scatter_about(arg_keys[3], (D, CLASSES), 1.0, 6.0, ((0, 16), (1, 8)), jnp.float32),
    }


def matmul(left, right):
    return jnp.dot(left.astype(jnp.float32), right.astype(jnp.float32), precision=lax.Precision.HIGHEST, preferred_element_type=jnp.float32)

def contract_rows(left, right):
    return lax.dot_general(left.astype(jnp.float32), right.astype(jnp.float32), (((0,), (0,)), ((), ())), precision=lax.Precision.HIGHEST, preferred_element_type=jnp.float32)

def contract_cols(left, right):
    return lax.dot_general(left.astype(jnp.float32), right.astype(jnp.float32), (((1,), (1,)), ((), ())), precision=lax.Precision.HIGHEST, preferred_element_type=jnp.float32)

def invert_system(gram):
    identity_mat = jnp.eye(gram.shape[0], dtype=jnp.float32)
    factor = jnp.linalg.cholesky(identity_mat + gram)
    return jax.scipy.linalg.cho_solve((factor, True), identity_mat)

def reference(features_t, labels, inv_corr, heads):
    classes = jnp.arange(CLASSES, dtype=jnp.int32)
    targets = (labels[:, None] == classes[None, :]).astype(jnp.float32)
    tile = inv_corr
    head = heads
    for phase in range(PHASES):
        lower = phase * EXAMPLES
        current = features_t[:, lower:lower + EXAMPLES]
        panel = matmul(tile, current)
        gram = contract_rows(current, panel)
        fitted = contract_rows(current, head)
        inverse = invert_system(gram)
        gain = matmul(panel, inverse)
        head = head + matmul(gain, targets[lower:lower + EXAMPLES] - fitted)
        tile = tile - contract_cols(gain, panel)
    return (tile, head)
```

```python
import jax
import jax.numpy as jnp
from jax import lax
from jax.experimental import pallas as pl
from jax.experimental.pallas import tpu as pltpu
from jax.sharding import PartitionSpec as P

F32 = jnp.float32
BF16 = jnp.bfloat16
MESH = pl.DeviceIdType.MESH
ALL = 512
CHUNK = 64
MIB = 1 << 20


def split(value):
    hi = value.astype(BF16)
    lo = (value - hi.astype(F32)).astype(BF16)
    return hi, lo


def mm(left, right):
    return jnp.dot(left, right, preferred_element_type=F32)


def dot3(left, right):
    (lh, ll), (rh, rl) = left, right
    return mm(lh, rh) + (mm(lh, rl) + mm(ll, rh))


class Place:
    def __init__(self):
        self.row, self.col = row, col = lax.axis_index("row"), lax.axis_index("col")
        self.core = core = lax.rem(row, 2)
        self.chip_row = chip_row = row // 2
        self.y_hi, self.x = y_hi, x = chip_row // 4, lax.rem(chip_row, 4)
        self.y_lo, self.z = y_lo, z = col // 4, lax.rem(col, 4)
        self.sibling = (chip_row * 2 + (1 - core), col)
        self.x_up = ((y_hi * 4 + lax.rem(x + 1, 4)) * 2 + core, col)
        self.x_down = ((y_hi * 4 + lax.rem(x + 3, 4)) * 2 + core, col)
        self.x_far = ((y_hi * 4 + lax.rem(x + 2, 4)) * 2 + core, col)
        self.y_far = (((1 - y_hi) * 4 + x) * 2 + core, col)
        self.z_up = (row, y_lo * 4 + lax.rem(z + 1, 4))
        self.z_down = (row, y_lo * 4 + lax.rem(z + 3, 4))
        self.y_near = (row, (1 - y_lo) * 4 + z)
        self.swapped = (col * 2 + core, chip_row)


class Copies:
    def __init__(self, send_sems, recv_sems):
        self.send_sems, self.recv_sems = send_sems, recv_sems
        self.count = 0
        self.started = []

    def take(self):
        self.count += 1
        return self.count - 1

    def make(self, index, src, dst, device):
        return pltpu.make_async_remote_copy(
            src_ref=src, dst_ref=dst, send_sem=self.send_sems.at[index], recv_sem=self.recv_sems.at[index],
            device_id=device, device_id_type=MESH)

    def start(self, src, dst, device):
        index = self.take()
        copy = self.make(index, src, dst, device)
        copy.start()
        self.started.append(copy)
        return index

    def arrived(self, index, landing, device):
        self.make(index, landing, landing, device).wait_recv()

    def finish(self):
        for copy in self.started:
            copy.wait_send()


def greet(devices):
    barrier = pltpu.get_barrier_semaphore()
    for device in devices:
        pl.semaphore_signal(barrier, inc=1, device_id=device, device_id_type=MESH)
    pl.semaphore_wait(barrier, len(devices))


class Gather:
    def __init__(self, copies, buf, pair_at, ring_at, pair, up, down, rows):
        self.c, self.buf, self.rows = copies, buf, rows
        self.a, self.b = pair_at, ring_at
        self.pair, self.up, self.down = pair, up, down

    def slot(self, pair_step, ring_step):
        a = self.a if pair_step == 0 else 1 - self.a
        return a * 4 + lax.rem(self.b + ring_step, 4)

    def part(self, pair_step, ring_step, half=None):
        at = self.slot(pair_step, ring_step)
        if half is None:
            return self.buf.at[at]
        n = self.rows // 2
        return self.buf.at[at, pl.ds(half * n, n)]

    def same(self, part, device):
        return self.c.start(part, part, device)

    def own(self):
        mine = self.part(0, 0)
        self.i_up = self.same(mine, self.up)
        self.i_down = self.same(mine, self.down)
        self.i_pair = self.same(mine, self.pair)

    def forward_own(self):
        self.c.arrived(self.i_up, self.part(0, 3), self.down)
        self.h_up = self.same(self.part(0, 3, 0), self.up)
        self.c.arrived(self.i_down, self.part(0, 1), self.up)
        self.h_down = self.same(self.part(0, 1, 1), self.down)

    def pair_across(self):
        self.c.arrived(self.i_pair, self.part(1, 0), self.pair)
        self.q_up = self.same(self.part(1, 0), self.up)
        self.q_down = self.same(self.part(1, 0), self.down)

    def far_own(self):
        self.c.arrived(self.h_up, self.part(0, 2, 0), self.down)
        self.c.arrived(self.h_down, self.part(0, 2, 1), self.up)

    def far_by_pair(self):
        self.f_pair = self.same(self.part(0, 2), self.pair)

    def end_by_pair(self):
        self.c.arrived(self.q_up, self.part(1, 3), self.down)
        self.c.arrived(self.q_down, self.part(1, 1), self.up)
        self.c.arrived(self.f_pair, self.part(1, 2), self.pair)

    def forward_pair(self):
        self.c.arrived(self.q_up, self.part(1, 3), self.down)
        self.g_up = self.same(self.part(1, 3, 0), self.up)
        self.c.arrived(self.q_down, self.part(1, 1), self.up)
        self.g_down = self.same(self.part(1, 1, 1), self.down)

    def end_by_ring(self):
        self.c.arrived(self.g_up, self.part(1, 2, 0), self.down)
        self.c.arrived(self.g_down, self.part(1, 2, 1), self.up)


def gather_kernel(x_ref, out_ref, local_sem, send_sems, recv_sems):
    at = Place()
    mine = pltpu.make_async_copy(x_ref, out_ref.at[at.col], local_sem)
    mine.start()
    greet([at.y_near, at.z_up, at.z_down])
    mine.wait()
    copies = Copies(send_sems, recv_sems)
    g = Gather(copies, out_ref, at.y_lo, at.z, at.y_near, at.z_up, at.z_down, x_ref.shape[0])
    g.own()
    g.forward_own()
    g.pair_across()
    g.far_own()
    g.far_by_pair()
    g.end_by_pair()
    copies.finish()


def gather_rows(features_t):
    rows, examples = features_t.shape
    out = pl.pallas_call(
        gather_kernel,
        out_shape=jax.ShapeDtypeStruct((8, rows, examples), F32),
        in_specs=[pl.BlockSpec(memory_space=pltpu.VMEM)],
        out_specs=pl.BlockSpec(memory_space=pltpu.VMEM),
        scratch_shapes=[pltpu.SemaphoreType.DMA, pltpu.SemaphoreType.DMA((8,)), pltpu.SemaphoreType.DMA((8,))],
        compiler_params=pltpu.CompilerParams(collective_id=0, has_side_effects=True, vmem_limit_bytes=48 * MIB),
        name="gather_rows",
    )(features_t)
    return out.reshape(8 * rows, examples)


def partial_kernel(x_ref, r_ref, w_ref, p_ref, f_ref, xh_ref, xl_ref):
    @pl.when((pl.program_id(0) == 0) & (pl.program_id(1) == 0))
    def _():
        xh, xl = split(x_ref[...].T)
        xh_ref[...] = xh
        xl_ref[...] = xl
        f_ref[...] = dot3((xh, xl), split(w_ref[...]))

    p_ref[0] = dot3((xh_ref[...], xl_ref[...]), split(r_ref[...]))


def partial_panel(x_rows, tile, head):
    rows, examples = x_rows.shape
    width = tile.shape[1] // 2
    block = width // 3
    return pl.pallas_call(
        partial_kernel,
        grid=(2, 3),
        out_shape=(jax.ShapeDtypeStruct((2, examples, width), F32), jax.ShapeDtypeStruct((examples, head.shape[1]), F32)),
        in_specs=[
            pl.BlockSpec((rows, examples), lambda h, j: (0, 0)),
            pl.BlockSpec((rows, block), lambda h, j: (0, h * 3 + j)),
            pl.BlockSpec(head.shape, lambda h, j: (0, 0)),
        ],
        out_specs=(
            pl.BlockSpec((1, examples, block), lambda h, j: (h, 0, j)),
            pl.BlockSpec((examples, head.shape[1]), lambda h, j: (0, 0)),
        ),
        scratch_shapes=[pltpu.VMEM((examples, rows), BF16), pltpu.VMEM((examples, rows), BF16)],
        compiler_params=pltpu.CompilerParams(vmem_limit_bytes=48 * MIB),
        name="partial_panel",
    )(x_rows, tile, head)


def panels_kernel(p_ref, x_ref, uc_ref, ur_ref, s_ref, from_sib, acc, ra, rb, ry, sp, rs0, sh, rs1, sh2, rs2,
                  send_sems, recv_sems):
    at = Place()
    k, p, col = at.core, at.chip_row, at.col
    barrier = pltpu.get_barrier_semaphore()
    near = [at.sibling, at.x_up, at.x_down, at.x_far, at.y_far, at.z_up, at.z_down, at.y_near]
    for device in near:
        pl.semaphore_signal(barrier, inc=1, device_id=device, device_id_type=MESH)
    off_diagonal = p != col

    @pl.when(off_diagonal)
    def _():
        pl.semaphore_signal(barrier, inc=1, device_id=at.swapped, device_id_type=MESH)
        pl.semaphore_wait(barrier, len(near) + 1)

    @pl.when(jnp.logical_not(off_diagonal))
    def _():
        pl.semaphore_wait(barrier, len(near))

    copies = Copies(send_sems, recv_sems)

    def chunk(y_step, x_step):
        y = at.y_hi if y_step == 0 else 1 - at.y_hi
        return y * 4 + lax.rem(at.x + x_step, 4)

    order = [(1, 2), (0, 2), (1, 1), (0, 1), (1, 3), (0, 3), (1, 0), (0, 0)]
    sib = {}
    for step in order:
        ch = chunk(*step)
        sib[step] = copies.start(p_ref.at[1 - k, ch], from_sib.at[ch], at.sibling)

    def add_sibling(step):
        ch = chunk(*step)
        copies.arrived(sib[step], from_sib.at[ch], at.sibling)
        acc[ch] = p_ref[k, ch] + from_sib[ch]

    half = CHUNK // 2
    low, high = pl.ds(0, half), pl.ds(half, half)
    a_up, a_down, b_up, b_down = {}, {}, {}, {}
    for y in (1, 0):
        add_sibling((y, 2))
        ch = chunk(y, 2)
        a_up[y] = copies.start(acc.at[ch, low], ra.at[0, y], at.x_up)
        a_down[y] = copies.start(acc.at[ch, high], ra.at[1, y], at.x_down)
    for y in (1, 0):
        add_sibling((y, 1))
        add_sibling((y, 3))
    for y in (1, 0):
        ch = chunk(y, 1)
        copies.arrived(a_up[y], ra.at[0, y], at.x_down)
        acc[ch, low] = acc[ch, low] + ra[0, y]
        b_up[y] = copies.start(acc.at[ch], rb.at[0, y], at.x_up)
        ch = chunk(y, 3)
        copies.arrived(a_down[y], ra.at[1, y], at.x_up)
        acc[ch, high] = acc[ch, high] + ra[1, y]
        b_down[y] = copies.start(acc.at[ch], rb.at[1, y], at.x_down)
    add_sibling((1, 0))
    add_sibling((0, 0))

    def add_x(y):
        ch = chunk(y, 0)
        copies.arrived(b_up[y], rb.at[0, y], at.x_down)
        copies.arrived(b_down[y], rb.at[1, y], at.x_up)
        return acc[ch] + (rb[0, y] + rb[1, y])

    ch = chunk(1, 0)
    acc[ch] = add_x(1)
    c_far = copies.start(acc.at[ch], ry, at.y_far)
    mine = add_x(0)
    copies.arrived(c_far, ry, at.y_far)
    uc_ref[k, p] = mine + ry[...]

    own_block = uc_ref.at[k]
    t = copies.take()
    swap = copies.make(t, uc_ref.at[k, p], ur_ref.at[p], at.swapped)

    @pl.when(off_diagonal)
    def _():
        swap.start()

    gc = Gather(copies, own_block, at.y_hi, at.x, at.y_far, at.x_up, at.x_down, CHUNK)
    gr = Gather(copies, ur_ref, at.y_lo, at.z, at.y_near, at.z_up, at.z_down, CHUNK)
    gc.own()

    @pl.when(off_diagonal)
    def _():
        copies.make(t, ur_ref.at[col], ur_ref.at[col], at.swapped).wait_recv()
        swap.wait_send()

    @pl.when(jnp.logical_not(off_diagonal))
    def _():
        ur_ref[col] = uc_ref[k, p]

    gr.own()
    sp[...] = dot3(split(ur_ref[col]), split(x_ref[...]))
    s0 = copies.start(sp.at[pl.ds((1 - k) * half, half)], rs0, at.sibling)
    gc.forward_own()
    copies.arrived(s0, rs0, at.sibling)
    sh[...] = sp[pl.ds(pl.multiple_of(k * half, half), half)] + rs0[...]
    s1 = [copies.start(sh, rs1.at[i], d) for i, d in enumerate((at.x_up, at.x_down, at.x_far))]
    gc.pair_across()
    gr.forward_own()
    gr.pair_across()
    for i, d in enumerate((at.x_down, at.x_up, at.x_far)):
        copies.arrived(s1[i], rs1.at[i], d)
    sh2[...] = sh[...] + rs1[0] + (rs1[1] + rs1[2])
    s2 = copies.start(sh2, rs2, at.y_far)
    copies.arrived(s2, rs2, at.y_far)
    s_ref[k, col] = sh2[...] + rs2[...]
    gs = Gather(copies, s_ref.at[k], at.y_lo, at.z, at.y_near, at.z_up, at.z_down, half)
    gs.own()
    gs.forward_own()
    gs.pair_across()
    gs.far_own()
    gs.forward_pair()
    gs.end_by_ring()
    s4 = copies.start(s_ref.at[k], s_ref.at[k], at.sibling)

    gc.far_own()
    gc.forward_pair()
    gr.far_own()
    gr.forward_pair()
    gc.end_by_ring()
    u4 = copies.start(own_block, own_block, at.sibling)
    gr.end_by_ring()
    copies.arrived(s4, s_ref.at[1 - k], at.sibling)
    copies.arrived(u4, uc_ref.at[1 - k], at.sibling)
    copies.finish()


def panels(partial, x_rows):
    width = partial.shape[2]
    half = CHUNK // 2
    vmem = pl.BlockSpec(memory_space=pltpu.VMEM)
    return pl.pallas_call(
        panels_kernel,
        out_shape=(
            jax.ShapeDtypeStruct((2, 8, CHUNK, width), F32),
            jax.ShapeDtypeStruct((8, CHUNK, width), F32),
            jax.ShapeDtypeStruct((2, 8, half, ALL), F32),
        ),
        in_specs=[vmem] * 2,
        out_specs=(vmem,) * 3,
        scratch_shapes=[
            pltpu.VMEM((8, CHUNK, width), F32),
            pltpu.VMEM((8, CHUNK, width), F32),
            pltpu.VMEM((2, 2, half, width), F32),
            pltpu.VMEM((2, 2, CHUNK, width), F32),
            pltpu.VMEM((CHUNK, width), F32),
            pltpu.VMEM((CHUNK, ALL), F32),
            pltpu.VMEM((half, ALL), F32),
            pltpu.VMEM((half, ALL), F32),
            pltpu.VMEM((3, half, ALL), F32),
            pltpu.VMEM((half, ALL), F32),
            pltpu.VMEM((half, ALL), F32),
            pltpu.SemaphoreType.DMA((64,)),
            pltpu.SemaphoreType.DMA((64,)),
        ],
        compiler_params=pltpu.CompilerParams(collective_id=1, has_side_effects=True, vmem_limit_bytes=48 * MIB),
        name="panels",
    )(partial.reshape(2, 8, CHUNK, width), x_rows)


def inverse_kernel(s_ref, ur_ref, mh_ref, ml_ref, a_ref, g_ref):
    half = CHUNK // 2
    for c in range(8):
        for k in range(2):
            a_ref[pl.ds(c * CHUNK + k * half, half)] = s_ref[k, c]
    rows = lax.broadcasted_iota(jnp.int32, (ALL, ALL), 0)
    cols = lax.broadcasted_iota(jnp.int32, (ALL, ALL), 1)
    eye = jnp.where(rows == cols, 1.0, 0.0).astype(F32)
    a_ref[...] = a_ref[...] + eye
    bound = jnp.max(jnp.sum(jnp.abs(a_ref[...]), axis=0, keepdims=True))
    scale = 2.0 / (1.0 + bound)
    g_ref[...] = scale * (2.0 * eye - scale * a_ref[...])

    def more(state):
        step, size = state
        return (step < 60) & (size > 1e-7)

    def refine(state):
        step, _ = state
        g = g_ref[...]
        error = eye - jnp.dot(a_ref[...], g, precision=lax.Precision.HIGHEST, preferred_element_type=F32)
        g_ref[...] = g + dot3(split(g), split(error))
        return step + 1, jnp.sum(error * error)

    lax.while_loop(more, refine, (jnp.int32(0), F32(1.0)))
    mh, ml = split(dot3(split(ur_ref[...].T), split(g_ref[...])))
    mh_ref[...] = mh
    ml_ref[...] = ml


def gain_of(gram, rows_t):
    width = rows_t.shape[1]
    vmem = pl.BlockSpec(memory_space=pltpu.VMEM)
    return pl.pallas_call(
        inverse_kernel,
        out_shape=(jax.ShapeDtypeStruct((width, ALL), BF16),) * 2,
        in_specs=[vmem] * 2,
        out_specs=(vmem,) * 2,
        scratch_shapes=[pltpu.VMEM((ALL, ALL), F32), pltpu.VMEM((ALL, ALL), F32)],
        compiler_params=pltpu.CompilerParams(vmem_limit_bytes=48 * MIB),
        name="gain",
    )(gram, rows_t)


def update_kernel(mh_ref, ml_ref, u_ref, r_ref, resid_ref, w_ref, out_ref, head_ref):
    gain = (mh_ref[...], ml_ref[...])

    @pl.when((pl.program_id(0) == 0) & (pl.program_id(1) == 0))
    def _():
        head_ref[...] = w_ref[...] + dot3(gain, split(resid_ref[...]))

    out_ref[...] = r_ref[...] - dot3(gain, split(u_ref[0]))


def update(gain_hi, gain_lo, cols_t, tile, resid, head):
    rows = tile.shape[0]
    width = tile.shape[1] // 2
    block = width // 3
    whole = lambda h, j: (0, 0)
    return pl.pallas_call(
        update_kernel,
        grid=(2, 3),
        out_shape=(jax.ShapeDtypeStruct(tile.shape, F32), jax.ShapeDtypeStruct(head.shape, F32)),
        in_specs=[
            pl.BlockSpec((rows, ALL), whole),
            pl.BlockSpec((rows, ALL), whole),
            pl.BlockSpec((1, ALL, block), lambda h, j: (h, 0, j)),
            pl.BlockSpec((rows, block), lambda h, j: (0, h * 3 + j)),
            pl.BlockSpec(resid.shape, whole),
            pl.BlockSpec(head.shape, whole),
        ],
        out_specs=(pl.BlockSpec((rows, block), lambda h, j: (0, h * 3 + j)), pl.BlockSpec(head.shape, whole)),
        compiler_params=pltpu.CompilerParams(vmem_limit_bytes=48 * MIB),
        name="update",
    )(gain_hi, gain_lo, cols_t, tile, resid, head)


def on_device(features_t, labels, inv_corr, heads):
    width = heads.shape[1]
    classes = lax.axis_index("col") * width + jnp.arange(width, dtype=jnp.int32)
    targets = (labels[:, None] == classes[None, :]).astype(F32)
    x_rows = gather_rows(features_t)
    partial, fitted = partial_panel(x_rows, inv_corr, heads)
    resid = targets - lax.psum(fitted, "row")
    cols_t, rows_t, gram = panels(partial, x_rows)
    block = partial.shape[2]
    gain_hi, gain_lo = gain_of(gram, rows_t.reshape(ALL, block))
    return update(gain_hi, gain_lo, cols_t.reshape(2, ALL, block), inv_corr, resid, heads)


def solution(mesh):
    placed = (P(("row", "col"), None), P(), P("row", "col"), P("row", "col"))
    return jax.shard_map(
        on_device,
        mesh=mesh,
        in_specs=placed,
        out_specs=(P("row", "col"), P("row", "col")),
        check_vma=False,
    )
```

```python
import jax
import jax.numpy as jnp
from jax import lax
from jax.experimental import pallas as pl
from jax.experimental.pallas import tpu as pltpu
from jax.sharding import PartitionSpec as P

F32 = jnp.float32
BF16 = jnp.bfloat16
MESH = pl.DeviceIdType.MESH
ALL = 512
CHUNK = 64
MIB = 1 << 20
VMEM_PANELS = 48 * MIB
VMEM_UPDATE = 48 * MIB


def split(value):
    hi = value.astype(BF16)
    lo = (value - hi.astype(F32)).astype(BF16)
    return hi, lo


def mm(left, right):
    return jnp.dot(left, right, preferred_element_type=F32)


def dot3(left, right):
    (lh, ll), (rh, rl) = left, right
    return mm(lh, rh) + (mm(lh, rl) + mm(ll, rh))


class Place:
    def __init__(self):
        self.row, self.col = row, col = lax.axis_index("row"), lax.axis_index("col")
        self.core = core = lax.rem(row, 2)
        self.chip_row = chip_row = row // 2
        self.y_hi, self.x = y_hi, x = chip_row // 4, lax.rem(chip_row, 4)
        self.y_lo, self.z = y_lo, z = col // 4, lax.rem(col, 4)
        self.sibling = (chip_row * 2 + (1 - core), col)
        self.x_up = ((y_hi * 4 + lax.rem(x + 1, 4)) * 2 + core, col)
        self.x_down = ((y_hi * 4 + lax.rem(x + 3, 4)) * 2 + core, col)
        self.x_far = ((y_hi * 4 + lax.rem(x + 2, 4)) * 2 + core, col)
        self.y_far = (((1 - y_hi) * 4 + x) * 2 + core, col)
        self.z_up = (row, y_lo * 4 + lax.rem(z + 1, 4))
        self.z_down = (row, y_lo * 4 + lax.rem(z + 3, 4))
        self.y_near = (row, (1 - y_lo) * 4 + z)
        self.y_next = (((1 - y_hi) * 4 + x) * 2 + core, (1 - y_lo) * 4 + z)
        self.swapped = ((y_hi * 4 + z) * 2 + core, y_lo * 4 + x)
        self.inner = y_hi != y_lo
        self.off_diagonal = x != z


class Copies:
    def __init__(self, send_sems, recv_sems):
        self.send_sems, self.recv_sems = send_sems, recv_sems
        self.count = 0
        self.started = []

    def take(self):
        self.count += 1
        return self.count - 1

    def make(self, index, src, dst, device):
        return pltpu.make_async_remote_copy(
            src_ref=src, dst_ref=dst, send_sem=self.send_sems.at[index], recv_sem=self.recv_sems.at[index],
            device_id=device, device_id_type=MESH)

    def start(self, src, dst, device):
        index = self.take()
        copy = self.make(index, src, dst, device)
        copy.start()
        self.started.append(copy)
        return index

    def arrived(self, index, landing, device):
        self.make(index, landing, landing, device).wait_recv()

    def finish(self):
        for copy in self.started:
            copy.wait_send()


def greet(devices, maybe):
    barrier = pltpu.get_barrier_semaphore()
    total = jnp.int32(len(devices))
    for device in devices:
        pl.semaphore_signal(barrier, inc=1, device_id=device, device_id_type=MESH)
    for there, device in maybe:
        total = total + jnp.where(there, 1, 0)

        @pl.when(there)
        def _():
            pl.semaphore_signal(barrier, inc=1, device_id=device, device_id_type=MESH)

    pl.semaphore_wait(barrier, total)


class Gather:
    def __init__(self, copies, buf, pair_at, ring_at, pair, up, down, rows):
        self.c, self.buf, self.rows = copies, buf, rows
        self.a, self.b = pair_at, ring_at
        self.pair, self.up, self.down = pair, up, down

    def slot(self, pair_step, ring_step):
        a = self.a if pair_step == 0 else 1 - self.a
        return a * 4 + lax.rem(self.b + ring_step, 4)

    def part(self, pair_step, ring_step, half=None):
        at = self.slot(pair_step, ring_step)
        if half is None:
            return self.buf.at[at]
        n = self.rows // 2
        return self.buf.at[at, pl.ds(half * n, n)]

    def same(self, part, device):
        return self.c.start(part, part, device)

    def own(self):
        mine = self.part(0, 0)
        self.i_up = self.same(mine, self.up)
        self.i_down = self.same(mine, self.down)
        self.i_pair = self.same(mine, self.pair)

    def forward_own(self):
        self.c.arrived(self.i_up, self.part(0, 3), self.down)
        self.h_up = self.same(self.part(0, 3, 0), self.up)
        self.c.arrived(self.i_down, self.part(0, 1), self.up)
        self.h_down = self.same(self.part(0, 1, 1), self.down)

    def pair_across(self):
        self.c.arrived(self.i_pair, self.part(1, 0), self.pair)
        self.q_up = self.same(self.part(1, 0), self.up)
        self.q_down = self.same(self.part(1, 0), self.down)

    def far_own(self):
        self.c.arrived(self.h_up, self.part(0, 2, 0), self.down)
        self.c.arrived(self.h_down, self.part(0, 2, 1), self.up)

    def far_by_pair(self):
        self.f_pair = self.same(self.part(0, 2), self.pair)

    def end_by_pair(self):
        self.c.arrived(self.q_up, self.part(1, 3), self.down)
        self.c.arrived(self.q_down, self.part(1, 1), self.up)
        self.c.arrived(self.f_pair, self.part(1, 2), self.pair)

    def forward_pair(self):
        self.c.arrived(self.q_up, self.part(1, 3), self.down)
        self.g_up = self.same(self.part(1, 3, 0), self.up)
        self.c.arrived(self.q_down, self.part(1, 1), self.up)
        self.g_down = self.same(self.part(1, 1, 1), self.down)

    def end_by_ring(self):
        self.c.arrived(self.g_up, self.part(1, 2, 0), self.down)
        self.c.arrived(self.g_down, self.part(1, 2, 1), self.up)


def stack_left(ref, value):
    hi, lo = split(value)
    depth = value.shape[1]
    ref[:, 0:depth] = hi
    ref[:, depth:2 * depth] = hi
    ref[:, 2 * depth:] = lo


def stack_right(value):
    hi, lo = split(value)
    return jnp.concatenate([hi, lo, hi], 0)


def eye_of(order):
    rows = lax.broadcasted_iota(jnp.int32, (order, order), 0)
    cols = lax.broadcasted_iota(jnp.int32, (order, order), 1)
    return jnp.where(rows == cols, 1.0, 0.0).astype(F32)


BLOCKS = 3
BLOCK = 384


def panels_kernel(x_ref, w_ref, r_ref, uc_ref, ur_ref, a_ref, g_ref, fit_ref,
                  rv, xr, xs, part, from_sib, acc, ra, rb, ry, relay, s_all, sp, rs0, sh, rs1, sh2, rs2,
                  fx, rf0, fh, rf1, fh2, rf2, local_sems, send_sems, recv_sems):
    at = Place()
    k, p, col = at.core, at.chip_row, at.col
    rows = x_ref.shape[0]
    turns = [(1 - k, j) for j in range(BLOCKS)] + [(k, j) for j in range(BLOCKS)]

    def columns(h, j):
        return pl.ds(pl.multiple_of((h * BLOCKS + j) * BLOCK, 128), BLOCK)

    loads = []
    for i, (h, j) in enumerate(turns):
        loads.append(pltpu.make_async_copy(r_ref.at[:, columns(h, j)], rv.at[i], local_sems.at[i]))
        loads[-1].start()
    xr[col] = x_ref[...]
    greet([at.sibling, at.x_up, at.x_down, at.x_far, at.y_far, at.z_up, at.z_down, at.y_near],
          [(at.inner, at.y_next), (at.off_diagonal, at.swapped)])
    copies = Copies(send_sems, recv_sems)

    gx = Gather(copies, xr, at.y_lo, at.z, at.y_near, at.z_up, at.z_down, rows)
    gx.own()
    gx.forward_own()
    gx.pair_across()
    gx.far_own()
    gx.far_by_pair()
    gx.end_by_pair()
    stack_left(xs, xr[...].reshape(8 * rows, ALL).T)

    fx[...] = mm(xs[...], stack_right(w_ref[...]))
    n = ALL // 2
    f0 = copies.start(fx.at[pl.ds(pl.multiple_of((1 - k) * n, n), n)], rf0, at.sibling)

    def product(i):
        h, j = turns[i]
        loads[i].wait()
        value = mm(xs[...], stack_right(rv[i]))
        part[h, :, :, j * BLOCK:(j + 1) * BLOCK] = value.reshape(8, CHUNK, BLOCK)

    sib = []
    for j in range(BLOCKS):
        product(j)
        piece = (slice(None), slice(None), slice(j * BLOCK, (j + 1) * BLOCK))
        sib.append(copies.start(part.at[(1 - k,) + piece], from_sib.at[piece], at.sibling))
        if j == 0:
            copies.arrived(f0, rf0, at.sibling)
            fh[...] = fx[pl.ds(pl.multiple_of(k * n, n), n)] + rf0[...]
            f1 = [copies.start(fh, rf1.at[i], d) for i, d in enumerate((at.x_up, at.x_down, at.x_far))]
    for i, d in enumerate((at.x_down, at.x_up, at.x_far)):
        copies.arrived(f1[i], rf1.at[i], d)
    fh2[...] = (fh[...] + rf1[2]) + (rf1[0] + rf1[1])
    f2 = copies.start(fh2, rf2, at.y_far)
    for j in range(BLOCKS):
        product(BLOCKS + j)
    copies.arrived(f2, rf2, at.y_far)
    mine_fit = fit_ref.at[pl.ds(pl.multiple_of(k * n, n), n)]
    mine_fit[...] = fh2[...] + rf2[...]
    f3 = copies.start(mine_fit, mine_fit, at.sibling)
    for j in range(BLOCKS):
        copies.arrived(sib[j], from_sib.at[:, :, j * BLOCK:(j + 1) * BLOCK], at.sibling)

    def chunk(y_step, x_step):
        y = at.y_hi if y_step == 0 else 1 - at.y_hi
        return y * 4 + lax.rem(at.x + x_step, 4)

    def add_sibling(y, x_step):
        ch = chunk(y, x_step)
        acc[ch] = part[k, ch] + from_sib[ch]
        return ch

    half = CHUNK // 2
    low, high = pl.ds(0, half), pl.ds(half, half)
    a_up, a_down, b_up, b_down = {}, {}, {}, {}
    for y in (1, 0):
        ch = add_sibling(y, 2)
        a_up[y] = copies.start(acc.at[ch, low], ra.at[0, y], at.x_up)
        a_down[y] = copies.start(acc.at[ch, high], ra.at[1, y], at.x_down)
    for y in (1, 0):
        for x_step in (1, 3, 0):
            add_sibling(y, x_step)
    for y in (1, 0):
        ch = chunk(y, 1)
        copies.arrived(a_up[y], ra.at[0, y], at.x_down)
        acc[ch, low] = acc[ch, low] + ra[0, y]
        b_up[y] = copies.start(acc.at[ch], rb.at[0, y], at.x_up)
        ch = chunk(y, 3)
        copies.arrived(a_down[y], ra.at[1, y], at.x_up)
        acc[ch, high] = acc[ch, high] + ra[1, y]
        b_down[y] = copies.start(acc.at[ch], rb.at[1, y], at.x_down)

    def add_x(y):
        ch = chunk(y, 0)
        copies.arrived(b_up[y], rb.at[0, y], at.x_down)
        copies.arrived(b_down[y], rb.at[1, y], at.x_up)
        return acc[ch] + (rb[0, y] + rb[1, y])

    ch = chunk(1, 0)
    acc[ch] = add_x(1)
    c_far = copies.start(acc.at[ch], ry, at.y_far)
    mine = add_x(0)
    copies.arrived(c_far, ry, at.y_far)
    mine = mine + ry[...]
    uc_ref[k, p] = mine

    own_block = uc_ref.at[k]
    t0 = copies.take()
    step_y = copies.make(t0, uc_ref.at[k, p], relay, at.y_next)

    @pl.when(at.inner)
    def _():
        step_y.start()

    gc = Gather(copies, own_block, at.y_hi, at.x, at.y_far, at.x_up, at.x_down, CHUNK)
    gr = Gather(copies, ur_ref, at.y_lo, at.z, at.y_near, at.z_up, at.z_down, CHUNK)

    def to_sibling(pair_step, ring_step):
        piece = gc.part(pair_step, ring_step)
        return copies.start(piece, piece, at.sibling)

    gc.own()
    u = {(0, 0): to_sibling(0, 0)}

    @pl.when(at.inner)
    def _():
        copies.make(t0, relay, relay, at.y_next).wait_recv()
        step_y.wait_send()

    @pl.when(jnp.logical_not(at.inner))
    def _():
        relay[...] = uc_ref[k, p]

    t1 = copies.take()
    step_xz = copies.make(t1, relay, ur_ref.at[at.y_lo * 4 + at.x], at.swapped)

    @pl.when(at.off_diagonal)
    def _():
        step_xz.start()

    gc.forward_own()
    u[(0, 3)] = to_sibling(0, 3)
    u[(0, 1)] = to_sibling(0, 1)

    @pl.when(at.off_diagonal)
    def _():
        copies.make(t1, ur_ref.at[col], ur_ref.at[col], at.swapped).wait_recv()
        step_xz.wait_send()

    @pl.when(jnp.logical_not(at.off_diagonal))
    def _():
        ur_ref[col] = relay[...]

    gr.own()

    sp[...] = dot3(split(ur_ref[col]), split(xr[...].reshape(8 * rows, ALL)))
    s0 = copies.start(sp.at[pl.ds(pl.multiple_of((1 - k) * half, half), half)], rs0, at.sibling)
    gc.pair_across()
    u[(1, 0)] = to_sibling(1, 0)
    copies.arrived(s0, rs0, at.sibling)
    sh[...] = sp[pl.ds(pl.multiple_of(k * half, half), half)] + rs0[...]
    s1 = [copies.start(sh, rs1.at[i], d) for i, d in enumerate((at.x_up, at.x_down, at.x_far))]
    gr.forward_own()
    gr.pair_across()
    for i, d in enumerate((at.x_down, at.x_up, at.x_far)):
        copies.arrived(s1[i], rs1.at[i], d)
    sh2[...] = (sh[...] + rs1[2]) + (rs1[0] + rs1[1])
    s2 = copies.start(sh2, rs2, at.y_far)
    copies.arrived(s2, rs2, at.y_far)
    s_all[k, col] = sh2[...] + rs2[...]
    gs = Gather(copies, s_all.at[k], at.y_lo, at.z, at.y_near, at.z_up, at.z_down, half)
    gs.own()
    gc.far_own()
    u[(0, 2)] = to_sibling(0, 2)
    gc.forward_pair()
    u[(1, 3)] = to_sibling(1, 3)
    u[(1, 1)] = to_sibling(1, 1)
    gs.forward_own()
    gs.pair_across()
    gs.far_own()
    gs.forward_pair()
    gs.end_by_ring()
    s4 = copies.start(s_all.at[k], s_all.at[k], at.sibling)
    gr.far_own()
    gr.forward_pair()
    gc.end_by_ring()
    u[(1, 2)] = to_sibling(1, 2)
    copies.arrived(s4, s_all.at[1 - k], at.sibling)

    for c in range(8):
        for h in range(2):
            a_ref[pl.ds(c * CHUNK + h * half, half)] = s_all[h, c]
    eye = eye_of(ALL)
    a_ref[...] = a_ref[...] + eye
    bound = jnp.max(jnp.sum(jnp.abs(a_ref[...]), axis=0, keepdims=True))
    scale = 2.0 / (1.0 + bound)
    g_ref[...] = scale * (2.0 * eye - scale * a_ref[...])

    @pl.loop(0, 3)
    def _(_):
        g = split(g_ref[...])
        error = eye_of(ALL) - dot3(split(a_ref[...]), g)
        g_ref[...] = g_ref[...] + dot3(g, split(error))

    gr.end_by_ring()
    other = uc_ref.at[1 - k]
    for (pair_step, ring_step), index in u.items():
        copies.arrived(index, other.at[gc.slot(pair_step, ring_step)], at.sibling)
    copies.arrived(f3, fit_ref.at[pl.ds(pl.multiple_of((1 - k) * n, n), n)], at.sibling)
    copies.finish()


def panels(features_t, head, tile):
    rows, examples = features_t.shape
    depth, width = tile.shape[0], tile.shape[1] // 2
    classes = head.shape[1]
    half = CHUNK // 2
    vmem = pl.BlockSpec(memory_space=pltpu.VMEM)
    dma = pltpu.SemaphoreType.DMA
    return pl.pallas_call(
        panels_kernel,
        out_shape=(
            jax.ShapeDtypeStruct((2, 8, CHUNK, width), F32),
            jax.ShapeDtypeStruct((8, CHUNK, width), F32),
            jax.ShapeDtypeStruct((ALL, ALL), F32),
            jax.ShapeDtypeStruct((ALL, ALL), F32),
            jax.ShapeDtypeStruct((ALL, classes), F32),
        ),
        in_specs=[vmem, vmem, pl.BlockSpec(memory_space=pl.ANY)],
        out_specs=(vmem,) * 5,
        scratch_shapes=[
            pltpu.VMEM((2 * BLOCKS, depth, BLOCK), F32),
            pltpu.VMEM((8, rows, examples), F32),
            pltpu.VMEM((examples, 3 * depth), BF16),
            pltpu.VMEM((2, 8, CHUNK, width), F32),
            pltpu.VMEM((8, CHUNK, width), F32),
            pltpu.VMEM((8, CHUNK, width), F32),
            pltpu.VMEM((2, 2, half, width), F32),
            pltpu.VMEM((2, 2, CHUNK, width), F32),
            pltpu.VMEM((CHUNK, width), F32),
            pltpu.VMEM((CHUNK, width), F32),
            pltpu.VMEM((2, 8, half, ALL), F32),
            pltpu.VMEM((CHUNK, ALL), F32),
            pltpu.VMEM((half, ALL), F32),
            pltpu.VMEM((half, ALL), F32),
            pltpu.VMEM((3, half, ALL), F32),
            pltpu.VMEM((half, ALL), F32),
            pltpu.VMEM((half, ALL), F32),
            pltpu.VMEM((ALL, classes), F32),
            pltpu.VMEM((ALL // 2, classes), F32),
            pltpu.VMEM((ALL // 2, classes), F32),
            pltpu.VMEM((3, ALL // 2, classes), F32),
            pltpu.VMEM((ALL // 2, classes), F32),
            pltpu.VMEM((ALL // 2, classes), F32),
            dma((2 * BLOCKS,)),
            dma((80,)),
            dma((80,)),
        ],
        compiler_params=pltpu.CompilerParams(collective_id=0, has_side_effects=True, vmem_limit_bytes=VMEM_PANELS),
        name="panels",
    )(features_t, head, tile)


def update_kernel(a_ref, g_ref, ur_ref, u_ref, r_ref, targets_ref, fit_ref, w_ref, out_ref, head_ref, inv_ref, gain_ref):
    at = pl.program_id(0)

    @pl.when(at == 0)
    def _():
        inv_ref[...] = g_ref[...]

        def more(state):
            step, size = state
            return (step < 60) & (size > 1e-7)

        def refine(state):
            step, _ = state
            g = inv_ref[...]
            error = eye_of(ALL) - jnp.dot(a_ref[...], g, precision=lax.Precision.HIGHEST, preferred_element_type=F32)
            inv_ref[...] = g + dot3(split(g), split(error))
            return step + 1, jnp.sum(error * error)

        lax.while_loop(more, refine, (jnp.int32(0), F32(1.0)))
        stack_left(gain_ref, dot3(split(ur_ref[...].T), split(inv_ref[...])))
        head_ref[...] = w_ref[...] + mm(gain_ref[...], stack_right(targets_ref[...] - fit_ref[...]))

    block = r_ref[:, pl.ds(pl.multiple_of(at * BLOCK, 128), BLOCK)]
    out_ref[...] = block - mm(gain_ref[...], stack_right(u_ref[0]))


def update(inv_system, inverse, rows_t, cols_t, tile, targets, fitted, head):
    rows = tile.shape[0]
    vmem = pl.BlockSpec(memory_space=pltpu.VMEM)
    return pl.pallas_call(
        update_kernel,
        grid=(2 * BLOCKS,),
        out_shape=(jax.ShapeDtypeStruct(tile.shape, F32), jax.ShapeDtypeStruct(head.shape, F32)),
        in_specs=[
            vmem,
            vmem,
            vmem,
            pl.BlockSpec((1, ALL, BLOCK), lambda i: (i // BLOCKS, 0, lax.rem(i, BLOCKS))),
            vmem,
            vmem,
            vmem,
            vmem,
        ],
        out_specs=(pl.BlockSpec((rows, BLOCK), lambda i: (0, i)), pl.BlockSpec(head.shape, lambda i: (0, 0))),
        scratch_shapes=[pltpu.VMEM((ALL, ALL), F32), pltpu.VMEM((rows, 3 * ALL), BF16)],
        compiler_params=pltpu.CompilerParams(vmem_limit_bytes=VMEM_UPDATE),
        name="update",
    )(inv_system, inverse, rows_t, cols_t, tile, targets, fitted, head)


def on_device(features_t, labels, inv_corr, heads):
    width = heads.shape[1]
    classes = lax.axis_index("col") * width + jnp.arange(width, dtype=jnp.int32)
    targets = (labels[:, None] == classes[None, :]).astype(F32)
    cols_t, rows_t, system, inverse, fitted = panels(features_t, heads, inv_corr)
    block = cols_t.shape[3]
    return update(system, inverse, rows_t.reshape(ALL, block), cols_t.reshape(2, ALL, block), inv_corr, targets, fitted, heads)


def solution(mesh):
    placed = (P(("row", "col"), None), P(), P("row", "col"), P("row", "col"))
    return jax.shard_map(
        on_device,
        mesh=mesh,
        in_specs=placed,
        out_specs=(P("row", "col"), P("row", "col")),
        check_vma=False,
    )
```

```python
import jax
import jax.numpy as jnp
from jax import lax
from jax.experimental import pallas as pl
from jax.experimental.pallas import tpu as pltpu
from jax.sharding import PartitionSpec as P

F32 = jnp.float32
BF16 = jnp.bfloat16
MESH = pl.DeviceIdType.MESH
ALL = 512
CHUNK = 64
MIB = 1 << 20
VMEM_PANELS = 48 * MIB
VMEM_UPDATE = 48 * MIB


def split(value):
    hi = value.astype(BF16)
    lo = (value - hi.astype(F32)).astype(BF16)
    return hi, lo


def mm(left, right):
    return jnp.dot(left, right, preferred_element_type=F32)


def dot3(left, right):
    (lh, ll), (rh, rl) = left, right
    return mm(lh, rh) + (mm(lh, rl) + mm(ll, rh))


class Place:
    def __init__(self):
        self.row, self.col = row, col = lax.axis_index("row"), lax.axis_index("col")
        self.core = core = lax.rem(row, 2)
        self.chip_row = chip_row = row // 2
        self.y_hi, self.x = y_hi, x = chip_row // 4, lax.rem(chip_row, 4)
        self.y_lo, self.z = y_lo, z = col // 4, lax.rem(col, 4)
        self.sibling = (chip_row * 2 + (1 - core), col)
        self.x_up = ((y_hi * 4 + lax.rem(x + 1, 4)) * 2 + core, col)
        self.x_down = ((y_hi * 4 + lax.rem(x + 3, 4)) * 2 + core, col)
        self.x_far = ((y_hi * 4 + lax.rem(x + 2, 4)) * 2 + core, col)
        self.y_far = (((1 - y_hi) * 4 + x) * 2 + core, col)
        self.z_up = (row, y_lo * 4 + lax.rem(z + 1, 4))
        self.z_down = (row, y_lo * 4 + lax.rem(z + 3, 4))
        self.y_near = (row, (1 - y_lo) * 4 + z)
        self.y_next = (((1 - y_hi) * 4 + x) * 2 + core, (1 - y_lo) * 4 + z)
        self.swapped = ((y_hi * 4 + z) * 2 + core, y_lo * 4 + x)
        self.inner = y_hi != y_lo
        self.off_diagonal = x != z
        between = lax.rem(y_hi + y_lo, 2)
        far_y, near_y = lax.rem(y_hi + between, 2), lax.rem(y_lo + 1 - between, 2)
        self.sum_to = ((far_y * 4 + x) * 2 + core, near_y * 4 + z)
        back_y, side_y = lax.rem(y_hi + 1 - between, 2), lax.rem(y_lo + between, 2)
        self.spread_to = ((back_y * 4 + x) * 2 + core, side_y * 4 + z)
        self.spread_slot = far_y * 4 + x


class Copies:
    def __init__(self, send_sems, recv_sems):
        self.send_sems, self.recv_sems = send_sems, recv_sems
        self.count = 0
        self.started = []

    def take(self):
        self.count += 1
        return self.count - 1

    def make(self, index, src, dst, device):
        return pltpu.make_async_remote_copy(
            src_ref=src, dst_ref=dst, send_sem=self.send_sems.at[index], recv_sem=self.recv_sems.at[index],
            device_id=device, device_id_type=MESH)

    def start(self, src, dst, device):
        index = self.take()
        copy = self.make(index, src, dst, device)
        copy.start()
        self.started.append(copy)
        return index

    def arrived(self, index, landing, device):
        self.make(index, landing, landing, device).wait_recv()

    def finish(self):
        for copy in self.started:
            copy.wait_send()


def greet(devices, maybe):
    barrier = pltpu.get_barrier_semaphore()
    total = jnp.int32(len(devices))
    for device in devices:
        pl.semaphore_signal(barrier, inc=1, device_id=device, device_id_type=MESH)
    for there, device in maybe:
        total = total + jnp.where(there, 1, 0)

        @pl.when(there)
        def _():
            pl.semaphore_signal(barrier, inc=1, device_id=device, device_id_type=MESH)

    pl.semaphore_wait(barrier, total)


class Gather:
    def __init__(self, copies, buf, pair_at, ring_at, pair, up, down, rows):
        self.c, self.buf, self.rows = copies, buf, rows
        self.a, self.b = pair_at, ring_at
        self.pair, self.up, self.down = pair, up, down

    def slot(self, pair_step, ring_step):
        a = self.a if pair_step == 0 else 1 - self.a
        return a * 4 + lax.rem(self.b + ring_step, 4)

    def part(self, pair_step, ring_step, half=None):
        at = self.slot(pair_step, ring_step)
        if half is None:
            return self.buf.at[at]
        n = self.rows // 2
        return self.buf.at[at, pl.ds(half * n, n)]

    def same(self, part, device):
        return self.c.start(part, part, device)

    def own(self):
        self.own_ring()
        self.i_pair = self.same(self.part(0, 0), self.pair)

    def own_ring(self):
        mine = self.part(0, 0)
        self.i_up = self.same(mine, self.up)
        self.i_down = self.same(mine, self.down)

    def forward_own(self):
        self.c.arrived(self.i_up, self.part(0, 3), self.down)
        self.h_up = self.same(self.part(0, 3, 0), self.up)
        self.c.arrived(self.i_down, self.part(0, 1), self.up)
        self.h_down = self.same(self.part(0, 1, 1), self.down)

    def pair_across(self):
        self.c.arrived(self.i_pair, self.part(1, 0), self.pair)
        self.q_up = self.same(self.part(1, 0), self.up)
        self.q_down = self.same(self.part(1, 0), self.down)

    def far_own(self):
        self.c.arrived(self.h_up, self.part(0, 2, 0), self.down)
        self.c.arrived(self.h_down, self.part(0, 2, 1), self.up)

    def far_by_pair(self):
        self.f_pair = self.same(self.part(0, 2), self.pair)

    def end_by_pair(self):
        self.c.arrived(self.q_up, self.part(1, 3), self.down)
        self.c.arrived(self.q_down, self.part(1, 1), self.up)
        self.c.arrived(self.f_pair, self.part(1, 2), self.pair)

    def forward_pair(self):
        self.c.arrived(self.q_up, self.part(1, 3), self.down)
        self.g_up = self.same(self.part(1, 3, 0), self.up)
        self.c.arrived(self.q_down, self.part(1, 1), self.up)
        self.g_down = self.same(self.part(1, 1, 1), self.down)

    def end_by_ring(self):
        self.c.arrived(self.g_up, self.part(1, 2, 0), self.down)
        self.c.arrived(self.g_down, self.part(1, 2, 1), self.up)


def stack_left(ref, value):
    hi, lo = split(value)
    depth = value.shape[1]
    ref[:, 0:depth] = hi
    ref[:, depth:2 * depth] = hi
    ref[:, 2 * depth:] = lo


def stack_right(value):
    hi, lo = split(value)
    return jnp.concatenate([hi, lo, hi], 0)


def eye_of(order):
    rows = lax.broadcasted_iota(jnp.int32, (order, order), 0)
    cols = lax.broadcasted_iota(jnp.int32, (order, order), 1)
    return jnp.where(rows == cols, 1.0, 0.0).astype(F32)


BLOCKS = 3
BLOCK = 384


def panels_kernel(x_ref, w_ref, r_ref, uc_ref, ur_ref, a_ref, g_ref, size_ref, fit_ref,
                  wv, rv, xr, xs, part, from_sib, acc, ra, rb, ry, ry2, relay, s_all, sp, rs0, sh, rs1, sh2, rs2,
                  fx, rf0, fh, rf1, fh2, rf2, local_sems, send_sems, recv_sems):
    at = Place()
    k, p, col = at.core, at.chip_row, at.col
    rows = x_ref.shape[0]
    turns = [(1 - k, j) for j in range(BLOCKS)] + [(k, j) for j in range(BLOCKS)]

    def columns(h, j):
        return pl.ds(pl.multiple_of((h * BLOCKS + j) * BLOCK, 128), BLOCK)

    own_x = pltpu.make_async_copy(x_ref, xr.at[col], local_sems.at[2 * BLOCKS])
    own_x.start()
    own_w = pltpu.make_async_copy(w_ref, wv, local_sems.at[2 * BLOCKS + 1])
    own_w.start()
    loads = []
    for i, (h, j) in enumerate(turns):
        loads.append(pltpu.make_async_copy(r_ref.at[:, columns(h, j)], rv.at[i], local_sems.at[i]))
        loads[-1].start()
    greet([at.sibling, at.x_up, at.x_down, at.x_far, at.y_far, at.z_up, at.z_down, at.y_near],
          [(at.inner, at.y_next), (at.off_diagonal, at.swapped)])
    own_x.wait()
    copies = Copies(send_sems, recv_sems)

    gx = Gather(copies, xr, at.y_lo, at.z, at.y_near, at.z_up, at.z_down, rows)
    gx.own()
    gx.forward_own()
    gx.pair_across()
    gx.far_own()
    gx.far_by_pair()
    gx.end_by_pair()
    stack_left(xs, xr[...].reshape(8 * rows, ALL).T)

    own_w.wait()
    fx[...] = mm(xs[...], stack_right(wv[...]))
    n = ALL // 2
    f0 = copies.start(fx.at[pl.ds(pl.multiple_of((1 - k) * n, n), n)], rf0, at.sibling)

    def product(i):
        h, j = turns[i]
        loads[i].wait()
        value = mm(xs[...], stack_right(rv[i]))
        part[h, :, :, j * BLOCK:(j + 1) * BLOCK] = value.reshape(8, CHUNK, BLOCK)

    sib = []
    for j in range(BLOCKS):
        product(j)
        piece = (slice(None), slice(None), slice(j * BLOCK, (j + 1) * BLOCK))
        sib.append(copies.start(part.at[(1 - k,) + piece], from_sib.at[piece], at.sibling))
        if j == 0:
            copies.arrived(f0, rf0, at.sibling)
            fh[...] = fx[pl.ds(pl.multiple_of(k * n, n), n)] + rf0[...]
            f1 = [copies.start(fh, rf1.at[i], d) for i, d in enumerate((at.x_up, at.x_down, at.x_far))]
    for j in range(BLOCKS):
        product(BLOCKS + j)
    for j in range(BLOCKS):
        copies.arrived(sib[j], from_sib.at[:, :, j * BLOCK:(j + 1) * BLOCK], at.sibling)

    def chunk(y_step, x_step):
        y = at.y_hi if y_step == 0 else 1 - at.y_hi
        return y * 4 + lax.rem(at.x + x_step, 4)

    def add_sibling(y, x_step):
        ch = chunk(y, x_step)
        acc[ch] = part[k, ch] + from_sib[ch]
        return ch

    half = CHUNK // 2
    low, high = pl.ds(0, half), pl.ds(half, half)
    a_up, a_down, b_up, b_down = {}, {}, {}, {}
    for y in (1, 0):
        ch = add_sibling(y, 2)
        a_up[y] = copies.start(acc.at[ch, low], ra.at[0, y], at.x_up)
        a_down[y] = copies.start(acc.at[ch, high], ra.at[1, y], at.x_down)
    for y in (1, 0):
        for x_step in (1, 3, 0):
            add_sibling(y, x_step)
    for i, d in enumerate((at.x_down, at.x_up, at.x_far)):
        copies.arrived(f1[i], rf1.at[i], d)
    fh2[...] = (fh[...] + rf1[2]) + (rf1[0] + rf1[1])
    f2 = copies.start(fh2, rf2, at.y_far)
    for y in (1, 0):
        ch = chunk(y, 1)
        copies.arrived(a_up[y], ra.at[0, y], at.x_down)
        acc[ch, low] = acc[ch, low] + ra[0, y]
        b_up[y] = copies.start(acc.at[ch], rb.at[0, y], at.x_up)
        ch = chunk(y, 3)
        copies.arrived(a_down[y], ra.at[1, y], at.x_up)
        acc[ch, high] = acc[ch, high] + ra[1, y]
        b_down[y] = copies.start(acc.at[ch], rb.at[1, y], at.x_down)

    def add_x(y):
        ch = chunk(y, 0)
        copies.arrived(b_up[y], rb.at[0, y], at.x_down)
        copies.arrived(b_down[y], rb.at[1, y], at.x_up)
        return acc[ch] + (rb[0, y] + rb[1, y])

    other, own = chunk(1, 0), chunk(0, 0)
    acc[other] = add_x(1)
    c1 = copies.start(acc.at[other], ry, at.sum_to)
    acc[own] = add_x(0)
    c2 = copies.take()
    inner_sum = copies.make(c2, acc.at[own], ry2, at.y_next)

    @pl.when(at.inner)
    def _():
        inner_sum.start()

    copies.arrived(c1, ry, at.sum_to)

    @pl.when(at.inner)
    def _():
        copies.make(c2, ry2, ry2, at.y_next).wait_recv()
        relay[...] = ry[...] + ry2[...]
        inner_sum.wait_send()

    @pl.when(jnp.logical_not(at.inner))
    def _():
        relay[...] = acc[own] + ry[...]
        uc_ref[k, p] = relay[...]

    t1 = copies.take()
    step_xz = copies.make(t1, relay, ur_ref.at[at.y_lo * 4 + at.x], at.swapped)

    @pl.when(at.off_diagonal)
    def _():
        step_xz.start()

    d1 = copies.start(relay, uc_ref.at[k, at.spread_slot], at.spread_to)
    d2 = copies.take()
    inner_back = copies.make(d2, relay, uc_ref.at[k, at.spread_slot], at.y_next)

    @pl.when(at.inner)
    def _():
        inner_back.start()

    own_block = uc_ref.at[k]
    gc = Gather(copies, own_block, at.y_hi, at.x, at.y_far, at.x_up, at.x_down, CHUNK)
    gr = Gather(copies, ur_ref, at.y_lo, at.z, at.y_near, at.z_up, at.z_down, CHUNK)
    gc.i_pair = d1

    def to_sibling(pair_step, ring_step):
        piece = gc.part(pair_step, ring_step)
        return copies.start(piece, piece, at.sibling)

    copies.arrived(f2, rf2, at.y_far)
    mine_fit = fit_ref.at[pl.ds(pl.multiple_of(k * n, n), n)]
    mine_fit[...] = fh2[...] + rf2[...]
    f3 = copies.start(mine_fit, mine_fit, at.sibling)

    @pl.when(at.inner)
    def _():
        copies.make(d2, uc_ref.at[k, p], uc_ref.at[k, p], at.y_next).wait_recv()
        inner_back.wait_send()

    gc.own_ring()
    u = {(0, 0): to_sibling(0, 0)}

    @pl.when(at.off_diagonal)
    def _():
        copies.make(t1, ur_ref.at[col], ur_ref.at[col], at.swapped).wait_recv()
        step_xz.wait_send()

    @pl.when(jnp.logical_not(at.off_diagonal))
    def _():
        ur_ref[col] = relay[...]

    gr.own()

    sp[...] = dot3(split(ur_ref[col]), split(xr[...].reshape(8 * rows, ALL)))
    s0 = copies.start(sp.at[pl.ds(pl.multiple_of((1 - k) * half, half), half)], rs0, at.sibling)
    copies.arrived(s0, rs0, at.sibling)
    sh[...] = sp[pl.ds(pl.multiple_of(k * half, half), half)] + rs0[...]
    s1 = [copies.start(sh, rs1.at[i], d) for i, d in enumerate((at.x_up, at.x_down, at.x_far))]
    for i, d in enumerate((at.x_down, at.x_up, at.x_far)):
        copies.arrived(s1[i], rs1.at[i], d)
    sh2[...] = (sh[...] + rs1[2]) + (rs1[0] + rs1[1])
    s2 = copies.start(sh2, rs2, at.y_far)
    gc.forward_own()
    gc.pair_across()
    for step in ((0, 3), (0, 1), (1, 0)):
        u[step] = to_sibling(*step)
    copies.arrived(s2, rs2, at.y_far)
    s_all[k, col] = sh2[...] + rs2[...]
    gs = Gather(copies, s_all.at[k], at.y_lo, at.z, at.y_near, at.z_up, at.z_down, half)
    gs.own()
    gs.forward_own()
    gs.pair_across()
    gs.far_own()
    gs.forward_pair()
    gs.end_by_ring()
    s4 = copies.start(s_all.at[k], s_all.at[k], at.sibling)
    gr.forward_own()
    gr.pair_across()
    gc.far_own()
    u[(0, 2)] = to_sibling(0, 2)
    gc.forward_pair()
    for step in ((1, 3), (1, 1)):
        u[step] = to_sibling(*step)
    copies.arrived(s4, s_all.at[1 - k], at.sibling)

    for c in range(8):
        for h in range(2):
            a_ref[pl.ds(c * CHUNK + h * half, half)] = s_all[h, c]
    eye = eye_of(ALL)
    a_ref[...] = a_ref[...] + eye
    bound = jnp.max(jnp.sum(jnp.abs(a_ref[...]), axis=0, keepdims=True))
    scale = 2.0 / (1.0 + bound)
    g_ref[...] = scale * (2.0 * eye - scale * a_ref[...])

    def refine(_):
        g = split(g_ref[...])
        error = eye_of(ALL) - dot3(split(a_ref[...]), g)
        g_ref[...] = g_ref[...] + dot3(g, split(error))
        size_ref[...] = jnp.broadcast_to(jnp.sum(error * error), size_ref.shape)

    pl.loop(0, 2)(refine)
    gr.far_own()
    gr.far_by_pair()
    pl.loop(0, 2)(refine)
    gc.end_by_ring()
    u[(1, 2)] = to_sibling(1, 2)
    gr.end_by_pair()
    other_block = uc_ref.at[1 - k]
    for (pair_step, ring_step), index in u.items():
        copies.arrived(index, other_block.at[gc.slot(pair_step, ring_step)], at.sibling)
    copies.arrived(f3, fit_ref.at[pl.ds(pl.multiple_of((1 - k) * n, n), n)], at.sibling)
    copies.finish()


def panels(features_t, head, tile):
    rows, examples = features_t.shape
    depth, width = tile.shape[0], tile.shape[1] // 2
    classes = head.shape[1]
    half = CHUNK // 2
    vmem = pl.BlockSpec(memory_space=pltpu.VMEM)
    dma = pltpu.SemaphoreType.DMA
    return pl.pallas_call(
        panels_kernel,
        out_shape=(
            jax.ShapeDtypeStruct((2, 8, CHUNK, width), F32),
            jax.ShapeDtypeStruct((8, CHUNK, width), F32),
            jax.ShapeDtypeStruct((ALL, ALL), F32),
            jax.ShapeDtypeStruct((ALL, ALL), F32),
            jax.ShapeDtypeStruct((8, 128), F32),
            jax.ShapeDtypeStruct((ALL, classes), F32),
        ),
        in_specs=[pl.BlockSpec(memory_space=pltpu.HBM)] * 3,
        out_specs=(vmem,) * 6,
        scratch_shapes=[
            pltpu.VMEM(head.shape, F32),
            pltpu.VMEM((2 * BLOCKS, depth, BLOCK), F32),
            pltpu.VMEM((8, rows, examples), F32),
            pltpu.VMEM((examples, 3 * depth), BF16),
            pltpu.VMEM((2, 8, CHUNK, width), F32),
            pltpu.VMEM((8, CHUNK, width), F32),
            pltpu.VMEM((8, CHUNK, width), F32),
            pltpu.VMEM((2, 2, half, width), F32),
            pltpu.VMEM((2, 2, CHUNK, width), F32),
            pltpu.VMEM((CHUNK, width), F32),
            pltpu.VMEM((CHUNK, width), F32),
            pltpu.VMEM((CHUNK, width), F32),
            pltpu.VMEM((2, 8, half, ALL), F32),
            pltpu.VMEM((CHUNK, ALL), F32),
            pltpu.VMEM((half, ALL), F32),
            pltpu.VMEM((half, ALL), F32),
            pltpu.VMEM((3, half, ALL), F32),
            pltpu.VMEM((half, ALL), F32),
            pltpu.VMEM((half, ALL), F32),
            pltpu.VMEM((ALL, classes), F32),
            pltpu.VMEM((ALL // 2, classes), F32),
            pltpu.VMEM((ALL // 2, classes), F32),
            pltpu.VMEM((3, ALL // 2, classes), F32),
            pltpu.VMEM((ALL // 2, classes), F32),
            pltpu.VMEM((ALL // 2, classes), F32),
            dma((2 * BLOCKS + 2,)),
            dma((80,)),
            dma((80,)),
        ],
        compiler_params=pltpu.CompilerParams(collective_id=0, has_side_effects=True, vmem_limit_bytes=VMEM_PANELS),
        name="panels",
    )(features_t, head, tile)


def update_kernel(a_ref, g_ref, size_ref, ur_ref, u_ref, r_ref, labels_ref, fit_ref, w_ref, out_ref, head_ref,
                  inv_ref, gain_ref, rv, sems):
    at = pl.program_id(0)

    def load(i):
        return pltpu.make_async_copy(r_ref.at[:, pl.ds(pl.multiple_of(i * BLOCK, 128), BLOCK)], rv.at[i], sems.at[i])

    @pl.when(at == 0)
    def _():
        for i in range(2 * BLOCKS):
            load(i).start()
        inv_ref[...] = g_ref[...]

        def more(state):
            step, size = state
            return (step < 60) & (size > 1e-5)

        def refine(state):
            step, _ = state
            g = inv_ref[...]
            error = eye_of(ALL) - jnp.dot(a_ref[...], g, precision=lax.Precision.HIGHEST, preferred_element_type=F32)
            inv_ref[...] = g + dot3(split(g), split(error))
            return step + 1, jnp.sum(error * error)

        lax.while_loop(more, refine, (jnp.int32(0), size_ref[0, 0]))
        stack_left(gain_ref, dot3(split(ur_ref[...].T), split(inv_ref[...])))
        width = w_ref.shape[1]
        classes = lax.axis_index("col") * width + lax.broadcasted_iota(jnp.int32, (width, ALL), 0)
        targets = jnp.where(labels_ref[...] == classes, 1.0, 0.0).astype(F32).T
        head_ref[...] = w_ref[...] + mm(gain_ref[...], stack_right(targets - fit_ref[...]))

    load(at).wait()
    out_ref[...] = rv[at] - mm(gain_ref[...], stack_right(u_ref[0]))


def update(system, inverse, size, rows_t, cols_t, tile, labels, fitted, head):
    rows = tile.shape[0]
    vmem = pl.BlockSpec(memory_space=pltpu.VMEM)
    return pl.pallas_call(
        update_kernel,
        grid=(2 * BLOCKS,),
        out_shape=(jax.ShapeDtypeStruct(tile.shape, F32), jax.ShapeDtypeStruct(head.shape, F32)),
        in_specs=[vmem] * 4 + [
            pl.BlockSpec((1, ALL, BLOCK), lambda i: (i // BLOCKS, 0, lax.rem(i, BLOCKS))),
            pl.BlockSpec(memory_space=pl.ANY),
        ] + [vmem] * 3,
        out_specs=(pl.BlockSpec((rows, BLOCK), lambda i: (0, i)), pl.BlockSpec(head.shape, lambda i: (0, 0))),
        scratch_shapes=[
            pltpu.VMEM((ALL, ALL), F32),
            pltpu.VMEM((rows, 3 * ALL), BF16),
            pltpu.VMEM((2 * BLOCKS, rows, BLOCK), F32),
            pltpu.SemaphoreType.DMA((2 * BLOCKS,)),
        ],
        compiler_params=pltpu.CompilerParams(vmem_limit_bytes=VMEM_UPDATE),
        name="update",
    )(system, inverse, size, rows_t, cols_t, tile, labels.reshape(1, ALL), fitted, head)


def on_device(features_t, labels, inv_corr, heads):
    cols_t, rows_t, system, inverse, size, fitted = panels(features_t, heads, inv_corr)
    block = cols_t.shape[3]
    return update(system, inverse, size, rows_t.reshape(ALL, block), cols_t.reshape(2, ALL, block), inv_corr, labels,
                  fitted, heads)


def solution(mesh):
    placed = (P(("row", "col"), None), P(), P("row", "col"), P("row", "col"))
    return jax.shard_map(
        on_device,
        mesh=mesh,
        in_specs=placed,
        out_specs=(P("row", "col"), P("row", "col")),
        check_vma=False,
    )
```

```python
import jax
import jax.numpy as jnp
from jax import lax
from jax.experimental import pallas as pl
from jax.experimental.pallas import tpu as pltpu
from jax.sharding import PartitionSpec as P

F32 = jnp.float32
BF16 = jnp.bfloat16
MESH = pl.DeviceIdType.MESH
ALL = 512
CHUNK = 64
MIB = 1 << 20
VMEM_PANELS = 48 * MIB
VMEM_UPDATE = 48 * MIB


def split(value):
    hi = value.astype(BF16)
    lo = (value - hi.astype(F32)).astype(BF16)
    return hi, lo


def mm(left, right):
    return jnp.dot(left, right, preferred_element_type=F32)


def dot3(left, right):
    (lh, ll), (rh, rl) = left, right
    return mm(lh, rh) + (mm(lh, rl) + mm(ll, rh))


class Place:
    def __init__(self):
        self.row, self.col = row, col = lax.axis_index("row"), lax.axis_index("col")
        self.core = core = lax.rem(row, 2)
        self.chip_row = chip_row = row // 2
        self.y_hi, self.x = y_hi, x = chip_row // 4, lax.rem(chip_row, 4)
        self.y_lo, self.z = y_lo, z = col // 4, lax.rem(col, 4)
        self.sibling = (chip_row * 2 + (1 - core), col)
        self.x_up = ((y_hi * 4 + lax.rem(x + 1, 4)) * 2 + core, col)
        self.x_down = ((y_hi * 4 + lax.rem(x + 3, 4)) * 2 + core, col)
        self.x_far = ((y_hi * 4 + lax.rem(x + 2, 4)) * 2 + core, col)
        self.y_far = (((1 - y_hi) * 4 + x) * 2 + core, col)
        self.z_up = (row, y_lo * 4 + lax.rem(z + 1, 4))
        self.z_down = (row, y_lo * 4 + lax.rem(z + 3, 4))
        self.y_near = (row, (1 - y_lo) * 4 + z)
        self.y_next = (((1 - y_hi) * 4 + x) * 2 + core, (1 - y_lo) * 4 + z)
        self.swapped = ((y_hi * 4 + z) * 2 + core, y_lo * 4 + x)
        self.inner = y_hi != y_lo
        self.off_diagonal = x != z
        between = lax.rem(y_hi + y_lo, 2)
        back_y, side_y = lax.rem(y_hi + 1 - between, 2), lax.rem(y_lo + between, 2)
        self.spread_to = ((back_y * 4 + x) * 2 + core, side_y * 4 + z)
        self.spread_slot = lax.rem(y_hi + between, 2) * 4 + x
        self.sum_to = [((y_lo * 4 + x) * 2 + core, part * 4 + z) for part in range(2)]


class Copies:
    def __init__(self, send_sems, recv_sems):
        self.send_sems, self.recv_sems = send_sems, recv_sems
        self.count = 0
        self.started = []

    def take(self):
        self.count += 1
        return self.count - 1

    def make(self, index, src, dst, device, recv=None):
        recv = index if recv is None else recv
        return pltpu.make_async_remote_copy(
            src_ref=src, dst_ref=dst, send_sem=self.send_sems.at[index], recv_sem=self.recv_sems.at[recv],
            device_id=device, device_id_type=MESH)

    def start(self, src, dst, device):
        index = self.take()
        copy = self.make(index, src, dst, device)
        copy.start()
        self.started.append(copy)
        return index

    def arrived(self, index, landing, device):
        self.make(index, landing, landing, device).wait_recv()

    def finish(self):
        for copy in self.started:
            copy.wait_send()


def greet(devices, maybe):
    barrier = pltpu.get_barrier_semaphore()
    total = jnp.int32(len(devices))
    for device in devices:
        pl.semaphore_signal(barrier, inc=1, device_id=device, device_id_type=MESH)
    for there, device in maybe:
        total = total + jnp.where(there, 1, 0)

        @pl.when(there)
        def _():
            pl.semaphore_signal(barrier, inc=1, device_id=device, device_id_type=MESH)

    pl.semaphore_wait(barrier, total)


class Gather:
    def __init__(self, copies, buf, pair_at, ring_at, pair, up, down, rows):
        self.c, self.buf, self.rows = copies, buf, rows
        self.a, self.b = pair_at, ring_at
        self.pair, self.up, self.down = pair, up, down

    def slot(self, pair_step, ring_step):
        a = self.a if pair_step == 0 else 1 - self.a
        return a * 4 + lax.rem(self.b + ring_step, 4)

    def part(self, pair_step, ring_step, half=None):
        at = self.slot(pair_step, ring_step)
        if half is None:
            return self.buf.at[at]
        n = self.rows // 2
        return self.buf.at[at, pl.ds(half * n, n)]

    def same(self, part, device):
        return self.c.start(part, part, device)

    def own(self):
        self.own_ring()
        self.i_pair = self.same(self.part(0, 0), self.pair)

    def own_ring(self):
        mine = self.part(0, 0)
        self.i_up = self.same(mine, self.up)
        self.i_down = self.same(mine, self.down)

    def forward_own(self):
        self.c.arrived(self.i_up, self.part(0, 3), self.down)
        self.h_up = self.same(self.part(0, 3, 0), self.up)
        self.c.arrived(self.i_down, self.part(0, 1), self.up)
        self.h_down = self.same(self.part(0, 1, 1), self.down)

    def pair_across(self):
        self.c.arrived(self.i_pair, self.part(1, 0), self.pair)
        self.q_up = self.same(self.part(1, 0), self.up)
        self.q_down = self.same(self.part(1, 0), self.down)

    def far_own(self):
        self.c.arrived(self.h_up, self.part(0, 2, 0), self.down)
        self.c.arrived(self.h_down, self.part(0, 2, 1), self.up)

    def far_by_pair(self):
        self.f_pair = self.same(self.part(0, 2), self.pair)

    def end_by_pair(self):
        self.c.arrived(self.q_up, self.part(1, 3), self.down)
        self.c.arrived(self.q_down, self.part(1, 1), self.up)
        self.c.arrived(self.f_pair, self.part(1, 2), self.pair)

    def forward_pair(self):
        self.c.arrived(self.q_up, self.part(1, 3), self.down)
        self.g_up = self.same(self.part(1, 3, 0), self.up)
        self.c.arrived(self.q_down, self.part(1, 1), self.up)
        self.g_down = self.same(self.part(1, 1, 1), self.down)

    def end_by_ring(self):
        self.c.arrived(self.g_up, self.part(1, 2, 0), self.down)
        self.c.arrived(self.g_down, self.part(1, 2, 1), self.up)


def stack_left(ref, value):
    hi, lo = split(value)
    depth = value.shape[1]
    ref[:, 0:depth] = hi
    ref[:, depth:2 * depth] = hi
    ref[:, 2 * depth:] = lo


def stack_right(value):
    hi, lo = split(value)
    return jnp.concatenate([hi, lo, hi], 0)


def eye_of(order):
    rows = lax.broadcasted_iota(jnp.int32, (order, order), 0)
    cols = lax.broadcasted_iota(jnp.int32, (order, order), 1)
    return jnp.where(rows == cols, 1.0, 0.0).astype(F32)


BLOCKS = 3
BLOCK = 384
PART = 256


def panels_kernel(x_ref, w_ref, r_ref, uc_ref, ur_ref, a_ref, g_ref, size_ref, fit_ref,
                  wv, rv, xr, xs, part, from_sib, acc, ra, rb, ry, relay, s_all, sp, rs0, sh, rs1, sh2, rs2,
                  fx, rf0, fh, rf1, fh2, rf2, local_sems, send_sems, recv_sems):
    at = Place()
    k, p, col = at.core, at.chip_row, at.col
    rows = x_ref.shape[0]
    turns = [(1 - k, j) for j in range(BLOCKS)] + [(k, j) for j in range(BLOCKS)]

    def columns(h, j):
        return pl.ds(pl.multiple_of((h * BLOCKS + j) * BLOCK, 128), BLOCK)

    own_x = [pltpu.make_async_copy(x_ref.at[:, pl.ds(e * PART, PART)], xr.at[e, col], local_sems.at[2 * BLOCKS + e])
             for e in range(2)]
    for copy in own_x:
        copy.start()
    own_w = pltpu.make_async_copy(w_ref, wv, local_sems.at[2 * BLOCKS + 2])
    own_w.start()
    loads = []
    for i, (h, j) in enumerate(turns):
        loads.append(pltpu.make_async_copy(r_ref.at[:, columns(h, j)], rv.at[i], local_sems.at[i]))
        loads[-1].start()
    greet([at.sibling, at.x_up, at.x_down, at.x_far, at.y_far, at.z_up, at.z_down, at.y_near],
          [(at.inner, at.y_next), (at.off_diagonal, at.swapped)])
    for copy in own_x:
        copy.wait()
    copies = Copies(send_sems, recv_sems)

    ga, gb = (Gather(copies, xr.at[e], at.y_lo, at.z, at.y_near, at.z_up, at.z_down, rows) for e in range(2))
    ga.own()
    ga.forward_own()
    ga.pair_across()
    ga.far_own()
    ga.far_by_pair()
    gb.own()
    ga.end_by_pair()

    def stack_features(e):
        stack_left(xs.at[pl.ds(e * PART, PART)], xr[e].reshape(8 * rows, PART).T)

    def product(e, i):
        h, j = turns[i]
        if e == 0:
            loads[i].wait()
        value = mm(xs[e * PART:(e + 1) * PART], stack_right(rv[i]))
        part[h, 4 * e:4 * e + 4, :, j * BLOCK:(j + 1) * BLOCK] = value.reshape(4, CHUNK, BLOCK)

    sib = {}

    def part_to_sibling(e, j):
        piece = (pl.ds(4 * e, 4), slice(None), slice(j * BLOCK, (j + 1) * BLOCK))
        sib[e, j] = copies.start(part.at[(1 - k,) + piece], from_sib.at[piece], at.sibling)

    half = CHUNK // 2
    low, high = pl.ds(0, half), pl.ds(half, half)
    a_up, a_down, b_up, b_down = {}, {}, {}, {}

    def chunk(e, x_step):
        return e * 4 + lax.rem(at.x + x_step, 4)

    def scatter_far(e):
        for j in range(BLOCKS):
            copies.arrived(sib[e, j], from_sib.at[pl.ds(4 * e, 4), :, j * BLOCK:(j + 1) * BLOCK], at.sibling)
        for x_step in (2, 1, 3, 0):
            ch = chunk(e, x_step)
            acc[ch] = part[k, ch] + from_sib[ch]
            if x_step == 2:
                a_up[e] = copies.start(acc.at[ch, low], ra.at[0, e], at.x_up)
                a_down[e] = copies.start(acc.at[ch, high], ra.at[1, e], at.x_down)

    def scatter_near(e):
        ch = chunk(e, 1)
        copies.arrived(a_up[e], ra.at[0, e], at.x_down)
        acc[ch, low] = acc[ch, low] + ra[0, e]
        b_up[e] = copies.start(acc.at[ch], rb.at[0, e], at.x_up)
        ch = chunk(e, 3)
        copies.arrived(a_down[e], ra.at[1, e], at.x_up)
        acc[ch, high] = acc[ch, high] + ra[1, e]
        b_down[e] = copies.start(acc.at[ch], rb.at[1, e], at.x_down)

    y_sems = [copies.take() for _ in range(2)]

    def sum_copy(e):
        return copies.make(y_sems[e], acc.at[chunk(e, 0)], ry.at[at.y_hi], at.sum_to[e], y_sems[0] + at.y_hi)

    def stays(e):
        return (at.y_hi == e) & (at.y_lo == e)

    def scatter_end(e):
        ch = chunk(e, 0)
        copies.arrived(b_up[e], rb.at[0, e], at.x_down)
        copies.arrived(b_down[e], rb.at[1, e], at.x_up)
        acc[ch] = acc[ch] + (rb[0, e] + rb[1, e])

        @pl.when(jnp.logical_not(stays(e)))
        def _():
            sum_copy(e).start()

    stack_features(0)
    product(0, 0)
    part_to_sibling(0, 0)
    product(0, 1)
    part_to_sibling(0, 1)
    gb.forward_own()
    product(0, 2)
    part_to_sibling(0, 2)
    product(0, 3)
    gb.pair_across()
    product(0, 4)
    product(0, 5)
    scatter_far(0)
    gb.far_own()
    gb.far_by_pair()
    gb.end_by_pair()
    stack_features(1)
    product(1, 0)
    part_to_sibling(1, 0)
    scatter_near(0)

    own_w.wait()
    fx[...] = mm(xs[...], stack_right(wv[...]))
    n = ALL // 2
    quarter = n // 4
    f0 = copies.start(fx.at[pl.ds(pl.multiple_of((1 - k) * n, n), n)], rf0, at.sibling)
    product(1, 1)
    part_to_sibling(1, 1)
    product(1, 2)
    part_to_sibling(1, 2)
    copies.arrived(f0, rf0, at.sibling)
    fh[...] = fx[pl.ds(pl.multiple_of(k * n, n), n)] + rf0[...]

    def quarter_at(x_step, base=0):
        return pl.ds(pl.multiple_of(base + lax.rem(at.x + x_step, 4) * quarter, quarter), quarter)

    steps = ((1, at.x_up), (3, at.x_down), (2, at.x_far))
    f1 = [copies.start(fh.at[quarter_at(t)], rf1.at[i], d) for i, (t, d) in enumerate(steps)]
    product(1, 3)
    product(1, 4)
    product(1, 5)
    scatter_far(1)
    scatter_end(0)
    for i, d in enumerate((at.x_down, at.x_up, at.x_far)):
        copies.arrived(f1[i], rf1.at[i], d)
    fh2[...] = (fh[quarter_at(0)] + rf1[2]) + (rf1[0] + rf1[1])
    f2 = copies.start(fh2, rf2, at.y_far)
    scatter_near(1)
    copies.arrived(f2, rf2, at.y_far)
    fit_own = fit_ref.at[quarter_at(0, k * n)]
    fit_own[...] = fh2[...] + rf2[...]
    f3 = [copies.start(fit_own, fit_own, d) for _, d in steps]
    scatter_end(1)

    own = at.y_hi * 4 + at.x

    @pl.when(at.inner)
    def _():
        for i in range(2):
            copies.make(y_sems[0], ry.at[i], ry.at[i], at.y_next, y_sems[i]).wait_recv()
        relay[...] = ry[0] + ry[1]

    @pl.when(jnp.logical_not(at.inner))
    def _():
        there = 1 - at.y_hi
        copies.make(y_sems[0], ry.at[there], ry.at[there], at.y_far, y_sems[0] + there).wait_recv()
        relay[...] = acc[own] + ry[there]
        uc_ref[k, p] = relay[...]

    for e in range(2):
        @pl.when(jnp.logical_not(stays(e)))
        def _():
            sum_copy(e).wait_send()

    t1 = copies.take()
    step_xz = copies.make(t1, relay, ur_ref.at[at.y_lo * 4 + at.x], at.swapped)

    @pl.when(at.off_diagonal)
    def _():
        step_xz.start()

    d1 = copies.start(relay, uc_ref.at[k, at.spread_slot], at.spread_to)
    d2 = copies.take()
    inner_back = copies.make(d2, relay, uc_ref.at[k, at.spread_slot], at.y_next)

    @pl.when(at.inner)
    def _():
        inner_back.start()

    own_block = uc_ref.at[k]
    gc = Gather(copies, own_block, at.y_hi, at.x, at.y_far, at.x_up, at.x_down, CHUNK)
    gr = Gather(copies, ur_ref, at.y_lo, at.z, at.y_near, at.z_up, at.z_down, CHUNK)
    gc.i_pair = d1

    def to_sibling(pair_step, ring_step):
        piece = gc.part(pair_step, ring_step)
        return copies.start(piece, piece, at.sibling)

    for f, t, d in zip(f3, (3, 1, 2), (at.x_down, at.x_up, at.x_far)):
        copies.arrived(f, fit_ref.at[quarter_at(t, k * n)], d)
    fit_half = fit_ref.at[pl.ds(pl.multiple_of(k * n, n), n)]
    f4 = copies.start(fit_half, fit_half, at.sibling)

    @pl.when(at.inner)
    def _():
        copies.make(d2, uc_ref.at[k, p], uc_ref.at[k, p], at.y_next).wait_recv()
        inner_back.wait_send()

    gc.own_ring()
    u = {(0, 0): to_sibling(0, 0)}

    @pl.when(at.off_diagonal)
    def _():
        copies.make(t1, ur_ref.at[col], ur_ref.at[col], at.swapped).wait_recv()
        step_xz.wait_send()

    @pl.when(jnp.logical_not(at.off_diagonal))
    def _():
        ur_ref[col] = relay[...]

    gr.own()

    left = split(ur_ref[col])
    for e in range(2):
        sp[:, e * PART:(e + 1) * PART] = dot3(left, split(xr[e].reshape(8 * rows, PART)))
    s0 = copies.start(sp.at[pl.ds(pl.multiple_of((1 - k) * half, half), half)], rs0, at.sibling)
    copies.arrived(s0, rs0, at.sibling)
    sh[...] = sp[pl.ds(pl.multiple_of(k * half, half), half)] + rs0[...]
    s1 = [copies.start(sh, rs1.at[i], d) for i, d in enumerate((at.x_up, at.x_down, at.x_far))]
    for i, d in enumerate((at.x_down, at.x_up, at.x_far)):
        copies.arrived(s1[i], rs1.at[i], d)
    sh2[...] = (sh[...] + rs1[2]) + (rs1[0] + rs1[1])
    s2 = copies.start(sh2, rs2, at.y_far)
    gc.forward_own()
    gc.pair_across()
    for step in ((0, 3), (0, 1), (1, 0)):
        u[step] = to_sibling(*step)
    copies.arrived(s2, rs2, at.y_far)
    s_all[k, col] = sh2[...] + rs2[...]
    gs = Gather(copies, s_all.at[k], at.y_lo, at.z, at.y_near, at.z_up, at.z_down, half)
    gs.own()
    gs.forward_own()
    gs.pair_across()
    gs.far_own()
    gs.forward_pair()
    gs.end_by_ring()
    s4 = copies.start(s_all.at[k], s_all.at[k], at.sibling)
    gr.forward_own()
    gr.pair_across()
    gc.far_own()
    u[(0, 2)] = to_sibling(0, 2)
    gc.forward_pair()
    for step in ((1, 3), (1, 1)):
        u[step] = to_sibling(*step)
    copies.arrived(s4, s_all.at[1 - k], at.sibling)

    for c in range(8):
        for h in range(2):
            a_ref[pl.ds(c * CHUNK + h * half, half)] = s_all[h, c]
    eye = eye_of(ALL)
    a_ref[...] = a_ref[...] + eye
    bound = jnp.max(jnp.sum(jnp.abs(a_ref[...]), axis=0, keepdims=True))
    scale = 2.0 / (1.0 + bound)
    g_ref[...] = scale * (2.0 * eye - scale * a_ref[...])

    def refine(_):
        g = split(g_ref[...])
        error = eye_of(ALL) - dot3(split(a_ref[...]), g)
        g_ref[...] = g_ref[...] + dot3(g, split(error))
        size_ref[...] = jnp.broadcast_to(jnp.sum(error * error), size_ref.shape)

    pl.loop(0, 2)(refine)
    gr.far_own()
    gr.far_by_pair()
    pl.loop(0, 2)(refine)
    gc.end_by_ring()
    u[(1, 2)] = to_sibling(1, 2)
    gr.end_by_pair()
    other_block = uc_ref.at[1 - k]
    for (pair_step, ring_step), index in u.items():
        copies.arrived(index, other_block.at[gc.slot(pair_step, ring_step)], at.sibling)
    copies.arrived(f4, fit_ref.at[pl.ds(pl.multiple_of((1 - k) * n, n), n)], at.sibling)
    copies.finish()


def panels(features_t, head, tile):
    rows, examples = features_t.shape
    depth, width = tile.shape[0], tile.shape[1] // 2
    classes = head.shape[1]
    half = CHUNK // 2
    vmem = pl.BlockSpec(memory_space=pltpu.VMEM)
    dma = pltpu.SemaphoreType.DMA
    return pl.pallas_call(
        panels_kernel,
        out_shape=(
            jax.ShapeDtypeStruct((2, 8, CHUNK, width), F32),
            jax.ShapeDtypeStruct((8, CHUNK, width), F32),
            jax.ShapeDtypeStruct((ALL, ALL), F32),
            jax.ShapeDtypeStruct((ALL, ALL), F32),
            jax.ShapeDtypeStruct((8, 128), F32),
            jax.ShapeDtypeStruct((ALL, classes), F32),
        ),
        in_specs=[pl.BlockSpec(memory_space=pltpu.HBM)] * 3,
        out_specs=(vmem,) * 6,
        scratch_shapes=[
            pltpu.VMEM(head.shape, F32),
            pltpu.VMEM((2 * BLOCKS, depth, BLOCK), F32),
            pltpu.VMEM((2, 8, rows, PART), F32),
            pltpu.VMEM((examples, 3 * depth), BF16),
            pltpu.VMEM((2, 8, CHUNK, width), F32),
            pltpu.VMEM((8, CHUNK, width), F32),
            pltpu.VMEM((8, CHUNK, width), F32),
            pltpu.VMEM((2, 2, half, width), F32),
            pltpu.VMEM((2, 2, CHUNK, width), F32),
            pltpu.VMEM((2, CHUNK, width), F32),
            pltpu.VMEM((CHUNK, width), F32),
            pltpu.VMEM((2, 8, half, ALL), F32),
            pltpu.VMEM((CHUNK, ALL), F32),
            pltpu.VMEM((half, ALL), F32),
            pltpu.VMEM((half, ALL), F32),
            pltpu.VMEM((3, half, ALL), F32),
            pltpu.VMEM((half, ALL), F32),
            pltpu.VMEM((half, ALL), F32),
            pltpu.VMEM((ALL, classes), F32),
            pltpu.VMEM((ALL // 2, classes), F32),
            pltpu.VMEM((ALL // 2, classes), F32),
            pltpu.VMEM((3, ALL // 8, classes), F32),
            pltpu.VMEM((ALL // 8, classes), F32),
            pltpu.VMEM((ALL // 8, classes), F32),
            dma((2 * BLOCKS + 3,)),
            dma((96,)),
            dma((96,)),
        ],
        compiler_params=pltpu.CompilerParams(collective_id=0, has_side_effects=True, vmem_limit_bytes=VMEM_PANELS),
        name="panels",
    )(features_t, head, tile)


def update_kernel(a_ref, g_ref, size_ref, ur_ref, u_ref, r_ref, labels_ref, fit_ref, w_ref, out_ref, head_ref,
                  inv_ref, gain_ref, rv, sems):
    at = pl.program_id(0)

    def load(i):
        return pltpu.make_async_copy(r_ref.at[:, pl.ds(pl.multiple_of(i * BLOCK, 128), BLOCK)], rv.at[i], sems.at[i])

    @pl.when(at == 0)
    def _():
        for i in range(2 * BLOCKS):
            load(i).start()
        inv_ref[...] = g_ref[...]

        def more(state):
            step, size = state
            return (step < 60) & (size > 1e-5)

        def refine(state):
            step, _ = state
            g = inv_ref[...]
            error = eye_of(ALL) - jnp.dot(a_ref[...], g, precision=lax.Precision.HIGHEST, preferred_element_type=F32)
            inv_ref[...] = g + dot3(split(g), split(error))
            return step + 1, jnp.sum(error * error)

        lax.while_loop(more, refine, (jnp.int32(0), size_ref[0, 0]))
        stack_left(gain_ref, dot3(split(ur_ref[...].T), split(inv_ref[...])))
        width = w_ref.shape[1]
        classes = lax.axis_index("col") * width + lax.broadcasted_iota(jnp.int32, (width, ALL), 0)
        targets = jnp.where(labels_ref[...] == classes, 1.0, 0.0).astype(F32).T
        head_ref[...] = w_ref[...] + mm(gain_ref[...], stack_right(targets - fit_ref[...]))

    load(at).wait()
    out_ref[...] = rv[at] - mm(gain_ref[...], stack_right(u_ref[0]))


def update(system, inverse, size, rows_t, cols_t, tile, labels, fitted, head):
    rows = tile.shape[0]
    vmem = pl.BlockSpec(memory_space=pltpu.VMEM)
    return pl.pallas_call(
        update_kernel,
        grid=(2 * BLOCKS,),
        out_shape=(jax.ShapeDtypeStruct(tile.shape, F32), jax.ShapeDtypeStruct(head.shape, F32)),
        in_specs=[vmem] * 4 + [
            pl.BlockSpec((1, ALL, BLOCK), lambda i: (i // BLOCKS, 0, lax.rem(i, BLOCKS))),
            pl.BlockSpec(memory_space=pl.ANY),
        ] + [vmem] * 3,
        out_specs=(pl.BlockSpec((rows, BLOCK), lambda i: (0, i)), pl.BlockSpec(head.shape, lambda i: (0, 0))),
        scratch_shapes=[
            pltpu.VMEM((ALL, ALL), F32),
            pltpu.VMEM((rows, 3 * ALL), BF16),
            pltpu.VMEM((2 * BLOCKS, rows, BLOCK), F32),
            pltpu.SemaphoreType.DMA((2 * BLOCKS,)),
        ],
        compiler_params=pltpu.CompilerParams(vmem_limit_bytes=VMEM_UPDATE),
        name="update",
    )(system, inverse, size, rows_t, cols_t, tile, labels.reshape(1, ALL), fitted, head)


def on_device(features_t, labels, inv_corr, heads):
    cols_t, rows_t, system, inverse, size, fitted = panels(features_t, heads, inv_corr)
    block = cols_t.shape[3]
    return update(system, inverse, size, rows_t.reshape(ALL, block), cols_t.reshape(2, ALL, block), inv_corr, labels,
                  fitted, heads)


def solution(mesh):
    placed = (P(("row", "col"), None), P(), P("row", "col"), P("row", "col"))
    return jax.shard_map(
        on_device,
        mesh=mesh,
        in_specs=placed,
        out_specs=(P("row", "col"), P("row", "col")),
        check_vma=False,
    )
```

```python
import jax
import jax.numpy as jnp
from jax import lax
from jax.experimental import pallas as pl
from jax.experimental.pallas import tpu as pltpu
from jax.sharding import PartitionSpec as P

F32 = jnp.float32
BF16 = jnp.bfloat16
MESH = pl.DeviceIdType.MESH
ALL = 512
CHUNK = 64
MIB = 1 << 20
VMEM_PANELS = 44 * MIB
VMEM_UPDATE = 30 * MIB


def split(value):
    hi = value.astype(BF16)
    lo = (value - hi.astype(F32)).astype(BF16)
    return hi, lo


def mm(left, right):
    return jnp.dot(left, right, preferred_element_type=F32)


def dot3(left, right):
    (lh, ll), (rh, rl) = left, right
    return mm(lh, rh) + (mm(lh, rl) + mm(ll, rh))


class Place:
    def __init__(self):
        self.row, self.col = row, col = lax.axis_index("row"), lax.axis_index("col")
        self.core = core = lax.rem(row, 2)
        self.chip_row = chip_row = row // 2
        self.y_hi, self.x = y_hi, x = chip_row // 4, lax.rem(chip_row, 4)
        self.y_lo, self.z = y_lo, z = col // 4, lax.rem(col, 4)
        self.sibling = (chip_row * 2 + (1 - core), col)
        self.x_up = ((y_hi * 4 + lax.rem(x + 1, 4)) * 2 + core, col)
        self.x_down = ((y_hi * 4 + lax.rem(x + 3, 4)) * 2 + core, col)
        self.x_far = ((y_hi * 4 + lax.rem(x + 2, 4)) * 2 + core, col)
        self.y_far = (((1 - y_hi) * 4 + x) * 2 + core, col)
        self.z_up = (row, y_lo * 4 + lax.rem(z + 1, 4))
        self.z_down = (row, y_lo * 4 + lax.rem(z + 3, 4))
        self.y_near = (row, (1 - y_lo) * 4 + z)
        self.y_next = (((1 - y_hi) * 4 + x) * 2 + core, (1 - y_lo) * 4 + z)
        self.swapped = ((y_hi * 4 + z) * 2 + core, y_lo * 4 + x)
        self.inner = y_hi != y_lo
        self.off_diagonal = x != z
        between = lax.rem(y_hi + y_lo, 2)
        back_y, side_y = lax.rem(y_hi + 1 - between, 2), lax.rem(y_lo + between, 2)
        self.spread_to = ((back_y * 4 + x) * 2 + core, side_y * 4 + z)
        self.spread_slot = lax.rem(y_hi + between, 2) * 4 + x
        self.sum_to = [((y_lo * 4 + x) * 2 + core, part * 4 + z) for part in range(2)]


class Copies:
    def __init__(self, send_sems, recv_sems):
        self.send_sems, self.recv_sems = send_sems, recv_sems
        self.count = 0
        self.started = []

    def take(self):
        self.count += 1
        return self.count - 1

    def make(self, index, src, dst, device, recv=None):
        recv = index if recv is None else recv
        return pltpu.make_async_remote_copy(
            src_ref=src, dst_ref=dst, send_sem=self.send_sems.at[index], recv_sem=self.recv_sems.at[recv],
            device_id=device, device_id_type=MESH)

    def start(self, src, dst, device):
        index = self.take()
        copy = self.make(index, src, dst, device)
        copy.start()
        self.started.append(copy)
        return index

    def arrived(self, index, landing, device):
        self.make(index, landing, landing, device).wait_recv()

    def finish(self):
        for copy in self.started:
            copy.wait_send()


def greet(devices, maybe):
    barrier = pltpu.get_barrier_semaphore()
    total = jnp.int32(len(devices))
    for device in devices:
        pl.semaphore_signal(barrier, inc=1, device_id=device, device_id_type=MESH)
    for there, device in maybe:
        total = total + jnp.where(there, 1, 0)

        @pl.when(there)
        def _():
            pl.semaphore_signal(barrier, inc=1, device_id=device, device_id_type=MESH)

    pl.semaphore_wait(barrier, total)


class Gather:
    def __init__(self, copies, buf, pair_at, ring_at, pair, up, down, rows):
        self.c, self.buf, self.rows = copies, buf, rows
        self.a, self.b = pair_at, ring_at
        self.pair, self.up, self.down = pair, up, down

    def slot(self, pair_step, ring_step):
        a = self.a if pair_step == 0 else 1 - self.a
        return a * 4 + lax.rem(self.b + ring_step, 4)

    def part(self, pair_step, ring_step, half=None):
        at = self.slot(pair_step, ring_step)
        if half is None:
            return self.buf.at[at]
        n = self.rows // 2
        return self.buf.at[at, pl.ds(half * n, n)]

    def same(self, part, device):
        return self.c.start(part, part, device)

    def own(self):
        self.own_ring()
        self.own_pair()

    def own_pair(self):
        self.i_pair = self.same(self.part(0, 0), self.pair)

    def own_ring(self):
        mine = self.part(0, 0)
        self.i_up = self.same(mine, self.up)
        self.i_down = self.same(mine, self.down)

    def forward_own(self):
        self.c.arrived(self.i_up, self.part(0, 3), self.down)
        self.h_up = self.same(self.part(0, 3, 0), self.up)
        self.c.arrived(self.i_down, self.part(0, 1), self.up)
        self.h_down = self.same(self.part(0, 1, 1), self.down)

    def pair_across(self):
        self.c.arrived(self.i_pair, self.part(1, 0), self.pair)
        self.q_up = self.same(self.part(1, 0), self.up)
        self.q_down = self.same(self.part(1, 0), self.down)

    def far_own(self):
        self.c.arrived(self.h_up, self.part(0, 2, 0), self.down)
        self.c.arrived(self.h_down, self.part(0, 2, 1), self.up)

    def far_by_pair(self):
        self.f_pair = self.same(self.part(0, 2), self.pair)

    def end_by_pair(self):
        self.c.arrived(self.q_up, self.part(1, 3), self.down)
        self.c.arrived(self.q_down, self.part(1, 1), self.up)
        self.c.arrived(self.f_pair, self.part(1, 2), self.pair)

    def forward_pair(self):
        self.c.arrived(self.q_up, self.part(1, 3), self.down)
        self.g_up = self.same(self.part(1, 3, 0), self.up)
        self.c.arrived(self.q_down, self.part(1, 1), self.up)
        self.g_down = self.same(self.part(1, 1, 1), self.down)

    def end_by_ring(self):
        self.c.arrived(self.g_up, self.part(1, 2, 0), self.down)
        self.c.arrived(self.g_down, self.part(1, 2, 1), self.up)


def stack_left(ref, value):
    hi, lo = split(value)
    depth = value.shape[1]
    ref[:, 0:depth] = hi
    ref[:, depth:2 * depth] = hi
    ref[:, 2 * depth:] = lo


def stack_right(value):
    hi, lo = split(value)
    return jnp.concatenate([hi, lo, hi], 0)


def eye_of(order):
    rows = lax.broadcasted_iota(jnp.int32, (order, order), 0)
    cols = lax.broadcasted_iota(jnp.int32, (order, order), 1)
    return jnp.where(rows == cols, 1.0, 0.0).astype(F32)


BLOCKS = 3
BLOCK = 384
PART = 256


def panels_kernel(x_ref, w_ref, r_ref, uc_ref, ur_ref, a_ref, g_ref, size_ref, fit_ref,
                  wv, rv, xr, xs, part, from_sib, acc, ra, rb, ry, relay, xh, xl, s_all, sp, rs0, sh, rs1, sh2, rs2,
                  fx, rf0, fh, rf1, fh2, rf2, local_sems, send_sems, recv_sems):
    at = Place()
    k, p, col = at.core, at.chip_row, at.col
    rows = x_ref.shape[0]
    turns = [(1 - k, j) for j in range(BLOCKS)] + [(k, j) for j in range(BLOCKS)]

    def columns(h, j):
        return pl.ds(pl.multiple_of((h * BLOCKS + j) * BLOCK, 128), BLOCK)

    own_x = [pltpu.make_async_copy(x_ref.at[:, pl.ds(e * PART, PART)], xr.at[e, col], local_sems.at[2 * BLOCKS + e])
             for e in range(2)]
    for copy in own_x:
        copy.start()
    own_w = pltpu.make_async_copy(w_ref, wv, local_sems.at[2 * BLOCKS + 2])
    own_w.start()
    loads = []
    for i, (h, j) in enumerate(turns):
        loads.append(pltpu.make_async_copy(r_ref.at[:, columns(h, j)], rv.at[i], local_sems.at[i]))
        loads[-1].start()
    greet([at.sibling, at.x_up, at.x_down, at.x_far, at.y_far, at.z_up, at.z_down, at.y_near],
          [(at.inner, at.y_next), (at.off_diagonal, at.swapped)])
    for copy in own_x:
        copy.wait()
    copies = Copies(send_sems, recv_sems)

    ga, gb = (Gather(copies, xr.at[e], at.y_lo, at.z, at.y_near, at.z_up, at.z_down, rows) for e in range(2))
    ga.own()
    ga.forward_own()
    ga.pair_across()
    ga.far_own()
    ga.far_by_pair()
    gb.own()
    ga.end_by_pair()

    def stack_features(e):
        stack_left(xs.at[pl.ds(e * PART, PART)], xr[e].reshape(8 * rows, PART).T)

    def product(e, i):
        h, j = turns[i]
        if e == 0:
            loads[i].wait()
        value = mm(xs[e * PART:(e + 1) * PART], stack_right(rv[i]))
        part[h, 4 * e:4 * e + 4, :, j * BLOCK:(j + 1) * BLOCK] = value.reshape(4, CHUNK, BLOCK)

    sib = {}

    def part_to_sibling(e, j):
        piece = (pl.ds(4 * e, 4), slice(None), slice(j * BLOCK, (j + 1) * BLOCK))
        sib[e, j] = copies.start(part.at[(1 - k,) + piece], from_sib.at[piece], at.sibling)

    half = CHUNK // 2
    low, high = pl.ds(0, half), pl.ds(half, half)
    a_up, a_down, b_up, b_down = {}, {}, {}, {}

    def chunk(e, x_step):
        return e * 4 + lax.rem(at.x + x_step, 4)

    def scatter_far(e):
        for j in range(BLOCKS):
            copies.arrived(sib[e, j], from_sib.at[pl.ds(4 * e, 4), :, j * BLOCK:(j + 1) * BLOCK], at.sibling)
        for x_step in (2, 1, 3, 0):
            ch = chunk(e, x_step)
            acc[ch] = part[k, ch] + from_sib[ch]
            if x_step == 2:
                a_up[e] = copies.start(acc.at[ch, low], ra.at[0, e], at.x_up)
                a_down[e] = copies.start(acc.at[ch, high], ra.at[1, e], at.x_down)

    def scatter_near(e):
        ch = chunk(e, 1)
        copies.arrived(a_up[e], ra.at[0, e], at.x_down)
        acc[ch, low] = acc[ch, low] + ra[0, e]
        b_up[e] = copies.start(acc.at[ch], rb.at[0, e], at.x_up)
        ch = chunk(e, 3)
        copies.arrived(a_down[e], ra.at[1, e], at.x_up)
        acc[ch, high] = acc[ch, high] + ra[1, e]
        b_down[e] = copies.start(acc.at[ch], rb.at[1, e], at.x_down)

    y_sems = [copies.take() for _ in range(2)]

    def sum_copy(e):
        return copies.make(y_sems[e], acc.at[chunk(e, 0)], ry.at[at.y_hi], at.sum_to[e], y_sems[0] + at.y_hi)

    def stays(e):
        return (at.y_hi == e) & (at.y_lo == e)

    def scatter_end(e):
        ch = chunk(e, 0)
        copies.arrived(b_up[e], rb.at[0, e], at.x_down)
        copies.arrived(b_down[e], rb.at[1, e], at.x_up)
        acc[ch] = acc[ch] + (rb[0, e] + rb[1, e])

        @pl.when(jnp.logical_not(stays(e)))
        def _():
            sum_copy(e).start()

    stack_features(0)
    product(0, 0)
    part_to_sibling(0, 0)
    product(0, 1)
    part_to_sibling(0, 1)
    gb.forward_own()
    product(0, 2)
    part_to_sibling(0, 2)
    product(0, 3)
    gb.pair_across()
    product(0, 4)
    product(0, 5)
    scatter_far(0)
    gb.far_own()
    gb.far_by_pair()
    gb.end_by_pair()
    stack_features(1)
    product(1, 0)
    part_to_sibling(1, 0)
    scatter_near(0)

    own_w.wait()
    fx[...] = mm(xs[...], stack_right(wv[...]))
    n = ALL // 2
    quarter = n // 4
    f0 = copies.start(fx.at[pl.ds(pl.multiple_of((1 - k) * n, n), n)], rf0, at.sibling)
    product(1, 1)
    part_to_sibling(1, 1)
    product(1, 2)
    part_to_sibling(1, 2)
    copies.arrived(f0, rf0, at.sibling)
    fh[...] = fx[pl.ds(pl.multiple_of(k * n, n), n)] + rf0[...]

    def quarter_at(x_step, base=0):
        return pl.ds(pl.multiple_of(base + lax.rem(at.x + x_step, 4) * quarter, quarter), quarter)

    steps = ((1, at.x_up), (3, at.x_down), (2, at.x_far))
    f1 = [copies.start(fh.at[quarter_at(t)], rf1.at[i], d) for i, (t, d) in enumerate(steps)]
    product(1, 3)
    product(1, 4)
    product(1, 5)
    scatter_far(1)
    scatter_end(0)
    for i, d in enumerate((at.x_down, at.x_up, at.x_far)):
        copies.arrived(f1[i], rf1.at[i], d)
    fh2[...] = (fh[quarter_at(0)] + rf1[2]) + (rf1[0] + rf1[1])
    f2 = copies.start(fh2, rf2, at.y_far)
    scatter_near(1)
    copies.arrived(f2, rf2, at.y_far)
    fit_own = fit_ref.at[quarter_at(0, k * n)]
    fit_own[...] = fh2[...] + rf2[...]
    f3 = [copies.start(fit_own, fit_own, d) for _, d in steps]
    scatter_end(1)

    own = at.y_hi * 4 + at.x

    @pl.when(at.inner)
    def _():
        for i in range(2):
            copies.make(y_sems[0], ry.at[i], ry.at[i], at.y_next, y_sems[i]).wait_recv()
        relay[...] = ry[0] + ry[1]

    @pl.when(jnp.logical_not(at.inner))
    def _():
        there = 1 - at.y_hi
        copies.make(y_sems[0], ry.at[there], ry.at[there], at.y_far, y_sems[0] + there).wait_recv()
        relay[...] = acc[own] + ry[there]
        uc_ref[k, p] = relay[...]

    for e in range(2):
        @pl.when(jnp.logical_not(stays(e)))
        def _():
            sum_copy(e).wait_send()

    t1 = copies.take()
    step_xz = copies.make(t1, relay, ur_ref.at[at.y_lo * 4 + at.x], at.swapped)

    @pl.when(at.off_diagonal)
    def _():
        step_xz.start()

    d1 = copies.start(relay, uc_ref.at[k, at.spread_slot], at.spread_to)
    d2 = copies.take()
    inner_back = copies.make(d2, relay, uc_ref.at[k, at.spread_slot], at.y_next)

    @pl.when(at.inner)
    def _():
        inner_back.start()

    own_block = uc_ref.at[k]
    gc = Gather(copies, own_block, at.y_hi, at.x, at.y_far, at.x_up, at.x_down, CHUNK)
    gr = Gather(copies, ur_ref, at.y_lo, at.z, at.y_near, at.z_up, at.z_down, CHUNK)
    gc.i_pair = d1

    def to_sibling(pair_step, ring_step):
        piece = gc.part(pair_step, ring_step)
        return copies.start(piece, piece, at.sibling)

    for f, t, d in zip(f3, (3, 1, 2), (at.x_down, at.x_up, at.x_far)):
        copies.arrived(f, fit_ref.at[quarter_at(t, k * n)], d)
    fit_half = fit_ref.at[pl.ds(pl.multiple_of(k * n, n), n)]
    f4 = copies.start(fit_half, fit_half, at.sibling)

    for e in range(2):
        hi, lo = split(xr[e].reshape(8 * rows, PART))
        xh[:, e * PART:(e + 1) * PART] = hi
        xl[:, e * PART:(e + 1) * PART] = lo

    @pl.when(at.off_diagonal)
    def _():
        copies.make(t1, ur_ref.at[col], ur_ref.at[col], at.swapped).wait_recv()
        step_xz.wait_send()

    @pl.when(jnp.logical_not(at.off_diagonal))
    def _():
        ur_ref[col] = relay[...]

    gr.own_ring()

    sp[...] = dot3(split(ur_ref[col]), (xh[...], xl[...]))
    s0 = copies.start(sp.at[pl.ds(pl.multiple_of((1 - k) * half, half), half)], rs0, at.sibling)

    @pl.when(at.inner)
    def _():
        copies.make(d2, uc_ref.at[k, p], uc_ref.at[k, p], at.y_next).wait_recv()
        inner_back.wait_send()

    copies.arrived(s0, rs0, at.sibling)
    sh[...] = sp[pl.ds(pl.multiple_of(k * half, half), half)] + rs0[...]
    s1 = [copies.start(sh, rs1.at[i], d) for i, d in enumerate((at.x_up, at.x_down, at.x_far))]
    u = {(0, 0): to_sibling(0, 0)}
    for i, d in enumerate((at.x_down, at.x_up, at.x_far)):
        copies.arrived(s1[i], rs1.at[i], d)
    sh2[...] = (sh[...] + rs1[2]) + (rs1[0] + rs1[1])
    s2 = copies.start(sh2, rs2, at.y_far)
    gc.own_ring()
    copies.arrived(s2, rs2, at.y_far)
    s_all[k, col] = sh2[...] + rs2[...]
    gs = Gather(copies, s_all.at[k], at.y_lo, at.z, at.y_near, at.z_up, at.z_down, half)
    gs.own()
    gr.own_pair()
    gs.forward_own()
    gs.pair_across()
    gr.forward_own()
    gc.forward_own()
    gc.pair_across()
    for step in ((0, 3), (0, 1), (1, 0)):
        u[step] = to_sibling(*step)
    gs.far_own()
    gs.forward_pair()
    gs.end_by_ring()
    s4 = copies.start(s_all.at[k], s_all.at[k], at.sibling)
    gr.pair_across()
    gr.far_own()
    gr.far_by_pair()
    gc.far_own()
    u[(0, 2)] = to_sibling(0, 2)
    copies.arrived(s4, s_all.at[1 - k], at.sibling)

    for c in range(8):
        for h in range(2):
            a_ref[pl.ds(c * CHUNK + h * half, half)] = s_all[h, c]
    eye = eye_of(ALL)
    a_ref[...] = a_ref[...] + eye
    bound = jnp.max(jnp.sum(jnp.abs(a_ref[...]), axis=0, keepdims=True))
    scale = 2.0 / (1.0 + bound)
    g_ref[...] = scale * (2.0 * eye - scale * a_ref[...])

    def refine(_):
        g = split(g_ref[...])
        error = eye_of(ALL) - dot3(split(a_ref[...]), g)
        g_ref[...] = g_ref[...] + dot3(g, split(error))
        size_ref[...] = jnp.broadcast_to(jnp.sum(error * error), size_ref.shape)

    pl.loop(0, 3)(refine)
    gc.forward_pair()
    for step in ((1, 3), (1, 1)):
        u[step] = to_sibling(*step)
    pl.loop(0, 1)(refine)
    gc.end_by_ring()
    u[(1, 2)] = to_sibling(1, 2)
    gr.end_by_pair()
    other_block = uc_ref.at[1 - k]
    for (pair_step, ring_step), index in u.items():
        copies.arrived(index, other_block.at[gc.slot(pair_step, ring_step)], at.sibling)
    copies.arrived(f4, fit_ref.at[pl.ds(pl.multiple_of((1 - k) * n, n), n)], at.sibling)
    copies.finish()


def panels(features_t, head, tile):
    rows, examples = features_t.shape
    depth, width = tile.shape[0], tile.shape[1] // 2
    classes = head.shape[1]
    half = CHUNK // 2
    vmem = pl.BlockSpec(memory_space=pltpu.VMEM)
    dma = pltpu.SemaphoreType.DMA
    return pl.pallas_call(
        panels_kernel,
        out_shape=(
            jax.ShapeDtypeStruct((2, 8, CHUNK, width), F32),
            jax.ShapeDtypeStruct((8, CHUNK, width), F32),
            jax.ShapeDtypeStruct((ALL, ALL), F32),
            jax.ShapeDtypeStruct((ALL, ALL), F32),
            jax.ShapeDtypeStruct((8, 128), F32),
            jax.ShapeDtypeStruct((ALL, classes), F32),
        ),
        in_specs=[pl.BlockSpec(memory_space=pltpu.HBM)] * 3,
        out_specs=(vmem,) * 6,
        scratch_shapes=[
            pltpu.VMEM(head.shape, F32),
            pltpu.VMEM((2 * BLOCKS, depth, BLOCK), F32),
            pltpu.VMEM((2, 8, rows, PART), F32),
            pltpu.VMEM((examples, 3 * depth), BF16),
            pltpu.VMEM((2, 8, CHUNK, width), F32),
            pltpu.VMEM((8, CHUNK, width), F32),
            pltpu.VMEM((8, CHUNK, width), F32),
            pltpu.VMEM((2, 2, half, width), F32),
            pltpu.VMEM((2, 2, CHUNK, width), F32),
            pltpu.VMEM((2, CHUNK, width), F32),
            pltpu.VMEM((CHUNK, width), F32),
            pltpu.VMEM((depth, examples), BF16),
            pltpu.VMEM((depth, examples), BF16),
            pltpu.VMEM((2, 8, half, ALL), F32),
            pltpu.VMEM((CHUNK, ALL), F32),
            pltpu.VMEM((half, ALL), F32),
            pltpu.VMEM((half, ALL), F32),
            pltpu.VMEM((3, half, ALL), F32),
            pltpu.VMEM((half, ALL), F32),
            pltpu.VMEM((half, ALL), F32),
            pltpu.VMEM((ALL, classes), F32),
            pltpu.VMEM((ALL // 2, classes), F32),
            pltpu.VMEM((ALL // 2, classes), F32),
            pltpu.VMEM((3, ALL // 8, classes), F32),
            pltpu.VMEM((ALL // 8, classes), F32),
            pltpu.VMEM((ALL // 8, classes), F32),
            dma((2 * BLOCKS + 3,)),
            dma((96,)),
            dma((96,)),
        ],
        compiler_params=pltpu.CompilerParams(collective_id=0, has_side_effects=True, vmem_limit_bytes=VMEM_PANELS),
        name="panels",
    )(features_t, head, tile)


def update_kernel(a_ref, g_ref, size_ref, ur_ref, u_ref, r_ref, labels_ref, fit_ref, w_ref, out_ref, head_ref,
                  inv_ref, gain_ref, rv, sems):
    at = pl.program_id(0)

    def load(i):
        return pltpu.make_async_copy(r_ref.at[:, pl.ds(pl.multiple_of(i * BLOCK, 128), BLOCK)], rv.at[i], sems.at[i])

    @pl.when(at == 0)
    def _():
        for i in range(2 * BLOCKS):
            load(i).start()
        inv_ref[...] = g_ref[...]

        def more(state):
            step, size = state
            return (step < 60) & (size > 1e-5)

        def refine(state):
            step, _ = state
            g = inv_ref[...]
            error = eye_of(ALL) - jnp.dot(a_ref[...], g, precision=lax.Precision.HIGHEST, preferred_element_type=F32)
            inv_ref[...] = g + dot3(split(g), split(error))
            return step + 1, jnp.sum(error * error)

        lax.while_loop(more, refine, (jnp.int32(0), size_ref[0, 0]))
        stack_left(gain_ref, dot3(split(ur_ref[...].T), split(inv_ref[...])))
        width = w_ref.shape[1]
        classes = lax.axis_index("col") * width + lax.broadcasted_iota(jnp.int32, (width, ALL), 0)
        targets = jnp.where(labels_ref[...] == classes, 1.0, 0.0).astype(F32).T
        head_ref[...] = w_ref[...] + mm(gain_ref[...], stack_right(targets - fit_ref[...]))

    load(at).wait()
    out_ref[...] = rv[at] - mm(gain_ref[...], stack_right(u_ref[0]))


def update(system, inverse, size, rows_t, cols_t, tile, labels, fitted, head):
    rows = tile.shape[0]
    vmem = pl.BlockSpec(memory_space=pltpu.VMEM)
    return pl.pallas_call(
        update_kernel,
        grid=(2 * BLOCKS,),
        out_shape=(jax.ShapeDtypeStruct(tile.shape, F32), jax.ShapeDtypeStruct(head.shape, F32)),
        in_specs=[vmem] * 4 + [
            pl.BlockSpec((1, ALL, BLOCK), lambda i: (i // BLOCKS, 0, lax.rem(i, BLOCKS))),
            pl.BlockSpec(memory_space=pl.ANY),
        ] + [vmem] * 3,
        out_specs=(pl.BlockSpec((rows, BLOCK), lambda i: (0, i)), pl.BlockSpec(head.shape, lambda i: (0, 0))),
        scratch_shapes=[
            pltpu.VMEM((ALL, ALL), F32),
            pltpu.VMEM((rows, 3 * ALL), BF16),
            pltpu.VMEM((2 * BLOCKS, rows, BLOCK), F32),
            pltpu.SemaphoreType.DMA((2 * BLOCKS,)),
        ],
        compiler_params=pltpu.CompilerParams(vmem_limit_bytes=VMEM_UPDATE),
        name="update",
    )(system, inverse, size, rows_t, cols_t, tile, labels.reshape(1, ALL), fitted, head)


def on_device(features_t, labels, inv_corr, heads):
    cols_t, rows_t, system, inverse, size, fitted = panels(features_t, heads, inv_corr)
    block = cols_t.shape[3]
    return update(system, inverse, size, rows_t.reshape(ALL, block), cols_t.reshape(2, ALL, block), inv_corr, labels,
                  fitted, heads)


def solution(mesh):
    placed = (P(("row", "col"), None), P(), P("row", "col"), P("row", "col"))
    return jax.shard_map(
        on_device,
        mesh=mesh,
        in_specs=placed,
        out_specs=(P("row", "col"), P("row", "col")),
        check_vma=False,
    )
```

```python
import jax
import jax.numpy as jnp
from jax import lax
from jax.experimental import pallas as pl
from jax.experimental.pallas import tpu as pltpu
from jax.sharding import PartitionSpec as P

F32 = jnp.float32
BF16 = jnp.bfloat16
MESH = pl.DeviceIdType.MESH
ALL = 512
CHUNK = 64
MIB = 1 << 20
VMEM_PANELS = 44 * MIB
VMEM_UPDATE = 34 * MIB


def split(value):
    hi = value.astype(BF16)
    lo = (value - hi.astype(F32)).astype(BF16)
    return hi, lo


def mm(left, right):
    return jnp.dot(left, right, preferred_element_type=F32)


def dot3(left, right):
    (lh, ll), (rh, rl) = left, right
    return mm(lh, rh) + (mm(lh, rl) + mm(ll, rh))


class Place:
    def __init__(self):
        self.row, self.col = row, col = lax.axis_index("row"), lax.axis_index("col")
        self.core = core = lax.rem(row, 2)
        self.chip_row = chip_row = row // 2
        self.y_hi, self.x = y_hi, x = chip_row // 4, lax.rem(chip_row, 4)
        self.y_lo, self.z = y_lo, z = col // 4, lax.rem(col, 4)
        self.sibling = (chip_row * 2 + (1 - core), col)
        self.x_up = ((y_hi * 4 + lax.rem(x + 1, 4)) * 2 + core, col)
        self.x_down = ((y_hi * 4 + lax.rem(x + 3, 4)) * 2 + core, col)
        self.x_far = ((y_hi * 4 + lax.rem(x + 2, 4)) * 2 + core, col)
        self.y_far = (((1 - y_hi) * 4 + x) * 2 + core, col)
        self.z_up = (row, y_lo * 4 + lax.rem(z + 1, 4))
        self.z_down = (row, y_lo * 4 + lax.rem(z + 3, 4))
        self.y_near = (row, (1 - y_lo) * 4 + z)
        self.y_next = (((1 - y_hi) * 4 + x) * 2 + core, (1 - y_lo) * 4 + z)
        self.swapped = ((y_hi * 4 + z) * 2 + core, y_lo * 4 + x)
        self.inner = y_hi != y_lo
        self.off_diagonal = x != z
        between = lax.rem(y_hi + y_lo, 2)
        back_y, side_y = lax.rem(y_hi + 1 - between, 2), lax.rem(y_lo + between, 2)
        self.spread_to = ((back_y * 4 + x) * 2 + core, side_y * 4 + z)
        self.spread_slot = lax.rem(y_hi + between, 2) * 4 + x
        self.sum_to = [((y_lo * 4 + x) * 2 + core, part * 4 + z) for part in range(2)]


class Copies:
    def __init__(self, send_sems, recv_sems):
        self.send_sems, self.recv_sems = send_sems, recv_sems
        self.count = 0
        self.started = []

    def take(self):
        self.count += 1
        return self.count - 1

    def make(self, index, src, dst, device, recv=None):
        recv = index if recv is None else recv
        return pltpu.make_async_remote_copy(
            src_ref=src, dst_ref=dst, send_sem=self.send_sems.at[index], recv_sem=self.recv_sems.at[recv],
            device_id=device, device_id_type=MESH)

    def start(self, src, dst, device):
        index = self.take()
        copy = self.make(index, src, dst, device)
        copy.start()
        self.started.append(copy)
        return index

    def arrived(self, index, landing, device):
        self.make(index, landing, landing, device).wait_recv()

    def finish(self):
        for copy in self.started:
            copy.wait_send()


def greet(devices, maybe):
    barrier = pltpu.get_barrier_semaphore()
    total = jnp.int32(len(devices))
    for device in devices:
        pl.semaphore_signal(barrier, inc=1, device_id=device, device_id_type=MESH)
    for there, device in maybe:
        total = total + jnp.where(there, 1, 0)

        @pl.when(there)
        def _():
            pl.semaphore_signal(barrier, inc=1, device_id=device, device_id_type=MESH)

    pl.semaphore_wait(barrier, total)


class Gather:
    def __init__(self, copies, buf, pair_at, ring_at, pair, up, down, rows):
        self.c, self.buf, self.rows = copies, buf, rows
        self.a, self.b = pair_at, ring_at
        self.pair, self.up, self.down = pair, up, down

    def slot(self, pair_step, ring_step):
        a = self.a if pair_step == 0 else 1 - self.a
        return a * 4 + lax.rem(self.b + ring_step, 4)

    def part(self, pair_step, ring_step, half=None):
        at = self.slot(pair_step, ring_step)
        if half is None:
            return self.buf.at[at]
        n = self.rows // 2
        return self.buf.at[at, pl.ds(half * n, n)]

    def same(self, part, device):
        return self.c.start(part, part, device)

    def own(self):
        self.own_ring()
        self.own_pair()

    def own_pair(self):
        self.i_pair = self.same(self.part(0, 0), self.pair)

    def own_ring(self):
        mine = self.part(0, 0)
        self.i_up = self.same(mine, self.up)
        self.i_down = self.same(mine, self.down)

    def forward_own(self):
        self.c.arrived(self.i_up, self.part(0, 3), self.down)
        self.h_up = self.same(self.part(0, 3, 0), self.up)
        self.c.arrived(self.i_down, self.part(0, 1), self.up)
        self.h_down = self.same(self.part(0, 1, 1), self.down)

    def pair_across(self):
        self.c.arrived(self.i_pair, self.part(1, 0), self.pair)
        self.q_up = self.same(self.part(1, 0), self.up)
        self.q_down = self.same(self.part(1, 0), self.down)

    def far_own(self):
        self.c.arrived(self.h_up, self.part(0, 2, 0), self.down)
        self.c.arrived(self.h_down, self.part(0, 2, 1), self.up)

    def far_by_pair(self):
        self.f_pair = self.same(self.part(0, 2), self.pair)

    def end_by_pair(self):
        self.c.arrived(self.q_up, self.part(1, 3), self.down)
        self.c.arrived(self.q_down, self.part(1, 1), self.up)
        self.c.arrived(self.f_pair, self.part(1, 2), self.pair)

    def forward_pair(self):
        self.c.arrived(self.q_up, self.part(1, 3), self.down)
        self.g_up = self.same(self.part(1, 3, 0), self.up)
        self.c.arrived(self.q_down, self.part(1, 1), self.up)
        self.g_down = self.same(self.part(1, 1, 1), self.down)

    def end_by_ring(self):
        self.c.arrived(self.g_up, self.part(1, 2, 0), self.down)
        self.c.arrived(self.g_down, self.part(1, 2, 1), self.up)


def stack_left(ref, value):
    hi, lo = split(value)
    depth = value.shape[1]
    ref[:, 0:depth] = hi
    ref[:, depth:2 * depth] = hi
    ref[:, 2 * depth:] = lo


def stack_right(value):
    hi, lo = split(value)
    return jnp.concatenate([hi, lo, hi], 0)


def eye_of(order):
    rows = lax.broadcasted_iota(jnp.int32, (order, order), 0)
    cols = lax.broadcasted_iota(jnp.int32, (order, order), 1)
    return jnp.where(rows == cols, 1.0, 0.0).astype(F32)


BLOCKS = 3
BLOCK = 384
PART = 256


def panels_kernel(x_ref, w_ref, r_ref, uc_ref, ur_ref, a_ref, g_ref, size_ref, fit_ref,
                  wv, rv, xr, xs, part, from_sib, ra, rb, ry, relay, xh, xl, s_all, sp, rs0, sh, rs1, sh2, rs2,
                  fx, rf0, fh, rf1, fh2, rf2, local_sems, send_sems, recv_sems):
    at = Place()
    k, p, col = at.core, at.chip_row, at.col
    rows = x_ref.shape[0]
    turns = [(1 - k, j) for j in range(BLOCKS)] + [(k, j) for j in range(BLOCKS)]

    def columns(h, j):
        return pl.ds(pl.multiple_of((h * BLOCKS + j) * BLOCK, 128), BLOCK)

    own_x = [pltpu.make_async_copy(x_ref.at[:, pl.ds(e * PART, PART)], xr.at[e, col], local_sems.at[2 * BLOCKS + e])
             for e in range(2)]
    for copy in own_x:
        copy.start()
    own_w = pltpu.make_async_copy(w_ref, wv, local_sems.at[2 * BLOCKS + 2])
    own_w.start()
    loads = []
    for i, (h, j) in enumerate(turns):
        loads.append(pltpu.make_async_copy(r_ref.at[:, columns(h, j)], rv.at[i], local_sems.at[i]))
        loads[-1].start()
    greet([at.sibling, at.x_up, at.x_down, at.x_far, at.y_far, at.z_up, at.z_down, at.y_near],
          [(at.inner, at.y_next), (at.off_diagonal, at.swapped)])
    for copy in own_x:
        copy.wait()
    copies = Copies(send_sems, recv_sems)

    ga, gb = (Gather(copies, xr.at[e], at.y_lo, at.z, at.y_near, at.z_up, at.z_down, rows) for e in range(2))
    ga.own()
    ga.forward_own()
    ga.pair_across()
    ga.far_own()
    ga.far_by_pair()
    gb.own()
    ga.end_by_pair()

    def stack_features(e):
        stack_left(xs.at[pl.ds(e * PART, PART)], xr[e].reshape(8 * rows, PART).T)

    def product(e, i):
        h, j = turns[i]
        if e == 0:
            loads[i].wait()
        value = mm(xs[e * PART:(e + 1) * PART], stack_right(rv[i]))
        part[h, 4 * e:4 * e + 4, :, j * BLOCK:(j + 1) * BLOCK] = value.reshape(4, CHUNK, BLOCK)

    acc = part.at[k]
    sib = {}

    def part_to_sibling(e, j):
        piece = (pl.ds(4 * e, 4), slice(None), slice(j * BLOCK, (j + 1) * BLOCK))
        sib[e, j] = copies.start(part.at[(1 - k,) + piece], from_sib.at[piece], at.sibling)

    half = CHUNK // 2
    low, high = pl.ds(0, half), pl.ds(half, half)
    a_up, a_down, b_up, b_down = {}, {}, {}, {}

    def chunk(e, x_step):
        return e * 4 + lax.rem(at.x + x_step, 4)

    def scatter_far(e):
        for j in range(BLOCKS):
            copies.arrived(sib[e, j], from_sib.at[pl.ds(4 * e, 4), :, j * BLOCK:(j + 1) * BLOCK], at.sibling)
        for x_step in (2, 1, 3, 0):
            ch = chunk(e, x_step)
            acc[ch] = acc[ch] + from_sib[ch]
            if x_step == 2:
                a_up[e] = copies.start(acc.at[ch, low], ra.at[0, e], at.x_up)
                a_down[e] = copies.start(acc.at[ch, high], ra.at[1, e], at.x_down)

    def scatter_near(e):
        ch = chunk(e, 1)
        copies.arrived(a_up[e], ra.at[0, e], at.x_down)
        acc[ch, low] = acc[ch, low] + ra[0, e]
        b_up[e] = copies.start(acc.at[ch], rb.at[0, e], at.x_up)
        ch = chunk(e, 3)
        copies.arrived(a_down[e], ra.at[1, e], at.x_up)
        acc[ch, high] = acc[ch, high] + ra[1, e]
        b_down[e] = copies.start(acc.at[ch], rb.at[1, e], at.x_down)

    y_sems = [copies.take() for _ in range(2)]

    def sum_copy(e):
        return copies.make(y_sems[e], acc.at[chunk(e, 0)], ry.at[at.y_hi], at.sum_to[e], y_sems[0] + at.y_hi)

    def stays(e):
        return (at.y_hi == e) & (at.y_lo == e)

    def scatter_end(e):
        ch = chunk(e, 0)
        copies.arrived(b_up[e], rb.at[0, e], at.x_down)
        copies.arrived(b_down[e], rb.at[1, e], at.x_up)
        acc[ch] = acc[ch] + (rb[0, e] + rb[1, e])

        @pl.when(jnp.logical_not(stays(e)))
        def _():
            sum_copy(e).start()

    stack_features(0)
    product(0, 0)
    part_to_sibling(0, 0)
    product(0, 1)
    part_to_sibling(0, 1)
    gb.forward_own()
    product(0, 2)
    part_to_sibling(0, 2)
    product(0, 3)
    gb.pair_across()
    product(0, 4)
    product(0, 5)
    scatter_far(0)
    gb.far_own()
    gb.far_by_pair()
    gb.end_by_pair()
    stack_features(1)
    product(1, 0)
    part_to_sibling(1, 0)
    scatter_near(0)

    own_w.wait()
    fx[...] = mm(xs[...], stack_right(wv[...]))
    n = ALL // 2
    quarter = n // 4
    f0 = copies.start(fx.at[pl.ds(pl.multiple_of((1 - k) * n, n), n)], rf0, at.sibling)
    product(1, 1)
    part_to_sibling(1, 1)
    product(1, 2)
    part_to_sibling(1, 2)
    copies.arrived(f0, rf0, at.sibling)
    fh[...] = fx[pl.ds(pl.multiple_of(k * n, n), n)] + rf0[...]

    def quarter_at(x_step, base=0):
        return pl.ds(pl.multiple_of(base + lax.rem(at.x + x_step, 4) * quarter, quarter), quarter)

    steps = ((1, at.x_up), (3, at.x_down), (2, at.x_far))
    f1 = [copies.start(fh.at[quarter_at(t)], rf1.at[i], d) for i, (t, d) in enumerate(steps)]
    product(1, 3)
    product(1, 4)
    product(1, 5)
    scatter_far(1)
    scatter_end(0)
    for i, d in enumerate((at.x_down, at.x_up, at.x_far)):
        copies.arrived(f1[i], rf1.at[i], d)
    fh2[...] = (fh[quarter_at(0)] + rf1[2]) + (rf1[0] + rf1[1])
    f2 = copies.start(fh2, rf2, at.y_far)
    scatter_near(1)
    copies.arrived(f2, rf2, at.y_far)
    fit_own = fit_ref.at[quarter_at(0, k * n)]
    fit_own[...] = fh2[...] + rf2[...]
    f3 = [copies.start(fit_own, fit_own, d) for _, d in steps]
    scatter_end(1)

    own = at.y_hi * 4 + at.x

    @pl.when(at.inner)
    def _():
        for i in range(2):
            copies.make(y_sems[0], ry.at[i], ry.at[i], at.y_next, y_sems[i]).wait_recv()
        relay[...] = ry[0] + ry[1]

    @pl.when(jnp.logical_not(at.inner))
    def _():
        there = 1 - at.y_hi
        copies.make(y_sems[0], ry.at[there], ry.at[there], at.y_far, y_sems[0] + there).wait_recv()
        relay[...] = acc[own] + ry[there]
        uc_ref[k, p] = relay[...]

    for e in range(2):
        @pl.when(jnp.logical_not(stays(e)))
        def _():
            sum_copy(e).wait_send()

    t1 = copies.take()
    step_xz = copies.make(t1, relay, ur_ref.at[at.y_lo * 4 + at.x], at.swapped)

    @pl.when(at.off_diagonal)
    def _():
        step_xz.start()

    d1 = copies.start(relay, uc_ref.at[k, at.spread_slot], at.spread_to)
    d2 = copies.take()
    inner_back = copies.make(d2, relay, uc_ref.at[k, at.spread_slot], at.y_next)

    @pl.when(at.inner)
    def _():
        inner_back.start()

    own_block = uc_ref.at[k]
    gc = Gather(copies, own_block, at.y_hi, at.x, at.y_far, at.x_up, at.x_down, CHUNK)
    gr = Gather(copies, ur_ref, at.y_lo, at.z, at.y_near, at.z_up, at.z_down, CHUNK)
    gc.i_pair = d1

    def to_sibling(pair_step, ring_step):
        piece = gc.part(pair_step, ring_step)
        return copies.start(piece, piece, at.sibling)

    for f, t, d in zip(f3, (3, 1, 2), (at.x_down, at.x_up, at.x_far)):
        copies.arrived(f, fit_ref.at[quarter_at(t, k * n)], d)
    fit_half = fit_ref.at[pl.ds(pl.multiple_of(k * n, n), n)]
    f4 = copies.start(fit_half, fit_half, at.sibling)

    for e in range(2):
        hi, lo = split(xr[e].reshape(8 * rows, PART))
        xh[:, e * PART:(e + 1) * PART] = hi
        xl[:, e * PART:(e + 1) * PART] = lo

    @pl.when(at.off_diagonal)
    def _():
        copies.make(t1, ur_ref.at[col], ur_ref.at[col], at.swapped).wait_recv()
        step_xz.wait_send()

    @pl.when(jnp.logical_not(at.off_diagonal))
    def _():
        ur_ref[col] = relay[...]

    gr.own_ring()

    sp[...] = dot3(split(ur_ref[col]), (xh[...], xl[...]))
    s0 = copies.start(sp.at[pl.ds(pl.multiple_of((1 - k) * half, half), half)], rs0, at.sibling)

    @pl.when(at.inner)
    def _():
        copies.make(d2, uc_ref.at[k, p], uc_ref.at[k, p], at.y_next).wait_recv()
        inner_back.wait_send()

    copies.arrived(s0, rs0, at.sibling)
    sh[...] = sp[pl.ds(pl.multiple_of(k * half, half), half)] + rs0[...]
    s1 = [copies.start(sh, rs1.at[i], d) for i, d in enumerate((at.x_up, at.x_down, at.x_far))]
    u = {(0, 0): to_sibling(0, 0)}
    for i, d in enumerate((at.x_down, at.x_up, at.x_far)):
        copies.arrived(s1[i], rs1.at[i], d)
    sh2[...] = (sh[...] + rs1[2]) + (rs1[0] + rs1[1])
    s2 = copies.start(sh2, rs2, at.y_far)
    gc.own_ring()
    copies.arrived(s2, rs2, at.y_far)
    s_all[k, col] = sh2[...] + rs2[...]
    gs = Gather(copies, s_all.at[k], at.y_lo, at.z, at.y_near, at.z_up, at.z_down, half)
    gs.own()
    gr.own_pair()
    gs.forward_own()
    gs.pair_across()
    gr.forward_own()
    gc.forward_own()
    gc.pair_across()
    for step in ((0, 3), (0, 1), (1, 0)):
        u[step] = to_sibling(*step)
    gs.far_own()
    gs.forward_pair()
    gs.end_by_ring()
    s4 = copies.start(s_all.at[k], s_all.at[k], at.sibling)
    gr.pair_across()
    gr.far_own()
    gr.far_by_pair()
    gc.far_own()
    u[(0, 2)] = to_sibling(0, 2)
    copies.arrived(s4, s_all.at[1 - k], at.sibling)

    for c in range(8):
        for h in range(2):
            a_ref[pl.ds(c * CHUNK + h * half, half)] = s_all[h, c]
    eye = eye_of(ALL)
    a_ref[...] = a_ref[...] + eye
    bound = jnp.max(jnp.sum(jnp.abs(a_ref[...]), axis=0, keepdims=True))
    scale = 2.0 / (1.0 + bound)
    g_ref[...] = scale * (2.0 * eye - scale * a_ref[...])

    def refine(_):
        g = split(g_ref[...])
        error = eye_of(ALL) - dot3(split(a_ref[...]), g)
        g_ref[...] = g_ref[...] + dot3(g, split(error))
        size_ref[...] = jnp.broadcast_to(jnp.sum(error * error), size_ref.shape)

    pl.loop(0, 3)(refine)
    gc.forward_pair()
    for step in ((1, 3), (1, 1)):
        u[step] = to_sibling(*step)
    pl.loop(0, 1)(refine)
    gc.end_by_ring()
    u[(1, 2)] = to_sibling(1, 2)
    gr.end_by_pair()
    other_block = uc_ref.at[1 - k]
    for (pair_step, ring_step), index in u.items():
        copies.arrived(index, other_block.at[gc.slot(pair_step, ring_step)], at.sibling)
    copies.arrived(f4, fit_ref.at[pl.ds(pl.multiple_of((1 - k) * n, n), n)], at.sibling)
    copies.finish()


def panels(features_t, head, tile):
    rows, examples = features_t.shape
    depth, width = tile.shape[0], tile.shape[1] // 2
    classes = head.shape[1]
    half = CHUNK // 2
    vmem = pl.BlockSpec(memory_space=pltpu.VMEM)
    dma = pltpu.SemaphoreType.DMA
    return pl.pallas_call(
        panels_kernel,
        out_shape=(
            jax.ShapeDtypeStruct((2, 8, CHUNK, width), F32),
            jax.ShapeDtypeStruct((8, CHUNK, width), F32),
            jax.ShapeDtypeStruct((ALL, ALL), F32),
            jax.ShapeDtypeStruct((ALL, ALL), F32),
            jax.ShapeDtypeStruct((8, 128), F32),
            jax.ShapeDtypeStruct((ALL, classes), F32),
        ),
        in_specs=[pl.BlockSpec(memory_space=pltpu.HBM)] * 3,
        out_specs=(vmem,) * 6,
        scratch_shapes=[
            pltpu.VMEM(head.shape, F32),
            pltpu.VMEM((2 * BLOCKS, depth, BLOCK), F32),
            pltpu.VMEM((2, 8, rows, PART), F32),
            pltpu.VMEM((examples, 3 * depth), BF16),
            pltpu.VMEM((2, 8, CHUNK, width), F32),
            pltpu.VMEM((8, CHUNK, width), F32),
            pltpu.VMEM((2, 2, half, width), F32),
            pltpu.VMEM((2, 2, CHUNK, width), F32),
            pltpu.VMEM((2, CHUNK, width), F32),
            pltpu.VMEM((CHUNK, width), F32),
            pltpu.VMEM((depth, examples), BF16),
            pltpu.VMEM((depth, examples), BF16),
            pltpu.VMEM((2, 8, half, ALL), F32),
            pltpu.VMEM((CHUNK, ALL), F32),
            pltpu.VMEM((half, ALL), F32),
            pltpu.VMEM((half, ALL), F32),
            pltpu.VMEM((3, half, ALL), F32),
            pltpu.VMEM((half, ALL), F32),
            pltpu.VMEM((half, ALL), F32),
            pltpu.VMEM((ALL, classes), F32),
            pltpu.VMEM((ALL // 2, classes), F32),
            pltpu.VMEM((ALL // 2, classes), F32),
            pltpu.VMEM((3, ALL // 8, classes), F32),
            pltpu.VMEM((ALL // 8, classes), F32),
            pltpu.VMEM((ALL // 8, classes), F32),
            dma((2 * BLOCKS + 3,)),
            dma((96,)),
            dma((96,)),
        ],
        compiler_params=pltpu.CompilerParams(collective_id=0, has_side_effects=True, vmem_limit_bytes=VMEM_PANELS),
        name="panels",
    )(pltpu.with_memory_space_constraint(features_t, pltpu.HBM),
      pltpu.with_memory_space_constraint(head, pltpu.HBM),
      pltpu.with_memory_space_constraint(tile, pltpu.HBM))


def update_kernel(a_ref, g_ref, size_ref, ur_ref, u_ref, r_ref, labels_ref, fit_ref, w_ref, out_ref, head_ref,
                  inv_ref, gain_ref, rv, sems):
    at = pl.program_id(0)

    def load(i):
        return pltpu.make_async_copy(r_ref.at[:, pl.ds(pl.multiple_of(i * BLOCK, 128), BLOCK)], rv.at[i], sems.at[i])

    @pl.when(at == 0)
    def _():
        for i in range(2 * BLOCKS):
            load(i).start()
        inv_ref[...] = g_ref[...]

        def more(state):
            step, size = state
            return (step < 60) & (size > 1e-5)

        def refine(state):
            step, _ = state
            g = inv_ref[...]
            error = eye_of(ALL) - jnp.dot(a_ref[...], g, precision=lax.Precision.HIGHEST, preferred_element_type=F32)
            inv_ref[...] = g + dot3(split(g), split(error))
            return step + 1, jnp.sum(error * error)

        lax.while_loop(more, refine, (jnp.int32(0), size_ref[0, 0]))
        stack_left(gain_ref, dot3(split(ur_ref[...].T), split(inv_ref[...])))
        width = w_ref.shape[1]
        classes = lax.axis_index("col") * width + lax.broadcasted_iota(jnp.int32, (width, ALL), 0)
        targets = jnp.where(labels_ref[...] == classes, 1.0, 0.0).astype(F32).T
        head_ref[...] = w_ref[...] + mm(gain_ref[...], stack_right(targets - fit_ref[...]))

    load(at).wait()
    block = u_ref[at // BLOCKS, :, pl.ds(pl.multiple_of(lax.rem(at, BLOCKS) * BLOCK, 128), BLOCK)]
    out_ref[...] = rv[at] - mm(gain_ref[...], stack_right(block))


def update(system, inverse, size, rows_t, cols_t, tile, labels, fitted, head):
    rows = tile.shape[0]
    vmem = pl.BlockSpec(memory_space=pltpu.VMEM)
    return pl.pallas_call(
        update_kernel,
        grid=(2 * BLOCKS,),
        out_shape=(jax.ShapeDtypeStruct(tile.shape, F32), jax.ShapeDtypeStruct(head.shape, F32)),
        in_specs=[vmem] * 4 + [
            vmem,
            pl.BlockSpec(memory_space=pl.ANY),
        ] + [vmem] * 3,
        out_specs=(pl.BlockSpec((rows, BLOCK), lambda i: (0, i)), pl.BlockSpec(head.shape, lambda i: (0, 0))),
        scratch_shapes=[
            pltpu.VMEM((ALL, ALL), F32),
            pltpu.VMEM((rows, 3 * ALL), BF16),
            pltpu.VMEM((2 * BLOCKS, rows, BLOCK), F32),
            pltpu.SemaphoreType.DMA((2 * BLOCKS,)),
        ],
        compiler_params=pltpu.CompilerParams(vmem_limit_bytes=VMEM_UPDATE),
        name="update",
    )(system, inverse, size, rows_t, cols_t, pltpu.with_memory_space_constraint(tile, pltpu.HBM), labels.reshape(1, ALL), fitted, head)


def on_device(features_t, labels, inv_corr, heads):
    cols_t, rows_t, system, inverse, size, fitted = panels(features_t, heads, inv_corr)
    block = cols_t.shape[3]
    return update(system, inverse, size, rows_t.reshape(ALL, block), cols_t.reshape(2, ALL, block), inv_corr, labels,
                  fitted, heads)


def solution(mesh):
    placed = (P(("row", "col"), None), P(), P("row", "col"), P("row", "col"))
    return jax.shard_map(
        on_device,
        mesh=mesh,
        in_specs=placed,
        out_specs=(P("row", "col"), P("row", "col")),
        check_vma=False,
    )
```

```python
import jax
import jax.numpy as jnp
from jax import lax
from jax.experimental import pallas as pl
from jax.experimental.pallas import tpu as pltpu
from jax.sharding import PartitionSpec as P

F32 = jnp.float32
BF16 = jnp.bfloat16
MESH = pl.DeviceIdType.MESH
ALL = 512
CHUNK = 64
MIB = 1 << 20
VMEM_PANELS = 44 * MIB
VMEM_UPDATE = 34 * MIB


def split(value):
    hi = value.astype(BF16)
    lo = (value - hi.astype(F32)).astype(BF16)
    return hi, lo


def mm(left, right):
    return jnp.dot(left, right, preferred_element_type=F32)


def dot3(left, right):
    (lh, ll), (rh, rl) = left, right
    return mm(lh, rh) + (mm(lh, rl) + mm(ll, rh))


class Place:
    def __init__(self):
        self.row, self.col = row, col = lax.axis_index("row"), lax.axis_index("col")
        self.core = core = lax.rem(row, 2)
        self.chip_row = chip_row = row // 2
        self.y_hi, self.x = y_hi, x = chip_row // 4, lax.rem(chip_row, 4)
        self.y_lo, self.z = y_lo, z = col // 4, lax.rem(col, 4)
        self.sibling = (chip_row * 2 + (1 - core), col)
        self.x_up = ((y_hi * 4 + lax.rem(x + 1, 4)) * 2 + core, col)
        self.x_down = ((y_hi * 4 + lax.rem(x + 3, 4)) * 2 + core, col)
        self.x_far = ((y_hi * 4 + lax.rem(x + 2, 4)) * 2 + core, col)
        self.y_far = (((1 - y_hi) * 4 + x) * 2 + core, col)
        self.z_up = (row, y_lo * 4 + lax.rem(z + 1, 4))
        self.z_down = (row, y_lo * 4 + lax.rem(z + 3, 4))
        self.y_near = (row, (1 - y_lo) * 4 + z)
        self.y_next = (((1 - y_hi) * 4 + x) * 2 + core, (1 - y_lo) * 4 + z)
        self.swapped = ((y_hi * 4 + z) * 2 + core, y_lo * 4 + x)
        self.inner = y_hi != y_lo
        self.off_diagonal = x != z
        between = lax.rem(y_hi + y_lo, 2)
        back_y, side_y = lax.rem(y_hi + 1 - between, 2), lax.rem(y_lo + between, 2)
        self.spread_to = ((back_y * 4 + x) * 2 + core, side_y * 4 + z)
        self.spread_slot = lax.rem(y_hi + between, 2) * 4 + x
        self.sum_to = [((y_lo * 4 + x) * 2 + core, part * 4 + z) for part in range(2)]


class Copies:
    def __init__(self, send_sems, recv_sems):
        self.send_sems, self.recv_sems = send_sems, recv_sems
        self.count = 0
        self.started = []

    def take(self):
        self.count += 1
        return self.count - 1

    def make(self, index, src, dst, device, recv=None):
        recv = index if recv is None else recv
        return pltpu.make_async_remote_copy(
            src_ref=src, dst_ref=dst, send_sem=self.send_sems.at[index], recv_sem=self.recv_sems.at[recv],
            device_id=device, device_id_type=MESH)

    def start(self, src, dst, device):
        index = self.take()
        copy = self.make(index, src, dst, device)
        copy.start()
        self.started.append(copy)
        return index

    def arrived(self, index, landing, device):
        self.make(index, landing, landing, device).wait_recv()

    def finish(self):
        for copy in self.started:
            copy.wait_send()


def greet(devices, maybe):
    barrier = pltpu.get_barrier_semaphore()
    total = jnp.int32(len(devices))
    for device in devices:
        pl.semaphore_signal(barrier, inc=1, device_id=device, device_id_type=MESH)
    for there, device in maybe:
        total = total + jnp.where(there, 1, 0)

        @pl.when(there)
        def _():
            pl.semaphore_signal(barrier, inc=1, device_id=device, device_id_type=MESH)

    pl.semaphore_wait(barrier, total)


class Gather:
    def __init__(self, copies, buf, pair_at, ring_at, pair, up, down, rows):
        self.c, self.buf, self.rows = copies, buf, rows
        self.a, self.b = pair_at, ring_at
        self.pair, self.up, self.down = pair, up, down

    def slot(self, pair_step, ring_step):
        a = self.a if pair_step == 0 else 1 - self.a
        return a * 4 + lax.rem(self.b + ring_step, 4)

    def part(self, pair_step, ring_step, half=None):
        at = self.slot(pair_step, ring_step)
        if half is None:
            return self.buf.at[at]
        n = self.rows // 2
        return self.buf.at[at, pl.ds(half * n, n)]

    def same(self, part, device):
        return self.c.start(part, part, device)

    def own(self):
        self.own_ring()
        self.own_pair()

    def own_pair(self):
        self.i_pair = self.same(self.part(0, 0), self.pair)

    def own_ring(self):
        mine = self.part(0, 0)
        self.i_up = self.same(mine, self.up)
        self.i_down = self.same(mine, self.down)

    def forward_own(self):
        self.c.arrived(self.i_up, self.part(0, 3), self.down)
        self.h_up = self.same(self.part(0, 3, 0), self.up)
        self.c.arrived(self.i_down, self.part(0, 1), self.up)
        self.h_down = self.same(self.part(0, 1, 1), self.down)

    def pair_across(self):
        self.c.arrived(self.i_pair, self.part(1, 0), self.pair)
        self.q_up = self.same(self.part(1, 0), self.up)
        self.q_down = self.same(self.part(1, 0), self.down)

    def far_own(self):
        self.c.arrived(self.h_up, self.part(0, 2, 0), self.down)
        self.c.arrived(self.h_down, self.part(0, 2, 1), self.up)

    def far_by_pair(self):
        self.f_pair = self.same(self.part(0, 2), self.pair)

    def end_by_pair(self):
        self.c.arrived(self.q_up, self.part(1, 3), self.down)
        self.c.arrived(self.q_down, self.part(1, 1), self.up)
        self.c.arrived(self.f_pair, self.part(1, 2), self.pair)

    def forward_pair(self):
        self.c.arrived(self.q_up, self.part(1, 3), self.down)
        self.g_up = self.same(self.part(1, 3, 0), self.up)
        self.c.arrived(self.q_down, self.part(1, 1), self.up)
        self.g_down = self.same(self.part(1, 1, 1), self.down)

    def end_by_ring(self):
        self.c.arrived(self.g_up, self.part(1, 2, 0), self.down)
        self.c.arrived(self.g_down, self.part(1, 2, 1), self.up)


def stack_left(ref, value):
    hi, lo = split(value)
    depth = value.shape[1]
    ref[:, 0:depth] = hi
    ref[:, depth:2 * depth] = hi
    ref[:, 2 * depth:] = lo


def stack_right(value):
    hi, lo = split(value)
    return jnp.concatenate([hi, lo, hi], 0)


def eye_of(order):
    rows = lax.broadcasted_iota(jnp.int32, (order, order), 0)
    cols = lax.broadcasted_iota(jnp.int32, (order, order), 1)
    return jnp.where(rows == cols, 1.0, 0.0).astype(F32)


BLOCKS = 3
BLOCK = 384
PART = 256


def panels_kernel(x_ref, w_ref, r_ref, uc_ref, ur_ref, a_ref, g_ref, size_ref, fit_ref,
                  wv, rv, xr, xs, part, from_sib, ra, rb, ry, relay, xh, xl, s_all, sp, rs0, sh, rs1, sh2, rs2,
                  fx, rf0, fh, rf1, fh2, rf2, local_sems, send_sems, recv_sems):
    at = Place()
    k, p, col = at.core, at.chip_row, at.col
    rows = x_ref.shape[0]
    turns = [(1 - k, j) for j in range(BLOCKS)] + [(k, j) for j in range(BLOCKS)]

    def columns(h, j):
        return pl.ds(pl.multiple_of((h * BLOCKS + j) * BLOCK, 128), BLOCK)

    own_x = [pltpu.make_async_copy(x_ref.at[:, pl.ds(e * PART, PART)], xr.at[e, col], local_sems.at[2 * BLOCKS + e])
             for e in range(2)]
    for copy in own_x:
        copy.start()
    own_w = pltpu.make_async_copy(w_ref, wv, local_sems.at[2 * BLOCKS + 2])
    own_w.start()
    loads = []
    for i, (h, j) in enumerate(turns):
        loads.append(pltpu.make_async_copy(r_ref.at[:, columns(h, j)], rv.at[i], local_sems.at[i]))
        loads[-1].start()
    greet([at.sibling, at.x_up, at.x_down, at.x_far, at.y_far, at.z_up, at.z_down, at.y_near],
          [(at.inner, at.y_next), (at.off_diagonal, at.swapped)])
    for copy in own_x:
        copy.wait()
    copies = Copies(send_sems, recv_sems)

    ga, gb = (Gather(copies, xr.at[e], at.y_lo, at.z, at.y_near, at.z_up, at.z_down, rows) for e in range(2))
    ga.own()
    ga.forward_own()
    ga.pair_across()
    gb.own()
    ga.far_own()
    ga.far_by_pair()
    ga.end_by_pair()

    def stack_features(e):
        stack_left(xs.at[pl.ds(e * PART, PART)], xr[e].reshape(8 * rows, PART).T)

    def product(e, i):
        h, j = turns[i]
        if e == 0:
            loads[i].wait()
        value = mm(xs[e * PART:(e + 1) * PART], stack_right(rv[i]))
        part[h, 4 * e:4 * e + 4, :, j * BLOCK:(j + 1) * BLOCK] = value.reshape(4, CHUNK, BLOCK)

    acc = part.at[k]
    sib = {}

    def part_to_sibling(e, j):
        piece = (pl.ds(4 * e, 4), slice(None), slice(j * BLOCK, (j + 1) * BLOCK))
        sib[e, j] = copies.start(part.at[(1 - k,) + piece], from_sib.at[piece], at.sibling)

    half = CHUNK // 2
    low, high = pl.ds(0, half), pl.ds(half, half)
    a_up, a_down, b_up, b_down = {}, {}, {}, {}

    def chunk(e, x_step):
        return e * 4 + lax.rem(at.x + x_step, 4)

    def scatter_far(e):
        for j in range(BLOCKS):
            copies.arrived(sib[e, j], from_sib.at[pl.ds(4 * e, 4), :, j * BLOCK:(j + 1) * BLOCK], at.sibling)
        for x_step in (2, 1, 3, 0):
            ch = chunk(e, x_step)
            acc[ch] = acc[ch] + from_sib[ch]
            if x_step == 2:
                a_up[e] = copies.start(acc.at[ch, low], ra.at[0, e], at.x_up)
                a_down[e] = copies.start(acc.at[ch, high], ra.at[1, e], at.x_down)

    def scatter_near(e):
        ch = chunk(e, 1)
        copies.arrived(a_up[e], ra.at[0, e], at.x_down)
        acc[ch, low] = acc[ch, low] + ra[0, e]
        b_up[e] = copies.start(acc.at[ch], rb.at[0, e], at.x_up)
        ch = chunk(e, 3)
        copies.arrived(a_down[e], ra.at[1, e], at.x_up)
        acc[ch, high] = acc[ch, high] + ra[1, e]
        b_down[e] = copies.start(acc.at[ch], rb.at[1, e], at.x_down)

    y_sems = [copies.take() for _ in range(2)]

    def sum_copy(e):
        return copies.make(y_sems[e], acc.at[chunk(e, 0)], ry.at[at.y_hi], at.sum_to[e], y_sems[0] + at.y_hi)

    def stays(e):
        return (at.y_hi == e) & (at.y_lo == e)

    def scatter_end(e):
        ch = chunk(e, 0)
        copies.arrived(b_up[e], rb.at[0, e], at.x_down)
        copies.arrived(b_down[e], rb.at[1, e], at.x_up)
        acc[ch] = acc[ch] + (rb[0, e] + rb[1, e])

        @pl.when(jnp.logical_not(stays(e)))
        def _():
            sum_copy(e).start()

    stack_features(0)
    gb.forward_own()
    product(0, 0)
    part_to_sibling(0, 0)
    gb.pair_across()
    product(0, 1)
    part_to_sibling(0, 1)
    product(0, 2)
    part_to_sibling(0, 2)
    gb.far_own()
    gb.far_by_pair()
    product(0, 3)
    product(0, 4)
    product(0, 5)
    scatter_far(0)
    gb.end_by_pair()
    stack_features(1)
    product(1, 0)
    part_to_sibling(1, 0)
    scatter_near(0)

    own_w.wait()
    fx[...] = mm(xs[...], stack_right(wv[...]))
    n = ALL // 2
    quarter = n // 4
    f0 = copies.start(fx.at[pl.ds(pl.multiple_of((1 - k) * n, n), n)], rf0, at.sibling)
    product(1, 1)
    part_to_sibling(1, 1)
    product(1, 2)
    part_to_sibling(1, 2)
    copies.arrived(f0, rf0, at.sibling)
    fh[...] = fx[pl.ds(pl.multiple_of(k * n, n), n)] + rf0[...]

    def quarter_at(x_step, base=0):
        return pl.ds(pl.multiple_of(base + lax.rem(at.x + x_step, 4) * quarter, quarter), quarter)

    steps = ((1, at.x_up), (3, at.x_down), (2, at.x_far))
    f1 = [copies.start(fh.at[quarter_at(t)], rf1.at[i], d) for i, (t, d) in enumerate(steps)]
    product(1, 3)
    product(1, 4)
    product(1, 5)
    scatter_far(1)
    scatter_end(0)
    for i, d in enumerate((at.x_down, at.x_up, at.x_far)):
        copies.arrived(f1[i], rf1.at[i], d)
    fh2[...] = (fh[quarter_at(0)] + rf1[2]) + (rf1[0] + rf1[1])
    f2 = copies.start(fh2, rf2, at.y_far)
    scatter_near(1)
    copies.arrived(f2, rf2, at.y_far)
    fit_own = fit_ref.at[quarter_at(0, k * n)]
    fit_own[...] = fh2[...] + rf2[...]
    f3 = [copies.start(fit_own, fit_own, d) for _, d in steps]
    scatter_end(1)

    own = at.y_hi * 4 + at.x

    @pl.when(at.inner)
    def _():
        for i in range(2):
            copies.make(y_sems[0], ry.at[i], ry.at[i], at.y_next, y_sems[i]).wait_recv()
        relay[...] = ry[0] + ry[1]

    @pl.when(jnp.logical_not(at.inner))
    def _():
        there = 1 - at.y_hi
        copies.make(y_sems[0], ry.at[there], ry.at[there], at.y_far, y_sems[0] + there).wait_recv()
        relay[...] = acc[own] + ry[there]
        uc_ref[k, p] = relay[...]

    for e in range(2):
        @pl.when(jnp.logical_not(stays(e)))
        def _():
            sum_copy(e).wait_send()

    t1 = copies.take()
    step_xz = copies.make(t1, relay, ur_ref.at[at.y_lo * 4 + at.x], at.swapped)

    @pl.when(at.off_diagonal)
    def _():
        step_xz.start()

    d1 = copies.start(relay, uc_ref.at[k, at.spread_slot], at.spread_to)
    d2 = copies.take()
    inner_back = copies.make(d2, relay, uc_ref.at[k, at.spread_slot], at.y_next)

    @pl.when(at.inner)
    def _():
        inner_back.start()

    own_block = uc_ref.at[k]
    gc = Gather(copies, own_block, at.y_hi, at.x, at.y_far, at.x_up, at.x_down, CHUNK)
    gr = Gather(copies, ur_ref, at.y_lo, at.z, at.y_near, at.z_up, at.z_down, CHUNK)
    gc.i_pair = d1

    def to_sibling(pair_step, ring_step):
        piece = gc.part(pair_step, ring_step)
        return copies.start(piece, piece, at.sibling)

    for f, t, d in zip(f3, (3, 1, 2), (at.x_down, at.x_up, at.x_far)):
        copies.arrived(f, fit_ref.at[quarter_at(t, k * n)], d)
    fit_half = fit_ref.at[pl.ds(pl.multiple_of(k * n, n), n)]
    f4 = copies.start(fit_half, fit_half, at.sibling)

    for e in range(2):
        hi, lo = split(xr[e].reshape(8 * rows, PART))
        xh[:, e * PART:(e + 1) * PART] = hi
        xl[:, e * PART:(e + 1) * PART] = lo

    @pl.when(at.off_diagonal)
    def _():
        copies.make(t1, ur_ref.at[col], ur_ref.at[col], at.swapped).wait_recv()
        step_xz.wait_send()

    @pl.when(jnp.logical_not(at.off_diagonal))
    def _():
        ur_ref[col] = relay[...]

    gr.own_ring()

    sp[...] = dot3(split(ur_ref[col]), (xh[...], xl[...]))
    s0 = copies.start(sp.at[pl.ds(pl.multiple_of((1 - k) * half, half), half)], rs0, at.sibling)

    @pl.when(at.inner)
    def _():
        copies.make(d2, uc_ref.at[k, p], uc_ref.at[k, p], at.y_next).wait_recv()
        inner_back.wait_send()

    copies.arrived(s0, rs0, at.sibling)
    sh[...] = sp[pl.ds(pl.multiple_of(k * half, half), half)] + rs0[...]
    s1 = [copies.start(sh, rs1.at[i], d) for i, d in enumerate((at.x_up, at.x_down, at.x_far))]
    u = {(0, 0): to_sibling(0, 0)}
    for i, d in enumerate((at.x_down, at.x_up, at.x_far)):
        copies.arrived(s1[i], rs1.at[i], d)
    sh2[...] = (sh[...] + rs1[2]) + (rs1[0] + rs1[1])
    s2 = copies.start(sh2, rs2, at.y_far)
    gc.own_ring()
    copies.arrived(s2, rs2, at.y_far)
    s_all[k, col] = sh2[...] + rs2[...]
    gs = Gather(copies, s_all.at[k], at.y_lo, at.z, at.y_near, at.z_up, at.z_down, half)
    gs.own()
    gr.own_pair()
    gs.forward_own()
    gs.pair_across()
    gr.forward_own()
    gc.forward_own()
    gc.pair_across()
    for step in ((0, 3), (0, 1), (1, 0)):
        u[step] = to_sibling(*step)
    gs.far_own()
    gs.forward_pair()
    gs.end_by_ring()
    s4 = copies.start(s_all.at[k], s_all.at[k], at.sibling)
    gr.pair_across()
    gr.far_own()
    gr.far_by_pair()
    gc.far_own()
    u[(0, 2)] = to_sibling(0, 2)
    copies.arrived(s4, s_all.at[1 - k], at.sibling)

    for c in range(8):
        for h in range(2):
            a_ref[pl.ds(c * CHUNK + h * half, half)] = s_all[h, c]
    eye = eye_of(ALL)
    a_ref[...] = a_ref[...] + eye
    bound = jnp.max(jnp.sum(jnp.abs(a_ref[...]), axis=0, keepdims=True))
    scale = 2.0 / (1.0 + bound)
    g_ref[...] = scale * (2.0 * eye - scale * a_ref[...])

    def refine(_):
        g = split(g_ref[...])
        error = eye_of(ALL) - dot3(split(a_ref[...]), g)
        g_ref[...] = g_ref[...] + dot3(g, split(error))
        size_ref[...] = jnp.broadcast_to(jnp.sum(error * error), size_ref.shape)

    pl.loop(0, 3)(refine)
    gc.forward_pair()
    for step in ((1, 3), (1, 1)):
        u[step] = to_sibling(*step)
    pl.loop(0, 1)(refine)
    gc.end_by_ring()
    u[(1, 2)] = to_sibling(1, 2)
    gr.end_by_pair()
    other_block = uc_ref.at[1 - k]
    for (pair_step, ring_step), index in u.items():
        copies.arrived(index, other_block.at[gc.slot(pair_step, ring_step)], at.sibling)
    copies.arrived(f4, fit_ref.at[pl.ds(pl.multiple_of((1 - k) * n, n), n)], at.sibling)
    copies.finish()


def panels(features_t, head, tile):
    rows, examples = features_t.shape
    depth, width = tile.shape[0], tile.shape[1] // 2
    classes = head.shape[1]
    half = CHUNK // 2
    vmem = pl.BlockSpec(memory_space=pltpu.VMEM)
    dma = pltpu.SemaphoreType.DMA
    return pl.pallas_call(
        panels_kernel,
        out_shape=(
            jax.ShapeDtypeStruct((2, 8, CHUNK, width), F32),
            jax.ShapeDtypeStruct((8, CHUNK, width), F32),
            jax.ShapeDtypeStruct((ALL, ALL), F32),
            jax.ShapeDtypeStruct((ALL, ALL), F32),
            jax.ShapeDtypeStruct((8, 128), F32),
            jax.ShapeDtypeStruct((ALL, classes), F32),
        ),
        in_specs=[pl.BlockSpec(memory_space=pltpu.HBM)] * 3,
        out_specs=(vmem,) * 6,
        scratch_shapes=[
            pltpu.VMEM(head.shape, F32),
            pltpu.VMEM((2 * BLOCKS, depth, BLOCK), F32),
            pltpu.VMEM((2, 8, rows, PART), F32),
            pltpu.VMEM((examples, 3 * depth), BF16),
            pltpu.VMEM((2, 8, CHUNK, width), F32),
            pltpu.VMEM((8, CHUNK, width), F32),
            pltpu.VMEM((2, 2, half, width), F32),
            pltpu.VMEM((2, 2, CHUNK, width), F32),
            pltpu.VMEM((2, CHUNK, width), F32),
            pltpu.VMEM((CHUNK, width), F32),
            pltpu.VMEM((depth, examples), BF16),
            pltpu.VMEM((depth, examples), BF16),
            pltpu.VMEM((2, 8, half, ALL), F32),
            pltpu.VMEM((CHUNK, ALL), F32),
            pltpu.VMEM((half, ALL), F32),
            pltpu.VMEM((half, ALL), F32),
            pltpu.VMEM((3, half, ALL), F32),
            pltpu.VMEM((half, ALL), F32),
            pltpu.VMEM((half, ALL), F32),
            pltpu.VMEM((ALL, classes), F32),
            pltpu.VMEM((ALL // 2, classes), F32),
            pltpu.VMEM((ALL // 2, classes), F32),
            pltpu.VMEM((3, ALL // 8, classes), F32),
            pltpu.VMEM((ALL // 8, classes), F32),
            pltpu.VMEM((ALL // 8, classes), F32),
            dma((2 * BLOCKS + 3,)),
            dma((96,)),
            dma((96,)),
        ],
        compiler_params=pltpu.CompilerParams(collective_id=0, has_side_effects=True, vmem_limit_bytes=VMEM_PANELS),
        name="panels",
    )(pltpu.with_memory_space_constraint(features_t, pltpu.HBM),
      pltpu.with_memory_space_constraint(head, pltpu.HBM),
      pltpu.with_memory_space_constraint(tile, pltpu.HBM))


def update_kernel(a_ref, g_ref, size_ref, ur_ref, u_ref, r_ref, labels_ref, fit_ref, w_ref, out_ref, head_ref,
                  inv_ref, gain_ref, rv, sems):
    at = pl.program_id(0)

    def load(i):
        return pltpu.make_async_copy(r_ref.at[:, pl.ds(pl.multiple_of(i * BLOCK, 128), BLOCK)], rv.at[i], sems.at[i])

    @pl.when(at == 0)
    def _():
        for i in range(2 * BLOCKS):
            load(i).start()
        inv_ref[...] = g_ref[...]

        def more(state):
            step, size = state
            return (step < 60) & (size > 1e-5)

        def refine(state):
            step, _ = state
            g = inv_ref[...]
            error = eye_of(ALL) - jnp.dot(a_ref[...], g, precision=lax.Precision.HIGHEST, preferred_element_type=F32)
            inv_ref[...] = g + dot3(split(g), split(error))
            return step + 1, jnp.sum(error * error)

        lax.while_loop(more, refine, (jnp.int32(0), size_ref[0, 0]))
        stack_left(gain_ref, dot3(split(ur_ref[...].T), split(inv_ref[...])))
        width = w_ref.shape[1]
        classes = lax.axis_index("col") * width + lax.broadcasted_iota(jnp.int32, (width, ALL), 0)
        targets = jnp.where(labels_ref[...] == classes, 1.0, 0.0).astype(F32).T
        head_ref[...] = w_ref[...] + mm(gain_ref[...], stack_right(targets - fit_ref[...]))

    load(at).wait()
    block = u_ref[at // BLOCKS, :, pl.ds(pl.multiple_of(lax.rem(at, BLOCKS) * BLOCK, 128), BLOCK)]
    out_ref[...] = rv[at] - mm(gain_ref[...], stack_right(block))


def update(system, inverse, size, rows_t, cols_t, tile, labels, fitted, head):
    rows = tile.shape[0]
    vmem = pl.BlockSpec(memory_space=pltpu.VMEM)
    return pl.pallas_call(
        update_kernel,
        grid=(2 * BLOCKS,),
        out_shape=(jax.ShapeDtypeStruct(tile.shape, F32), jax.ShapeDtypeStruct(head.shape, F32)),
        in_specs=[vmem] * 4 + [
            vmem,
            pl.BlockSpec(memory_space=pl.ANY),
        ] + [vmem] * 3,
        out_specs=(pl.BlockSpec((rows, BLOCK), lambda i: (0, i)), pl.BlockSpec(head.shape, lambda i: (0, 0))),
        scratch_shapes=[
            pltpu.VMEM((ALL, ALL), F32),
            pltpu.VMEM((rows, 3 * ALL), BF16),
            pltpu.VMEM((2 * BLOCKS, rows, BLOCK), F32),
            pltpu.SemaphoreType.DMA((2 * BLOCKS,)),
        ],
        compiler_params=pltpu.CompilerParams(vmem_limit_bytes=VMEM_UPDATE),
        name="update",
    )(system, inverse, size, rows_t, cols_t, pltpu.with_memory_space_constraint(tile, pltpu.HBM), labels.reshape(1, ALL), fitted, head)


def on_device(features_t, labels, inv_corr, heads):
    cols_t, rows_t, system, inverse, size, fitted = panels(features_t, heads, inv_corr)
    block = cols_t.shape[3]
    return update(system, inverse, size, rows_t.reshape(ALL, block), cols_t.reshape(2, ALL, block), inv_corr, labels,
                  fitted, heads)


def solution(mesh):
    placed = (P(("row", "col"), None), P(), P("row", "col"), P("row", "col"))
    return jax.shard_map(
        on_device,
        mesh=mesh,
        in_specs=placed,
        out_specs=(P("row", "col"), P("row", "col")),
        check_vma=False,
    )
```

```python
import jax
import jax.numpy as jnp
from jax import lax
from jax.experimental import pallas as pl
from jax.experimental.pallas import tpu as pltpu
from jax.sharding import PartitionSpec as P

F32 = jnp.float32
BF16 = jnp.bfloat16
MESH = pl.DeviceIdType.MESH
ALL = 512
CHUNK = 64
MIB = 1 << 20
VMEM_PANELS = 44 * MIB
VMEM_UPDATE = 34 * MIB


def split(value):
    hi = value.astype(BF16)
    lo = (value - hi.astype(F32)).astype(BF16)
    return hi, lo


def mm(left, right):
    return jnp.dot(left, right, preferred_element_type=F32)


def dot3(left, right):
    (lh, ll), (rh, rl) = left, right
    return mm(lh, rh) + (mm(lh, rl) + mm(ll, rh))


class Place:
    def __init__(self):
        self.row, self.col = row, col = lax.axis_index("row"), lax.axis_index("col")
        self.core = core = lax.rem(row, 2)
        self.chip_row = chip_row = row // 2
        self.y_hi, self.x = y_hi, x = chip_row // 4, lax.rem(chip_row, 4)
        self.y_lo, self.z = y_lo, z = col // 4, lax.rem(col, 4)
        self.sibling = (chip_row * 2 + (1 - core), col)
        self.x_up = ((y_hi * 4 + lax.rem(x + 1, 4)) * 2 + core, col)
        self.x_down = ((y_hi * 4 + lax.rem(x + 3, 4)) * 2 + core, col)
        self.x_far = ((y_hi * 4 + lax.rem(x + 2, 4)) * 2 + core, col)
        self.y_far = (((1 - y_hi) * 4 + x) * 2 + core, col)
        self.z_up = (row, y_lo * 4 + lax.rem(z + 1, 4))
        self.z_down = (row, y_lo * 4 + lax.rem(z + 3, 4))
        self.y_near = (row, (1 - y_lo) * 4 + z)
        self.y_next = (((1 - y_hi) * 4 + x) * 2 + core, (1 - y_lo) * 4 + z)
        self.swapped = ((y_hi * 4 + z) * 2 + core, y_lo * 4 + x)
        self.inner = y_hi != y_lo
        self.off_diagonal = x != z
        between = lax.rem(y_hi + y_lo, 2)
        back_y, side_y = lax.rem(y_hi + 1 - between, 2), lax.rem(y_lo + between, 2)
        self.spread_to = ((back_y * 4 + x) * 2 + core, side_y * 4 + z)
        self.spread_slot = lax.rem(y_hi + between, 2) * 4 + x
        self.sum_to = [((y_lo * 4 + x) * 2 + core, part * 4 + z) for part in range(2)]


class Copies:
    def __init__(self, send_sems, recv_sems):
        self.send_sems, self.recv_sems = send_sems, recv_sems
        self.count = 0
        self.started = []

    def take(self):
        self.count += 1
        return self.count - 1

    def make(self, index, src, dst, device, recv=None):
        recv = index if recv is None else recv
        return pltpu.make_async_remote_copy(
            src_ref=src, dst_ref=dst, send_sem=self.send_sems.at[index], recv_sem=self.recv_sems.at[recv],
            device_id=device, device_id_type=MESH)

    def start(self, src, dst, device):
        index = self.take()
        copy = self.make(index, src, dst, device)
        copy.start()
        self.started.append(copy)
        return index

    def arrived(self, index, landing, device):
        self.make(index, landing, landing, device).wait_recv()

    def finish(self):
        for copy in self.started:
            copy.wait_send()


def greet(devices, maybe):
    barrier = pltpu.get_barrier_semaphore()
    total = jnp.int32(len(devices))
    for device in devices:
        pl.semaphore_signal(barrier, inc=1, device_id=device, device_id_type=MESH)
    for there, device in maybe:
        total = total + jnp.where(there, 1, 0)

        @pl.when(there)
        def _():
            pl.semaphore_signal(barrier, inc=1, device_id=device, device_id_type=MESH)

    pl.semaphore_wait(barrier, total)


class Gather:
    def __init__(self, copies, buf, pair_at, ring_at, pair, up, down, rows):
        self.c, self.buf, self.rows = copies, buf, rows
        self.a, self.b = pair_at, ring_at
        self.pair, self.up, self.down = pair, up, down

    def slot(self, pair_step, ring_step):
        a = self.a if pair_step == 0 else 1 - self.a
        return a * 4 + lax.rem(self.b + ring_step, 4)

    def part(self, pair_step, ring_step, half=None):
        at = self.slot(pair_step, ring_step)
        if half is None:
            return self.buf.at[at]
        n = self.rows // 2
        return self.buf.at[at, pl.ds(half * n, n)]

    def same(self, part, device):
        return self.c.start(part, part, device)

    def own(self):
        self.own_ring()
        self.own_pair()

    def own_pair(self):
        self.i_pair = self.same(self.part(0, 0), self.pair)

    def own_ring(self):
        mine = self.part(0, 0)
        self.i_up = self.same(mine, self.up)
        self.i_down = self.same(mine, self.down)

    def forward_own(self):
        self.c.arrived(self.i_up, self.part(0, 3), self.down)
        self.h_up = self.same(self.part(0, 3, 0), self.up)
        self.c.arrived(self.i_down, self.part(0, 1), self.up)
        self.h_down = self.same(self.part(0, 1, 1), self.down)

    def pair_across(self):
        self.c.arrived(self.i_pair, self.part(1, 0), self.pair)
        self.q_up = self.same(self.part(1, 0), self.up)
        self.q_down = self.same(self.part(1, 0), self.down)

    def far_own(self):
        self.c.arrived(self.h_up, self.part(0, 2, 0), self.down)
        self.c.arrived(self.h_down, self.part(0, 2, 1), self.up)

    def far_by_pair(self):
        self.f_pair = self.same(self.part(0, 2), self.pair)

    def end_by_pair(self):
        self.c.arrived(self.q_up, self.part(1, 3), self.down)
        self.c.arrived(self.q_down, self.part(1, 1), self.up)
        self.c.arrived(self.f_pair, self.part(1, 2), self.pair)

    def forward_pair(self):
        self.c.arrived(self.q_up, self.part(1, 3), self.down)
        self.g_up = self.same(self.part(1, 3, 0), self.up)
        self.c.arrived(self.q_down, self.part(1, 1), self.up)
        self.g_down = self.same(self.part(1, 1, 1), self.down)

    def end_by_ring(self):
        self.c.arrived(self.g_up, self.part(1, 2, 0), self.down)
        self.c.arrived(self.g_down, self.part(1, 2, 1), self.up)


def stack_left(ref, value):
    hi, lo = split(value)
    depth = value.shape[1]
    ref[:, 0:depth] = hi
    ref[:, depth:2 * depth] = hi
    ref[:, 2 * depth:] = lo


def stack_right(value):
    hi, lo = split(value)
    return jnp.concatenate([hi, lo, hi], 0)


def eye_of(order):
    rows = lax.broadcasted_iota(jnp.int32, (order, order), 0)
    cols = lax.broadcasted_iota(jnp.int32, (order, order), 1)
    return jnp.where(rows == cols, 1.0, 0.0).astype(F32)


BLOCKS = 3
BLOCK = 384
PART = 256


def panels_kernel(x_ref, w_ref, r_ref, uc_ref, ur_ref, a_ref, g_ref, size_ref, fit_ref,
                  wv, rv, xr, xs, part, from_sib, ra, rb, ry, relay, xh, xl, s_all, sp, rs0, sh, rs1, sh2, rs2,
                  fx, rf0, fh, rf1, fh2, rf2, local_sems, send_sems, recv_sems):
    at = Place()
    k, p, col = at.core, at.chip_row, at.col
    rows = x_ref.shape[0]
    turns = [(1 - k, j) for j in range(BLOCKS)] + [(k, j) for j in range(BLOCKS)]

    def columns(h, j):
        return pl.ds(pl.multiple_of((h * BLOCKS + j) * BLOCK, 128), BLOCK)

    own_x = [pltpu.make_async_copy(x_ref.at[:, pl.ds(e * PART, PART)], xr.at[e, col], local_sems.at[2 * BLOCKS + e])
             for e in range(2)]
    for copy in own_x:
        copy.start()
    own_w = pltpu.make_async_copy(w_ref, wv, local_sems.at[2 * BLOCKS + 2])
    own_w.start()
    loads = []
    for i, (h, j) in enumerate(turns):
        loads.append(pltpu.make_async_copy(r_ref.at[:, columns(h, j)], rv.at[i], local_sems.at[i]))
        loads[-1].start()
    greet([at.sibling, at.x_up, at.x_down, at.x_far, at.y_far, at.z_up, at.z_down, at.y_near],
          [(at.inner, at.y_next), (at.off_diagonal, at.swapped)])
    for copy in own_x:
        copy.wait()
    copies = Copies(send_sems, recv_sems)

    ga, gb = (Gather(copies, xr.at[e], at.y_lo, at.z, at.y_near, at.z_up, at.z_down, rows) for e in range(2))
    ga.own()
    ga.forward_own()
    ga.pair_across()
    ga.far_own()
    ga.far_by_pair()
    gb.own()
    ga.end_by_pair()

    def stack_features(e):
        stack_left(xs.at[pl.ds(e * PART, PART)], xr[e].reshape(8 * rows, PART).T)

    def product(e, i):
        h, j = turns[i]
        if e == 0:
            loads[i].wait()
        value = mm(xs[e * PART:(e + 1) * PART], stack_right(rv[i]))
        part[h, 4 * e:4 * e + 4, :, j * BLOCK:(j + 1) * BLOCK] = value.reshape(4, CHUNK, BLOCK)

    acc = part.at[k]
    sib = {}

    def part_to_sibling(e, j):
        piece = (pl.ds(4 * e, 4), slice(None), slice(j * BLOCK, (j + 1) * BLOCK))
        sib[e, j] = copies.start(part.at[(1 - k,) + piece], from_sib.at[piece], at.sibling)

    half = CHUNK // 2
    low, high = pl.ds(0, half), pl.ds(half, half)
    a_up, a_down, b_up, b_down = {}, {}, {}, {}

    def chunk(e, x_step):
        return e * 4 + lax.rem(at.x + x_step, 4)

    def scatter_far(e):
        for j in range(BLOCKS):
            copies.arrived(sib[e, j], from_sib.at[pl.ds(4 * e, 4), :, j * BLOCK:(j + 1) * BLOCK], at.sibling)
        for x_step in (2, 1, 3, 0):
            ch = chunk(e, x_step)
            acc[ch] = acc[ch] + from_sib[ch]
            if x_step == 2:
                a_up[e] = copies.start(acc.at[ch, low], ra.at[0, e], at.x_up)
                a_down[e] = copies.start(acc.at[ch, high], ra.at[1, e], at.x_down)

    def scatter_near(e):
        ch = chunk(e, 1)
        copies.arrived(a_up[e], ra.at[0, e], at.x_down)
        acc[ch, low] = acc[ch, low] + ra[0, e]
        b_up[e] = copies.start(acc.at[ch], rb.at[0, e], at.x_up)
        ch = chunk(e, 3)
        copies.arrived(a_down[e], ra.at[1, e], at.x_up)
        acc[ch, high] = acc[ch, high] + ra[1, e]
        b_down[e] = copies.start(acc.at[ch], rb.at[1, e], at.x_down)

    y_sems = [copies.take() for _ in range(2)]

    def sum_copy(e):
        return copies.make(y_sems[e], acc.at[chunk(e, 0)], ry.at[at.y_hi], at.sum_to[e], y_sems[0] + at.y_hi)

    def stays(e):
        return (at.y_hi == e) & (at.y_lo == e)

    def scatter_end(e):
        ch = chunk(e, 0)
        copies.arrived(b_up[e], rb.at[0, e], at.x_down)
        copies.arrived(b_down[e], rb.at[1, e], at.x_up)
        acc[ch] = acc[ch] + (rb[0, e] + rb[1, e])

        @pl.when(jnp.logical_not(stays(e)))
        def _():
            sum_copy(e).start()

    stack_features(0)
    product(0, 0)
    part_to_sibling(0, 0)
    product(0, 1)
    part_to_sibling(0, 1)
    gb.forward_own()
    product(0, 2)
    part_to_sibling(0, 2)
    product(0, 3)
    gb.pair_across()
    product(0, 4)
    product(0, 5)
    scatter_far(0)
    gb.far_own()
    gb.far_by_pair()
    gb.end_by_pair()
    stack_features(1)
    product(1, 0)
    part_to_sibling(1, 0)
    scatter_near(0)

    own_w.wait()
    fx[...] = mm(xs[...], stack_right(wv[...]))
    n = ALL // 2
    quarter = n // 4
    f0 = copies.start(fx.at[pl.ds(pl.multiple_of((1 - k) * n, n), n)], rf0, at.sibling)
    product(1, 1)
    part_to_sibling(1, 1)
    product(1, 2)
    part_to_sibling(1, 2)
    copies.arrived(f0, rf0, at.sibling)
    fh[...] = fx[pl.ds(pl.multiple_of(k * n, n), n)] + rf0[...]

    def quarter_at(x_step, base=0):
        return pl.ds(pl.multiple_of(base + lax.rem(at.x + x_step, 4) * quarter, quarter), quarter)

    steps = ((1, at.x_up), (3, at.x_down), (2, at.x_far))
    f1 = [copies.start(fh.at[quarter_at(t)], rf1.at[i], d) for i, (t, d) in enumerate(steps)]
    product(1, 3)
    product(1, 4)
    product(1, 5)
    scatter_far(1)
    scatter_end(0)
    for i, d in enumerate((at.x_down, at.x_up, at.x_far)):
        copies.arrived(f1[i], rf1.at[i], d)
    fh2[...] = (fh[quarter_at(0)] + rf1[2]) + (rf1[0] + rf1[1])
    f2 = copies.start(fh2, rf2, at.y_far)
    scatter_near(1)
    copies.arrived(f2, rf2, at.y_far)
    fit_own = fit_ref.at[quarter_at(0, k * n)]
    fit_own[...] = fh2[...] + rf2[...]
    f3 = [copies.start(fit_own, fit_own, d) for _, d in steps]
    scatter_end(1)

    own = at.y_hi * 4 + at.x

    @pl.when(at.inner)
    def _():
        for i in range(2):
            copies.make(y_sems[0], ry.at[i], ry.at[i], at.y_next, y_sems[i]).wait_recv()
        relay[...] = ry[0] + ry[1]

    @pl.when(jnp.logical_not(at.inner))
    def _():
        there = 1 - at.y_hi
        copies.make(y_sems[0], ry.at[there], ry.at[there], at.y_far, y_sems[0] + there).wait_recv()
        relay[...] = acc[own] + ry[there]
        uc_ref[k, p] = relay[...]

    for e in range(2):
        @pl.when(jnp.logical_not(stays(e)))
        def _():
            sum_copy(e).wait_send()

    t1 = copies.take()
    step_xz = copies.make(t1, relay, ur_ref.at[at.y_lo * 4 + at.x], at.swapped)

    @pl.when(at.off_diagonal)
    def _():
        step_xz.start()

    d1 = copies.start(relay, uc_ref.at[k, at.spread_slot], at.spread_to)
    d2 = copies.take()
    inner_back = copies.make(d2, relay, uc_ref.at[k, at.spread_slot], at.y_next)

    @pl.when(at.inner)
    def _():
        inner_back.start()

    own_block = uc_ref.at[k]
    gc = Gather(copies, own_block, at.y_hi, at.x, at.y_far, at.x_up, at.x_down, CHUNK)
    gr = Gather(copies, ur_ref, at.y_lo, at.z, at.y_near, at.z_up, at.z_down, CHUNK)
    gc.i_pair = d1

    def to_sibling(pair_step, ring_step):
        piece = gc.part(pair_step, ring_step)
        return copies.start(piece, piece, at.sibling)

    for f, t, d in zip(f3, (3, 1, 2), (at.x_down, at.x_up, at.x_far)):
        copies.arrived(f, fit_ref.at[quarter_at(t, k * n)], d)
    fit_half = fit_ref.at[pl.ds(pl.multiple_of(k * n, n), n)]
    f4 = copies.start(fit_half, fit_half, at.sibling)

    for e in range(2):
        hi, lo = split(xr[e].reshape(8 * rows, PART))
        xh[:, e * PART:(e + 1) * PART] = hi
        xl[:, e * PART:(e + 1) * PART] = lo

    @pl.when(at.off_diagonal)
    def _():
        copies.make(t1, ur_ref.at[col], ur_ref.at[col], at.swapped).wait_recv()
        step_xz.wait_send()

    @pl.when(jnp.logical_not(at.off_diagonal))
    def _():
        ur_ref[col] = relay[...]

    gr.own_ring()

    sp[...] = dot3(split(ur_ref[col]), (xh[...], xl[...]))
    s0 = copies.start(sp.at[pl.ds(pl.multiple_of((1 - k) * half, half), half)], rs0, at.sibling)

    @pl.when(at.inner)
    def _():
        copies.make(d2, uc_ref.at[k, p], uc_ref.at[k, p], at.y_next).wait_recv()
        inner_back.wait_send()

    copies.arrived(s0, rs0, at.sibling)
    sh[...] = sp[pl.ds(pl.multiple_of(k * half, half), half)] + rs0[...]
    s1 = [copies.start(sh, rs1.at[i], d) for i, d in enumerate((at.x_up, at.x_down, at.x_far))]
    u = {(0, 0): to_sibling(0, 0)}
    for i, d in enumerate((at.x_down, at.x_up, at.x_far)):
        copies.arrived(s1[i], rs1.at[i], d)
    sh2[...] = (sh[...] + rs1[2]) + (rs1[0] + rs1[1])
    s2 = copies.start(sh2, rs2, at.y_far)
    gc.own_ring()
    copies.arrived(s2, rs2, at.y_far)
    s_all[k, col] = sh2[...] + rs2[...]
    gs = Gather(copies, s_all.at[k], at.y_lo, at.z, at.y_near, at.z_up, at.z_down, half)
    gs.own()
    gr.own_pair()
    gs.forward_own()
    gs.pair_across()
    gr.forward_own()
    gc.forward_own()
    gc.pair_across()
    for step in ((0, 3), (0, 1), (1, 0)):
        u[step] = to_sibling(*step)
    gs.far_own()
    gs.forward_pair()
    gs.end_by_ring()
    s4 = copies.start(s_all.at[k], s_all.at[k], at.sibling)
    gr.pair_across()
    gr.far_own()
    gr.far_by_pair()
    gc.far_own()
    u[(0, 2)] = to_sibling(0, 2)
    copies.arrived(s4, s_all.at[1 - k], at.sibling)

    for c in range(8):
        for h in range(2):
            a_ref[pl.ds(c * CHUNK + h * half, half)] = s_all[h, c]
    eye = eye_of(ALL)
    a_ref[...] = a_ref[...] + eye
    bound = jnp.max(jnp.sum(jnp.abs(a_ref[...]), axis=0, keepdims=True))
    scale = 2.0 / (1.0 + bound)
    g_ref[...] = scale * (2.0 * eye - scale * a_ref[...])

    def refine(_):
        g = split(g_ref[...])
        error = eye_of(ALL) - dot3(split(a_ref[...]), g)
        g_ref[...] = g_ref[...] + dot3(g, split(error))
        size_ref[...] = jnp.broadcast_to(jnp.sum(error * error), size_ref.shape)

    pl.loop(0, 1)(refine)
    gc.forward_pair()
    for step in ((1, 3), (1, 1)):
        u[step] = to_sibling(*step)
    pl.loop(0, 3)(refine)
    gc.end_by_ring()
    u[(1, 2)] = to_sibling(1, 2)
    gr.end_by_pair()
    other_block = uc_ref.at[1 - k]
    for (pair_step, ring_step), index in u.items():
        copies.arrived(index, other_block.at[gc.slot(pair_step, ring_step)], at.sibling)
    copies.arrived(f4, fit_ref.at[pl.ds(pl.multiple_of((1 - k) * n, n), n)], at.sibling)
    copies.finish()


def panels(features_t, head, tile):
    rows, examples = features_t.shape
    depth, width = tile.shape[0], tile.shape[1] // 2
    classes = head.shape[1]
    half = CHUNK // 2
    vmem = pl.BlockSpec(memory_space=pltpu.VMEM)
    dma = pltpu.SemaphoreType.DMA
    return pl.pallas_call(
        panels_kernel,
        out_shape=(
            jax.ShapeDtypeStruct((2, 8, CHUNK, width), F32),
            jax.ShapeDtypeStruct((8, CHUNK, width), F32),
            jax.ShapeDtypeStruct((ALL, ALL), F32),
            jax.ShapeDtypeStruct((ALL, ALL), F32),
            jax.ShapeDtypeStruct((8, 128), F32),
            jax.ShapeDtypeStruct((ALL, classes), F32),
        ),
        in_specs=[pl.BlockSpec(memory_space=pltpu.HBM)] * 3,
        out_specs=(vmem,) * 6,
        scratch_shapes=[
            pltpu.VMEM(head.shape, F32),
            pltpu.VMEM((2 * BLOCKS, depth, BLOCK), F32),
            pltpu.VMEM((2, 8, rows, PART), F32),
            pltpu.VMEM((examples, 3 * depth), BF16),
            pltpu.VMEM((2, 8, CHUNK, width), F32),
            pltpu.VMEM((8, CHUNK, width), F32),
            pltpu.VMEM((2, 2, half, width), F32),
            pltpu.VMEM((2, 2, CHUNK, width), F32),
            pltpu.VMEM((2, CHUNK, width), F32),
            pltpu.VMEM((CHUNK, width), F32),
            pltpu.VMEM((depth, examples), BF16),
            pltpu.VMEM((depth, examples), BF16),
            pltpu.VMEM((2, 8, half, ALL), F32),
            pltpu.VMEM((CHUNK, ALL), F32),
            pltpu.VMEM((half, ALL), F32),
            pltpu.VMEM((half, ALL), F32),
            pltpu.VMEM((3, half, ALL), F32),
            pltpu.VMEM((half, ALL), F32),
            pltpu.VMEM((half, ALL), F32),
            pltpu.VMEM((ALL, classes), F32),
            pltpu.VMEM((ALL // 2, classes), F32),
            pltpu.VMEM((ALL // 2, classes), F32),
            pltpu.VMEM((3, ALL // 8, classes), F32),
            pltpu.VMEM((ALL // 8, classes), F32),
            pltpu.VMEM((ALL // 8, classes), F32),
            dma((2 * BLOCKS + 3,)),
            dma((96,)),
            dma((96,)),
        ],
        compiler_params=pltpu.CompilerParams(collective_id=0, has_side_effects=True, vmem_limit_bytes=VMEM_PANELS),
        name="panels",
    )(pltpu.with_memory_space_constraint(features_t, pltpu.HBM),
      pltpu.with_memory_space_constraint(head, pltpu.HBM),
      pltpu.with_memory_space_constraint(tile, pltpu.HBM))


def update_kernel(a_ref, g_ref, size_ref, ur_ref, u_ref, r_ref, labels_ref, fit_ref, w_ref, out_ref, head_ref,
                  inv_ref, gain_ref, rv, sems):
    at = pl.program_id(0)

    def load(i):
        return pltpu.make_async_copy(r_ref.at[:, pl.ds(pl.multiple_of(i * BLOCK, 128), BLOCK)], rv.at[i], sems.at[i])

    @pl.when(at == 0)
    def _():
        for i in range(2 * BLOCKS):
            load(i).start()
        inv_ref[...] = g_ref[...]

        def more(state):
            step, size = state
            return (step < 60) & (size > 1e-5)

        def refine(state):
            step, _ = state
            g = inv_ref[...]
            error = eye_of(ALL) - jnp.dot(a_ref[...], g, precision=lax.Precision.HIGHEST, preferred_element_type=F32)
            inv_ref[...] = g + dot3(split(g), split(error))
            return step + 1, jnp.sum(error * error)

        lax.while_loop(more, refine, (jnp.int32(0), size_ref[0, 0]))
        stack_left(gain_ref, dot3(split(ur_ref[...].T), split(inv_ref[...])))
        width = w_ref.shape[1]
        classes = lax.axis_index("col") * width + lax.broadcasted_iota(jnp.int32, (width, ALL), 0)
        targets = jnp.where(labels_ref[...] == classes, 1.0, 0.0).astype(F32).T
        head_ref[...] = w_ref[...] + mm(gain_ref[...], stack_right(targets - fit_ref[...]))

    load(at).wait()
    block = u_ref[at // BLOCKS, :, pl.ds(pl.multiple_of(lax.rem(at, BLOCKS) * BLOCK, 128), BLOCK)]
    out_ref[...] = rv[at] - mm(gain_ref[...], stack_right(block))


def update(system, inverse, size, rows_t, cols_t, tile, labels, fitted, head):
    rows = tile.shape[0]
    vmem = pl.BlockSpec(memory_space=pltpu.VMEM)
    return pl.pallas_call(
        update_kernel,
        grid=(2 * BLOCKS,),
        out_shape=(jax.ShapeDtypeStruct(tile.shape, F32), jax.ShapeDtypeStruct(head.shape, F32)),
        in_specs=[vmem] * 4 + [
            vmem,
            pl.BlockSpec(memory_space=pl.ANY),
        ] + [vmem] * 3,
        out_specs=(pl.BlockSpec((rows, BLOCK), lambda i: (0, i)), pl.BlockSpec(head.shape, lambda i: (0, 0))),
        scratch_shapes=[
            pltpu.VMEM((ALL, ALL), F32),
            pltpu.VMEM((rows, 3 * ALL), BF16),
            pltpu.VMEM((2 * BLOCKS, rows, BLOCK), F32),
            pltpu.SemaphoreType.DMA((2 * BLOCKS,)),
        ],
        compiler_params=pltpu.CompilerParams(vmem_limit_bytes=VMEM_UPDATE),
        name="update",
    )(system, inverse, size, rows_t, cols_t, pltpu.with_memory_space_constraint(tile, pltpu.HBM), labels.reshape(1, ALL), fitted, head)


def on_device(features_t, labels, inv_corr, heads):
    cols_t, rows_t, system, inverse, size, fitted = panels(features_t, heads, inv_corr)
    block = cols_t.shape[3]
    return update(system, inverse, size, rows_t.reshape(ALL, block), cols_t.reshape(2, ALL, block), inv_corr, labels,
                  fitted, heads)


def solution(mesh):
    placed = (P(("row", "col"), None), P(), P("row", "col"), P("row", "col"))
    return jax.shard_map(
        on_device,
        mesh=mesh,
        in_specs=placed,
        out_specs=(P("row", "col"), P("row", "col")),
        check_vma=False,
    )
```

```python
import jax
import jax.numpy as jnp
from jax import lax
from jax.experimental import pallas as pl
from jax.experimental.pallas import tpu as pltpu
from jax.sharding import PartitionSpec as P

F32 = jnp.float32
BF16 = jnp.bfloat16
MESH = pl.DeviceIdType.MESH
ALL = 512
CHUNK = 64
MIB = 1 << 20
VMEM_PANELS = 44 * MIB
VMEM_UPDATE = 34 * MIB


def split(value):
    hi = value.astype(BF16)
    lo = (value - hi.astype(F32)).astype(BF16)
    return hi, lo


def mm(left, right):
    return jnp.dot(left, right, preferred_element_type=F32)


def dot3(left, right):
    (lh, ll), (rh, rl) = left, right
    return mm(lh, rh) + (mm(lh, rl) + mm(ll, rh))


class Place:
    def __init__(self):
        self.row, self.col = row, col = lax.axis_index("row"), lax.axis_index("col")
        self.core = core = lax.rem(row, 2)
        self.chip_row = chip_row = row // 2
        self.y_hi, self.x = y_hi, x = chip_row // 4, lax.rem(chip_row, 4)
        self.y_lo, self.z = y_lo, z = col // 4, lax.rem(col, 4)
        self.sibling = (chip_row * 2 + (1 - core), col)
        self.x_up = ((y_hi * 4 + lax.rem(x + 1, 4)) * 2 + core, col)
        self.x_down = ((y_hi * 4 + lax.rem(x + 3, 4)) * 2 + core, col)
        self.x_far = ((y_hi * 4 + lax.rem(x + 2, 4)) * 2 + core, col)
        self.y_far = (((1 - y_hi) * 4 + x) * 2 + core, col)
        self.z_up = (row, y_lo * 4 + lax.rem(z + 1, 4))
        self.z_down = (row, y_lo * 4 + lax.rem(z + 3, 4))
        self.y_near = (row, (1 - y_lo) * 4 + z)
        self.y_next = (((1 - y_hi) * 4 + x) * 2 + core, (1 - y_lo) * 4 + z)
        self.swapped = ((y_hi * 4 + z) * 2 + core, y_lo * 4 + x)
        self.inner = y_hi != y_lo
        self.off_diagonal = x != z
        between = lax.rem(y_hi + y_lo, 2)
        back_y, side_y = lax.rem(y_hi + 1 - between, 2), lax.rem(y_lo + between, 2)
        self.spread_to = ((back_y * 4 + x) * 2 + core, side_y * 4 + z)
        self.spread_slot = lax.rem(y_hi + between, 2) * 4 + x
        self.sum_to = [((y_lo * 4 + x) * 2 + core, part * 4 + z) for part in range(2)]


class Copies:
    def __init__(self, send_sems, recv_sems):
        self.send_sems, self.recv_sems = send_sems, recv_sems
        self.count = 0
        self.started = []

    def take(self):
        self.count += 1
        return self.count - 1

    def make(self, index, src, dst, device, recv=None):
        recv = index if recv is None else recv
        return pltpu.make_async_remote_copy(
            src_ref=src, dst_ref=dst, send_sem=self.send_sems.at[index], recv_sem=self.recv_sems.at[recv],
            device_id=device, device_id_type=MESH)

    def start(self, src, dst, device):
        index = self.take()
        copy = self.make(index, src, dst, device)
        copy.start()
        self.started.append(copy)
        return index

    def arrived(self, index, landing, device):
        self.make(index, landing, landing, device).wait_recv()

    def finish(self):
        for copy in self.started:
            copy.wait_send()


def greet(devices, maybe):
    barrier = pltpu.get_barrier_semaphore()
    total = jnp.int32(len(devices))
    for device in devices:
        pl.semaphore_signal(barrier, inc=1, device_id=device, device_id_type=MESH)
    for there, device in maybe:
        total = total + jnp.where(there, 1, 0)

        @pl.when(there)
        def _():
            pl.semaphore_signal(barrier, inc=1, device_id=device, device_id_type=MESH)

    pl.semaphore_wait(barrier, total)


class Gather:
    def __init__(self, copies, buf, pair_at, ring_at, pair, up, down, rows):
        self.c, self.buf, self.rows = copies, buf, rows
        self.a, self.b = pair_at, ring_at
        self.pair, self.up, self.down = pair, up, down

    def slot(self, pair_step, ring_step):
        a = self.a if pair_step == 0 else 1 - self.a
        return a * 4 + lax.rem(self.b + ring_step, 4)

    def part(self, pair_step, ring_step, half=None):
        at = self.slot(pair_step, ring_step)
        if half is None:
            return self.buf.at[at]
        n = self.rows // 2
        return self.buf.at[at, pl.ds(half * n, n)]

    def same(self, part, device):
        return self.c.start(part, part, device)

    def own(self):
        self.own_ring()
        self.own_pair()

    def own_pair(self):
        self.i_pair = self.same(self.part(0, 0), self.pair)

    def own_ring(self):
        mine = self.part(0, 0)
        self.i_up = self.same(mine, self.up)
        self.i_down = self.same(mine, self.down)

    def forward_own(self):
        self.c.arrived(self.i_up, self.part(0, 3), self.down)
        self.h_up = self.same(self.part(0, 3, 0), self.up)
        self.c.arrived(self.i_down, self.part(0, 1), self.up)
        self.h_down = self.same(self.part(0, 1, 1), self.down)

    def pair_across(self):
        self.c.arrived(self.i_pair, self.part(1, 0), self.pair)
        self.q_up = self.same(self.part(1, 0), self.up)
        self.q_down = self.same(self.part(1, 0), self.down)

    def far_own(self):
        self.c.arrived(self.h_up, self.part(0, 2, 0), self.down)
        self.c.arrived(self.h_down, self.part(0, 2, 1), self.up)

    def far_by_pair(self):
        self.f_pair = self.same(self.part(0, 2), self.pair)

    def end_by_pair(self):
        self.c.arrived(self.q_up, self.part(1, 3), self.down)
        self.c.arrived(self.q_down, self.part(1, 1), self.up)
        self.c.arrived(self.f_pair, self.part(1, 2), self.pair)

    def forward_pair(self):
        self.c.arrived(self.q_up, self.part(1, 3), self.down)
        self.g_up = self.same(self.part(1, 3, 0), self.up)
        self.c.arrived(self.q_down, self.part(1, 1), self.up)
        self.g_down = self.same(self.part(1, 1, 1), self.down)

    def end_by_ring(self):
        self.c.arrived(self.g_up, self.part(1, 2, 0), self.down)
        self.c.arrived(self.g_down, self.part(1, 2, 1), self.up)


def stack_left(ref, value):
    hi, lo = split(value)
    depth = value.shape[1]
    ref[:, 0:depth] = hi
    ref[:, depth:2 * depth] = hi
    ref[:, 2 * depth:] = lo


def stack_right(value):
    hi, lo = split(value)
    return jnp.concatenate([hi, lo, hi], 0)


def eye_of(order):
    rows = lax.broadcasted_iota(jnp.int32, (order, order), 0)
    cols = lax.broadcasted_iota(jnp.int32, (order, order), 1)
    return jnp.where(rows == cols, 1.0, 0.0).astype(F32)


BLOCKS = 3
BLOCK = 384
PART = 256


def panels_kernel(x_ref, w_ref, r_ref, uc_ref, ur_ref, a_ref, g_ref, size_ref, fit_ref,
                  wv, rv, xr, xs, part, from_sib, ra, rb, ry, relay, xh, xl, s_all, sp, rs0, sh, rs1, sh2, rs2,
                  fx, rf0, fh, rf1, fh2, rf2, local_sems, send_sems, recv_sems):
    at = Place()
    k, p, col = at.core, at.chip_row, at.col
    rows = x_ref.shape[0]
    turns = [(1 - k, j) for j in range(BLOCKS)] + [(k, j) for j in range(BLOCKS)]

    def columns(h, j):
        return pl.ds(pl.multiple_of((h * BLOCKS + j) * BLOCK, 128), BLOCK)

    own_x = [pltpu.make_async_copy(x_ref.at[:, pl.ds(e * PART, PART)], xr.at[e, col], local_sems.at[2 * BLOCKS + e])
             for e in range(2)]
    for copy in own_x:
        copy.start()
    own_w = pltpu.make_async_copy(w_ref, wv, local_sems.at[2 * BLOCKS + 2])
    own_w.start()
    loads = []
    for i, (h, j) in enumerate(turns):
        loads.append(pltpu.make_async_copy(r_ref.at[:, columns(h, j)], rv.at[i], local_sems.at[i]))
        loads[-1].start()
    greet([at.sibling, at.x_up, at.x_down, at.x_far, at.y_far, at.z_up, at.z_down, at.y_near],
          [(at.inner, at.y_next), (at.off_diagonal, at.swapped)])
    for copy in own_x:
        copy.wait()
    copies = Copies(send_sems, recv_sems)

    ga, gb = (Gather(copies, xr.at[e], at.y_lo, at.z, at.y_near, at.z_up, at.z_down, rows) for e in range(2))
    ga.own()
    ga.forward_own()
    ga.pair_across()
    ga.far_own()
    ga.far_by_pair()
    gb.own()
    ga.end_by_pair()

    def stack_features(e):
        stack_left(xs.at[pl.ds(e * PART, PART)], xr[e].reshape(8 * rows, PART).T)

    def product(e, i):
        h, j = turns[i]
        if e == 0:
            loads[i].wait()
        value = mm(xs[e * PART:(e + 1) * PART], stack_right(rv[i]))
        part[h, 4 * e:4 * e + 4, :, j * BLOCK:(j + 1) * BLOCK] = value.reshape(4, CHUNK, BLOCK)

    acc = part.at[k]
    sib = {}

    def part_to_sibling(e, j):
        piece = (pl.ds(4 * e, 4), slice(None), slice(j * BLOCK, (j + 1) * BLOCK))
        sib[e, j] = copies.start(part.at[(1 - k,) + piece], from_sib.at[piece], at.sibling)

    half = CHUNK // 2
    low, high = pl.ds(0, half), pl.ds(half, half)
    a_up, a_down, b_up, b_down = {}, {}, {}, {}

    def chunk(e, x_step):
        return e * 4 + lax.rem(at.x + x_step, 4)

    def scatter_far(e):
        for j in range(BLOCKS):
            copies.arrived(sib[e, j], from_sib.at[pl.ds(4 * e, 4), :, j * BLOCK:(j + 1) * BLOCK], at.sibling)
        for x_step in (2, 1, 3, 0):
            ch = chunk(e, x_step)
            acc[ch] = acc[ch] + from_sib[ch]
            if x_step == 2:
                a_up[e] = copies.start(acc.at[ch, low], ra.at[0, e], at.x_up)
                a_down[e] = copies.start(acc.at[ch, high], ra.at[1, e], at.x_down)

    def scatter_near(e):
        ch = chunk(e, 1)
        copies.arrived(a_up[e], ra.at[0, e], at.x_down)
        acc[ch, low] = acc[ch, low] + ra[0, e]
        b_up[e] = copies.start(acc.at[ch], rb.at[0, e], at.x_up)
        ch = chunk(e, 3)
        copies.arrived(a_down[e], ra.at[1, e], at.x_up)
        acc[ch, high] = acc[ch, high] + ra[1, e]
        b_down[e] = copies.start(acc.at[ch], rb.at[1, e], at.x_down)

    y_sems = [copies.take() for _ in range(2)]

    def sum_copy(e):
        return copies.make(y_sems[e], acc.at[chunk(e, 0)], ry.at[at.y_hi], at.sum_to[e], y_sems[0] + at.y_hi)

    def stays(e):
        return (at.y_hi == e) & (at.y_lo == e)

    def scatter_end(e):
        ch = chunk(e, 0)
        copies.arrived(b_up[e], rb.at[0, e], at.x_down)
        copies.arrived(b_down[e], rb.at[1, e], at.x_up)
        acc[ch] = acc[ch] + (rb[0, e] + rb[1, e])

        @pl.when(jnp.logical_not(stays(e)))
        def _():
            sum_copy(e).start()

    stack_features(0)
    product(0, 0)
    part_to_sibling(0, 0)
    product(0, 1)
    part_to_sibling(0, 1)
    gb.forward_own()
    product(0, 2)
    part_to_sibling(0, 2)
    product(0, 3)
    gb.pair_across()
    product(0, 4)
    product(0, 5)
    scatter_far(0)
    gb.far_own()
    gb.far_by_pair()
    gb.end_by_pair()
    stack_features(1)
    product(1, 0)
    part_to_sibling(1, 0)
    scatter_near(0)

    own_w.wait()
    fx[...] = mm(xs[...], stack_right(wv[...]))
    n = ALL // 2
    quarter = n // 4
    f0 = copies.start(fx.at[pl.ds(pl.multiple_of((1 - k) * n, n), n)], rf0, at.sibling)
    product(1, 1)
    part_to_sibling(1, 1)
    product(1, 2)
    part_to_sibling(1, 2)
    copies.arrived(f0, rf0, at.sibling)
    fh[...] = fx[pl.ds(pl.multiple_of(k * n, n), n)] + rf0[...]

    def quarter_at(x_step, base=0):
        return pl.ds(pl.multiple_of(base + lax.rem(at.x + x_step, 4) * quarter, quarter), quarter)

    steps = ((1, at.x_up), (3, at.x_down), (2, at.x_far))
    f1 = [copies.start(fh.at[quarter_at(t)], rf1.at[i], d) for i, (t, d) in enumerate(steps)]
    product(1, 3)
    product(1, 4)
    product(1, 5)
    scatter_far(1)
    scatter_end(0)
    for i, d in enumerate((at.x_down, at.x_up, at.x_far)):
        copies.arrived(f1[i], rf1.at[i], d)
    fh2[...] = (fh[quarter_at(0)] + rf1[2]) + (rf1[0] + rf1[1])
    f2 = copies.start(fh2, rf2, at.y_far)
    scatter_near(1)
    copies.arrived(f2, rf2, at.y_far)
    fit_own = fit_ref.at[quarter_at(0, k * n)]
    fit_own[...] = fh2[...] + rf2[...]
    f3 = [copies.start(fit_own, fit_own, d) for _, d in steps]
    scatter_end(1)

    own = at.y_hi * 4 + at.x

    @pl.when(at.inner)
    def _():
        for i in range(2):
            copies.make(y_sems[0], ry.at[i], ry.at[i], at.y_next, y_sems[i]).wait_recv()
        relay[...] = ry[0] + ry[1]

    @pl.when(jnp.logical_not(at.inner))
    def _():
        there = 1 - at.y_hi
        copies.make(y_sems[0], ry.at[there], ry.at[there], at.y_far, y_sems[0] + there).wait_recv()
        relay[...] = acc[own] + ry[there]
        uc_ref[k, p] = relay[...]

    for e in range(2):
        @pl.when(jnp.logical_not(stays(e)))
        def _():
            sum_copy(e).wait_send()

    t1 = copies.take()
    step_xz = copies.make(t1, relay, ur_ref.at[at.y_lo * 4 + at.x], at.swapped)

    @pl.when(at.off_diagonal)
    def _():
        step_xz.start()

    d1 = copies.start(relay, uc_ref.at[k, at.spread_slot], at.spread_to)
    d2 = copies.take()
    inner_back = copies.make(d2, relay, uc_ref.at[k, at.spread_slot], at.y_next)

    @pl.when(at.inner)
    def _():
        inner_back.start()

    own_block = uc_ref.at[k]
    gc = Gather(copies, own_block, at.y_hi, at.x, at.y_far, at.x_up, at.x_down, CHUNK)
    gr = Gather(copies, ur_ref, at.y_lo, at.z, at.y_near, at.z_up, at.z_down, CHUNK)
    gc.i_pair = d1

    def to_sibling(pair_step, ring_step):
        piece = gc.part(pair_step, ring_step)
        return copies.start(piece, piece, at.sibling)

    for f, t, d in zip(f3, (3, 1, 2), (at.x_down, at.x_up, at.x_far)):
        copies.arrived(f, fit_ref.at[quarter_at(t, k * n)], d)
    fit_half = fit_ref.at[pl.ds(pl.multiple_of(k * n, n), n)]
    f4 = copies.start(fit_half, fit_half, at.sibling)

    for e in range(2):
        hi, lo = split(xr[e].reshape(8 * rows, PART))
        xh[:, e * PART:(e + 1) * PART] = hi
        xl[:, e * PART:(e + 1) * PART] = lo

    @pl.when(at.off_diagonal)
    def _():
        copies.make(t1, ur_ref.at[col], ur_ref.at[col], at.swapped).wait_recv()
        step_xz.wait_send()

    @pl.when(jnp.logical_not(at.off_diagonal))
    def _():
        ur_ref[col] = relay[...]

    gr.own_ring()

    sp[...] = dot3(split(ur_ref[col]), (xh[...], xl[...]))
    s0 = copies.start(sp.at[pl.ds(pl.multiple_of((1 - k) * half, half), half)], rs0, at.sibling)

    @pl.when(at.inner)
    def _():
        copies.make(d2, uc_ref.at[k, p], uc_ref.at[k, p], at.y_next).wait_recv()
        inner_back.wait_send()

    copies.arrived(s0, rs0, at.sibling)
    sh[...] = sp[pl.ds(pl.multiple_of(k * half, half), half)] + rs0[...]
    s1 = [copies.start(sh, rs1.at[i], d) for i, d in enumerate((at.x_up, at.x_down, at.x_far))]
    u = {(0, 0): to_sibling(0, 0)}
    for i, d in enumerate((at.x_down, at.x_up, at.x_far)):
        copies.arrived(s1[i], rs1.at[i], d)
    sh2[...] = (sh[...] + rs1[2]) + (rs1[0] + rs1[1])
    s2 = copies.start(sh2, rs2, at.y_far)
    gc.own_ring()
    gc.pair_across()
    copies.arrived(s2, rs2, at.y_far)
    s_all[k, col] = sh2[...] + rs2[...]
    gs = Gather(copies, s_all.at[k], at.y_lo, at.z, at.y_near, at.z_up, at.z_down, half)
    gs.own()
    gr.own_pair()
    gs.forward_own()
    gs.pair_across()
    gr.forward_own()
    gc.forward_own()
    for step in ((0, 3), (0, 1), (1, 0)):
        u[step] = to_sibling(*step)
    gs.far_own()
    gs.forward_pair()
    gs.end_by_ring()
    s4 = copies.start(s_all.at[k], s_all.at[k], at.sibling)
    gr.pair_across()
    gr.far_own()
    gr.far_by_pair()
    gc.far_own()
    u[(0, 2)] = to_sibling(0, 2)
    copies.arrived(s4, s_all.at[1 - k], at.sibling)

    for c in range(8):
        for h in range(2):
            a_ref[pl.ds(c * CHUNK + h * half, half)] = s_all[h, c]
    eye = eye_of(ALL)
    a_ref[...] = a_ref[...] + eye
    bound = jnp.max(jnp.sum(jnp.abs(a_ref[...]), axis=0, keepdims=True))
    scale = 2.0 / (1.0 + bound)
    g_ref[...] = scale * (2.0 * eye - scale * a_ref[...])

    def refine(_):
        g = split(g_ref[...])
        error = eye_of(ALL) - dot3(split(a_ref[...]), g)
        g_ref[...] = g_ref[...] + dot3(g, split(error))
        size_ref[...] = jnp.broadcast_to(jnp.sum(error * error), size_ref.shape)

    pl.loop(0, 1)(refine)
    gc.forward_pair()
    for step in ((1, 3), (1, 1)):
        u[step] = to_sibling(*step)
    pl.loop(0, 3)(refine)
    gc.end_by_ring()
    u[(1, 2)] = to_sibling(1, 2)
    gr.end_by_pair()
    other_block = uc_ref.at[1 - k]
    for (pair_step, ring_step), index in u.items():
        copies.arrived(index, other_block.at[gc.slot(pair_step, ring_step)], at.sibling)
    copies.arrived(f4, fit_ref.at[pl.ds(pl.multiple_of((1 - k) * n, n), n)], at.sibling)
    copies.finish()


def panels(features_t, head, tile):
    rows, examples = features_t.shape
    depth, width = tile.shape[0], tile.shape[1] // 2
    classes = head.shape[1]
    half = CHUNK // 2
    vmem = pl.BlockSpec(memory_space=pltpu.VMEM)
    dma = pltpu.SemaphoreType.DMA
    return pl.pallas_call(
        panels_kernel,
        out_shape=(
            jax.ShapeDtypeStruct((2, 8, CHUNK, width), F32),
            jax.ShapeDtypeStruct((8, CHUNK, width), F32),
            jax.ShapeDtypeStruct((ALL, ALL), F32),
            jax.ShapeDtypeStruct((ALL, ALL), F32),
            jax.ShapeDtypeStruct((8, 128), F32),
            jax.ShapeDtypeStruct((ALL, classes), F32),
        ),
        in_specs=[pl.BlockSpec(memory_space=pltpu.HBM)] * 3,
        out_specs=(vmem,) * 6,
        scratch_shapes=[
            pltpu.VMEM(head.shape, F32),
            pltpu.VMEM((2 * BLOCKS, depth, BLOCK), F32),
            pltpu.VMEM((2, 8, rows, PART), F32),
            pltpu.VMEM((examples, 3 * depth), BF16),
            pltpu.VMEM((2, 8, CHUNK, width), F32),
            pltpu.VMEM((8, CHUNK, width), F32),
            pltpu.VMEM((2, 2, half, width), F32),
            pltpu.VMEM((2, 2, CHUNK, width), F32),
            pltpu.VMEM((2, CHUNK, width), F32),
            pltpu.VMEM((CHUNK, width), F32),
            pltpu.VMEM((depth, examples), BF16),
            pltpu.VMEM((depth, examples), BF16),
            pltpu.VMEM((2, 8, half, ALL), F32),
            pltpu.VMEM((CHUNK, ALL), F32),
            pltpu.VMEM((half, ALL), F32),
            pltpu.VMEM((half, ALL), F32),
            pltpu.VMEM((3, half, ALL), F32),
            pltpu.VMEM((half, ALL), F32),
            pltpu.VMEM((half, ALL), F32),
            pltpu.VMEM((ALL, classes), F32),
            pltpu.VMEM((ALL // 2, classes), F32),
            pltpu.VMEM((ALL // 2, classes), F32),
            pltpu.VMEM((3, ALL // 8, classes), F32),
            pltpu.VMEM((ALL // 8, classes), F32),
            pltpu.VMEM((ALL // 8, classes), F32),
            dma((2 * BLOCKS + 3,)),
            dma((96,)),
            dma((96,)),
        ],
        compiler_params=pltpu.CompilerParams(collective_id=0, has_side_effects=True, vmem_limit_bytes=VMEM_PANELS),
        name="panels",
    )(pltpu.with_memory_space_constraint(features_t, pltpu.HBM),
      pltpu.with_memory_space_constraint(head, pltpu.HBM),
      pltpu.with_memory_space_constraint(tile, pltpu.HBM))


def update_kernel(a_ref, g_ref, size_ref, ur_ref, u_ref, r_ref, labels_ref, fit_ref, w_ref, out_ref, head_ref,
                  inv_ref, gain_ref, rv, sems):
    at = pl.program_id(0)

    def load(i):
        return pltpu.make_async_copy(r_ref.at[:, pl.ds(pl.multiple_of(i * BLOCK, 128), BLOCK)], rv.at[i], sems.at[i])

    @pl.when(at == 0)
    def _():
        for i in range(2 * BLOCKS):
            load(i).start()
        inv_ref[...] = g_ref[...]

        def more(state):
            step, size = state
            return (step < 60) & (size > 1e-5)

        def refine(state):
            step, _ = state
            g = inv_ref[...]
            error = eye_of(ALL) - jnp.dot(a_ref[...], g, precision=lax.Precision.HIGHEST, preferred_element_type=F32)
            inv_ref[...] = g + dot3(split(g), split(error))
            return step + 1, jnp.sum(error * error)

        lax.while_loop(more, refine, (jnp.int32(0), size_ref[0, 0]))
        stack_left(gain_ref, dot3(split(ur_ref[...].T), split(inv_ref[...])))
        width = w_ref.shape[1]
        classes = lax.axis_index("col") * width + lax.broadcasted_iota(jnp.int32, (width, ALL), 0)
        targets = jnp.where(labels_ref[...] == classes, 1.0, 0.0).astype(F32).T
        head_ref[...] = w_ref[...] + mm(gain_ref[...], stack_right(targets - fit_ref[...]))

    load(at).wait()
    block = u_ref[at // BLOCKS, :, pl.ds(pl.multiple_of(lax.rem(at, BLOCKS) * BLOCK, 128), BLOCK)]
    out_ref[...] = rv[at] - mm(gain_ref[...], stack_right(block))


def update(system, inverse, size, rows_t, cols_t, tile, labels, fitted, head):
    rows = tile.shape[0]
    vmem = pl.BlockSpec(memory_space=pltpu.VMEM)
    return pl.pallas_call(
        update_kernel,
        grid=(2 * BLOCKS,),
        out_shape=(jax.ShapeDtypeStruct(tile.shape, F32), jax.ShapeDtypeStruct(head.shape, F32)),
        in_specs=[vmem] * 4 + [
            vmem,
            pl.BlockSpec(memory_space=pl.ANY),
        ] + [vmem] * 3,
        out_specs=(pl.BlockSpec((rows, BLOCK), lambda i: (0, i)), pl.BlockSpec(head.shape, lambda i: (0, 0))),
        scratch_shapes=[
            pltpu.VMEM((ALL, ALL), F32),
            pltpu.VMEM((rows, 3 * ALL), BF16),
            pltpu.VMEM((2 * BLOCKS, rows, BLOCK), F32),
            pltpu.SemaphoreType.DMA((2 * BLOCKS,)),
        ],
        compiler_params=pltpu.CompilerParams(vmem_limit_bytes=VMEM_UPDATE),
        name="update",
    )(system, inverse, size, rows_t, cols_t, pltpu.with_memory_space_constraint(tile, pltpu.HBM), labels.reshape(1, ALL), fitted, head)


def on_device(features_t, labels, inv_corr, heads):
    cols_t, rows_t, system, inverse, size, fitted = panels(features_t, heads, inv_corr)
    block = cols_t.shape[3]
    return update(system, inverse, size, rows_t.reshape(ALL, block), cols_t.reshape(2, ALL, block), inv_corr, labels,
                  fitted, heads)


def solution(mesh):
    placed = (P(("row", "col"), None), P(), P("row", "col"), P("row", "col"))
    return jax.shard_map(
        on_device,
        mesh=mesh,
        in_specs=placed,
        out_specs=(P("row", "col"), P("row", "col")),
        check_vma=False,
    )
```
